32 devices in a mesh: groups: 2 (over y), tok: 4 (over z), rep: 2 (over x), head: 2 (over core).
Axes of the slice: x: 2, y: 2, z: 4, core: 2. Of those that a mesh axis runs over, the one named last changes fastest.
Arguments:
- query_rows: float32 [4, 2, 1024, 512], P(('groups', 'rep'), 'head', 'tok'), parts along dimension 0, may hold values from -6 to 6
- key_rows: float32 [4, 2, 1024, 512], P(('groups', 'rep'), 'head', 'tok'), parts along dimension 0, may hold values from -6 to 6
- value_rows: float32 [4, 2, 1024, 512], P(('groups', 'rep'), 'head', 'tok'), parts along dimension 0, may hold values from -6 to 6
- step_logits: float32 [4, 2, 1024], P(('groups', 'rep'), 'head', 'tok'), parts along dimension 0, may hold values from -3 to 3
- read_cotangent: float32 [4, 2, 1024, 512], P(('groups', 'rep'), 'head', 'tok'), parts along dimension 0, may hold values from -6 to 6
- fast_gate: float32 [2, 512, 512], P('head', ('tok', 'rep')), may hold values from -0.25 to 0.25
- fast_up: float32 [2, 512, 512], P('head', ('tok', 'rep')), may hold values from -0.25 to 0.25
- fast_down: float32 [2, 512, 512], P('head', ('tok', 'rep')), may hold values from -0.25 to 0.25
Outputs:
- query_grad: float32 [4, 2, 1024, 512], P(('groups', 'rep'), 'head', 'tok'), parts along dimension 0
- key_grad: float32 [4, 2, 1024, 512], P(('groups', 'rep'), 'head', 'tok'), parts along dimension 0
- value_grad: float32 [4, 2, 1024, 512], P(('groups', 'rep'), 'head', 'tok'), parts along dimension 0
- logit_grad: float32 [4, 2, 1024], P(('groups', 'rep'), 'head', 'tok'), parts along dimension 0
- gate_grad: float32 [4, 512, 512], P(('groups', 'head'), ('tok', 'rep')), parts along dimension 0
- up_grad: float32 [4, 512, 512], P(('groups', 'head'), ('tok', 'rep')), parts along dimension 0
- down_grad: float32 [4, 512, 512], P(('groups', 'head'), ('tok', 'rep')), parts along dimension 0
The draws below stay inside these ranges and needn't reach their ends.
There are 2 independent parts, one for each index of `groups`. The reference program is written for one: setup_inputs(seed, part) draws one part's arguments, and reference() takes and returns one part's arrays. A program takes and returns all parts, laid end to end along the dimension named above; an argument that names none is the same for every part. Nothing has to cross between parts.
All inputs are finite; a program needn't handle non-finite values.
Results may differ from the reference program's by a relative error of at most 0.00023.
Values sent between devices are 32-bit elements; how exact they have to be, the bound alone decides.
No kernel may reach another device: no remote copies, remote signals or barrier semaphores. Data moves between devices by JAX's collectives and lax.ppermute only.
A program may use at most 64 MiB of HBM per device.

```python
import math
import jax
import jax.numpy as jnp
from jax import lax

D = 512
H = 512
HEADS = 2
BLOCK = 1024
REPS = 2


def block_scale(key, dims, pieces, low, top_value):
    def one(position, parts):
        steps = jax.random.uniform(jax.random.fold_in(jax.random.fold_in(key, 6), position), (parts,), jnp.float32, low / len(pieces), top_value / len(pieces))
        return jnp.repeat(jnp.exp(steps), dims[position] // parts).reshape((-1,) + (1,) * (len(dims) - position - 1))

    factor_of = one(*pieces[0])
    for cut in pieces[1:]:
        factor_of = factor_of * one(*cut)
    return factor_of


def centred(stream_key, shape, spread, reach, pieces=(), kind=jnp.bfloat16):
    values = spread * jax.random.normal(stream_key, shape, jnp.float32)
    if pieces:
        values = values * block_scale(stream_key, shape, pieces, -0.22, 0.18)
    return jnp.clip(values, -reach, reach).astype(kind)


def setup_inputs(seed: int = 0, part: int = 0) -> dict:
    arg_keys = jax.random.split(jax.random.key(seed), 9)
    own_keys = jax.random.split(jax.random.fold_in(arg_keys[8], part), 9)
    query_rows = centred(own_keys[0], (REPS, HEADS, BLOCK, D), 1.0, 6.0, ((0, 2), (1, 2), (2, 4)), jnp.float32)
    key_rows = centred(own_keys[1], (REPS, HEADS, BLOCK, D), 1.0, 6.0, ((0, 2), (1, 2), (2, 4)), jnp.float32)
    value_rows = centred(own_keys[2], (REPS, HEADS, BLOCK, D), 1.0, 6.0, ((0, 2), (1, 2), (2, 4)), jnp.float32)
    step_logits = centred(own_keys[3], (REPS, HEADS, BLOCK), 1.0, 3.0, ((0, 2), (1, 2), (2, 4)), jnp.float32)
    read_cotangent = centred(own_keys[4], (REPS, HEADS, BLOCK, D), 1.0, 6.0, ((0, 2), (1, 2), (2, 4)), jnp.float32)
    fast_gate = centred(arg_keys[5], (HEADS, D, H), D ** -0.5, 0.25, ((0, 2), (1, 8)), jnp.float32)
    fast_up = centred(arg_keys[6], (HEADS, D, H), D ** -0.5, 0.25, ((0, 2), (1, 8)), jnp.float32)
    fast_down = centred(arg_keys[7], (HEADS, D, H), H ** -0.5, 0.25, ((0, 2), (1, 8)), jnp.float32)
    return {"query_rows": query_rows, "key_rows": key_rows, "value_rows": value_rows, "step_logits": step_logits, "read_cotangent": read_cotangent, "fast_gate": fast_gate, "fast_up": fast_up, "fast_down": fast_down}


EPSILON = 1e-06

def contract(form, left, right):
    return jnp.einsum(form, left, right, precision=lax.Precision.HIGHEST)

def silu_slope(pre):
    sigma = jax.nn.sigmoid(pre)
    return sigma * (1.0 + pre * (1.0 - sigma))

def inner_gradient(key_head, value_head, logit_head, gate_head, up_head, down_head, factor):
    step = jax.nn.softplus(logit_head) * factor
    gate_pre = contract('td,df->tf', key_head, gate_head)
    up_pre = contract('td,df->tf', key_head, up_head)
    hidden = jax.nn.silu(gate_pre) * up_pre
    target = -step[:, None] * value_head
    back = contract('td,df->tf', target, down_head)
    down_step = contract('td,tf->df', target, hidden)
    gate_back = back * up_pre * silu_slope(gate_pre)
    up_back = back * jax.nn.silu(gate_pre)
    return (contract('td,tf->df', key_head, gate_back), contract('td,tf->df', key_head, up_back), down_step)

def renormalize(weight, step):
    moved = weight - step
    ratio = jnp.sqrt(lax.optimization_barrier(jnp.mean(weight * weight, axis=-2, keepdims=True)) + EPSILON) / jnp.sqrt(lax.optimization_barrier(jnp.mean(moved * moved, axis=-2, keepdims=True)) + EPSILON)
    return moved * ratio

def replica_loss(query_rep, key_rep, value_rep, logit_rep, cotangent_rep, fast_gate, fast_up, fast_down):
    factor = 1.0 / (8.0 * math.sqrt(BLOCK))

    def one_head(query_head, key_head, value_head, logit_head, cotangent_head, gate_head, up_head, down_head):
        steps = inner_gradient(key_head, value_head, logit_head, gate_head, up_head, down_head, factor)
        gate_new = renormalize(gate_head, steps[0])
        up_new = renormalize(up_head, steps[1])
        down_new = renormalize(down_head, steps[2])
        hidden = jax.nn.silu(contract('td,df->tf', query_head, gate_new)) * contract('td,df->tf', query_head, up_new)
        output = contract('tf,df->td', hidden, down_new)
        return jnp.sum(output * cotangent_head)
    return jnp.sum(jax.vmap(one_head)(query_rep, key_rep, value_rep, logit_rep, cotangent_rep, fast_gate, fast_up, fast_down))

def reference(query_rows, key_rows, value_rows, step_logits, read_cotangent, fast_gate, fast_up, fast_down):

    def total_loss(queries_all, keys_all, values_all, logits_all, gate_all, up_all, down_all):
        total = jnp.zeros((), jnp.float32)
        for replica in range(REPS):
            total = total + jax.checkpoint(replica_loss)(queries_all[replica], keys_all[replica], values_all[replica], logits_all[replica], read_cotangent[replica], gate_all, up_all, down_all)
        return total
    grads = jax.grad(total_loss, argnums=(0, 1, 2, 3, 4, 5, 6))(query_rows, key_rows, value_rows, step_logits, fast_gate, fast_up, fast_down)
    return (grads[0], grads[1], grads[2], grads[3], grads[4], grads[5], grads[6])
```

```python
import math

import jax
import jax.numpy as jnp
from jax import lax
from jax.sharding import PartitionSpec as P

EPSILON = 1e-06
CELL = 4
ROUNDS = CELL - 1
PLACE = ("tok", "head")
SWAP = [(0, 1), (1, 0)]


def home_of(head):
    return (CELL - 1) // 2 + head


def source_of(head, turn):
    return (home_of(head) + 1 + turn % ROUNDS) % CELL


def routes(cells):
    rounds = []
    for turn in range(ROUNDS):
        pairs = []
        for cell in range(cells):
            for head in range(2):
                for core in range(2):
                    origin = cell * CELL + source_of(head, turn + core)
                    home = cell * CELL + home_of(head)
                    pairs.append((origin * 2 + head, home * 2 + core))
        rounds.append(pairs)
    return rounds


def local_routes(cells):
    pairs = []
    for cell in range(cells):
        for head in range(2):
            home = cell * CELL + home_of(head)
            pairs.append((home * 2 + head, home * 2 + 1 - head))
    return pairs


def flipped(pairs):
    return [(second, first) for first, second in pairs]


def contract(form, left, right):
    return jnp.einsum(form, left, right, precision=lax.Precision.HIGH)


def per_device(
    query_rows, key_rows, value_rows, step_logits, read_cotangent, fast_gate, fast_up, fast_down
):
    tokens_here = key_rows.shape[2]
    half = tokens_here // 2
    tok_size = lax.axis_size("tok")
    rep_size = lax.axis_size("rep")
    cells = tok_size // CELL
    assert tok_size % CELL == 0 and lax.axis_size("head") == 2
    factor = 1.0 / (8.0 * math.sqrt(tokens_here * tok_size))
    pairs = routes(cells)
    local_pairs = local_routes(cells)
    place = lax.axis_index("tok") % CELL
    core = lax.axis_index("head")
    rep = lax.axis_index("rep")
    cell_groups = [[cell * CELL + spot for cell in range(cells)] for spot in range(CELL)]
    turn0 = jnp.mod(place - core - home_of(0) - 1, CELL)
    turn1 = jnp.mod(turn0 + ROUNDS - 1, ROUNDS)
    at_home = place == home_of(0) + core
    owner = core == place - home_of(0)

    step = jax.nn.softplus(step_logits[0, 0]) * factor
    target = -step[:, None] * value_rows[0, 0]
    keys = key_rows[0, 0]
    queries = query_rows[0, 0]
    cotangent = read_cotangent[0, 0]
    weights_own = jnp.stack((fast_gate[0], fast_up[0], fast_down[0]))
    rows = weights_own.shape[1]
    width = weights_own.shape[2]
    cols = width // 2

    def start_of(turn):
        return jnp.where(turn1 == turn, 1, 0)

    sent = []
    for turn in range(ROUNDS):
        piece = lax.dynamic_slice_in_dim(weights_own, start_of(turn) * cols, cols, axis=2)
        sent.append(lax.ppermute(piece, PLACE, pairs[turn]))
    mine = lax.dynamic_slice_in_dim(weights_own, core * cols, cols, axis=2)
    other = lax.dynamic_slice_in_dim(weights_own, (1 - core) * cols, cols, axis=2)
    sent.append(jnp.where(owner, mine, lax.ppermute(other, PLACE, local_pairs)))
    came = [
        jnp.mod(place + 1 + jnp.mod(turn + core, ROUNDS), CELL) for turn in range(ROUNDS)
    ] + [place]

    def pick(pieces, keys_of, wanted):
        out = pieces[-1]
        for piece, key in zip(pieces[:-1], keys_of[:-1]):
            out = jnp.where(key == wanted, piece, out)
        return out

    ordered = jnp.stack([pick(sent, came, spot) for spot in range(CELL)], axis=1)
    if rep_size == 2:
        across = lax.ppermute(ordered, "rep", SWAP)
        ordered = jnp.stack(
            (jnp.where(rep == 0, ordered, across), jnp.where(rep == 0, across, ordered)), axis=2
        )
    else:
        ordered = lax.all_gather(ordered, "rep", axis=2)
    ordered = ordered[:, None]
    if cells > 1:
        ordered = lax.all_gather(ordered, "tok", axis=1, tiled=True, axis_index_groups=cell_groups)
    weights = ordered.reshape(3, cells * CELL * rep_size * rows, cols)

    def gather(first, second):
        near, far = [], []
        for turn in range(ROUNDS):
            begin = start_of(turn) * half
            piece = jnp.stack(
                (
                    lax.dynamic_slice_in_dim(first, begin, half),
                    lax.dynamic_slice_in_dim(second, begin, half),
                )
            )
            near.append(lax.ppermute(piece, PLACE, pairs[turn]))
        for turn in range(ROUNDS):
            far.append(lax.ppermute(near[turn], "head", SWAP))
        whole = jnp.stack((first, second))
        local = jnp.where(owner, whole, lax.ppermute(whole, PLACE, local_pairs))
        return jnp.concatenate(near + far + [local], axis=1)

    def scatter(grads):
        near = grads[:, : ROUNDS * half]
        far = grads[:, ROUNDS * half : 2 * ROUNDS * half]
        local = grads[:, 2 * ROUNDS * half :]
        total = near + lax.ppermute(far, "head", SWAP)
        back = [
            lax.ppermute(total[:, turn * half : (turn + 1) * half], PLACE, flipped(pairs[turn]))
            for turn in range(ROUNDS)
        ]
        local = local + lax.ppermute(local, PLACE, flipped(local_pairs))

        def choose(turn):
            return jnp.where(turn == 0, back[0], jnp.where(turn == 1, back[1], back[2]))

        remote = jnp.concatenate((choose(turn0), choose(turn1)), axis=1)
        return jnp.where(at_home, local, remote)

    gathered = gather(keys, target)
    keys_all, target_all = gathered[0], gathered[1]
    gathered = gather(queries, cotangent)
    query_all, cot_all = gathered[0], gathered[1]

    gate, up, down = weights[0], weights[1], weights[2]
    gate_pre = contract("td,df->tf", keys_all, gate)
    up_pre = contract("td,df->tf", keys_all, up)
    back = contract("td,df->tf", target_all, down)
    sigma = jax.nn.sigmoid(gate_pre)
    slope = sigma * (1.0 + gate_pre * (1.0 - sigma))
    act = gate_pre * sigma
    hidden = act * up_pre
    gate_back = back * up_pre * slope
    up_back = back * act
    steps = jnp.stack(
        (
            contract("td,tf->df", keys_all, gate_back),
            contract("td,tf->df", keys_all, up_back),
            contract("td,tf->df", target_all, hidden),
        )
    )
    if cells > 1:
        steps = lax.psum(steps, "tok", axis_index_groups=cell_groups)
    moved = weights - steps
    norm_old = jnp.mean(weights * weights, axis=1, keepdims=True) + EPSILON
    norm_new = jnp.mean(moved * moved, axis=1, keepdims=True) + EPSILON
    ratio = jnp.sqrt(norm_old) / jnp.sqrt(norm_new)
    renewed = moved * ratio

    gate_new, up_new, down_new = renewed[0], renewed[1], renewed[2]
    read_gate = contract("td,df->tf", query_all, gate_new)
    read_up = contract("td,df->tf", query_all, up_new)
    hidden_back = contract("td,df->tf", cot_all, down_new)
    read_sigma = jax.nn.sigmoid(read_gate)
    read_slope = read_sigma * (1.0 + read_gate * (1.0 - read_sigma))
    read_act = read_gate * read_sigma
    read_gate_back = hidden_back * read_up * read_slope
    read_up_back = hidden_back * read_act
    totals = jnp.stack(
        (
            contract("td,tf->df", query_all, read_gate_back),
            contract("td,tf->df", query_all, read_up_back),
            contract("td,tf->df", cot_all, read_act * read_up),
        )
    )
    query_part = contract("tf,df->td", read_gate_back, gate_new) + contract(
        "tf,df->td", read_up_back, up_new
    )
    query_grad = scatter(query_part[None])
    if cells > 1:
        totals = lax.psum(totals, "tok", axis_index_groups=cell_groups)

    ratio_cot = jnp.sum(totals * moved, axis=1, keepdims=True)
    moved_cot = ratio * (totals - moved * (ratio_cot / (width * norm_new)))
    direct = moved_cot + weights * (ratio_cot * ratio / (width * norm_old))
    step_cot = -moved_cot

    gate_back_cot = contract("td,df->tf", keys_all, step_cot[0])
    up_back_cot = contract("td,df->tf", keys_all, step_cot[1])
    hidden_cot = contract("td,df->tf", target_all, step_cot[2])
    bend = sigma * (1.0 - sigma) * (2.0 + gate_pre * (1.0 - 2.0 * sigma))
    back_cot = gate_back_cot * up_pre * slope + up_back_cot * act
    up_cot = gate_back_cot * back * slope + hidden_cot * act
    gate_cot = (
        gate_back_cot * back * up_pre * bend + (up_back_cot * back + hidden_cot * up_pre) * slope
    )
    grads = jnp.stack(
        (
            contract("td,tf->df", keys_all, gate_cot),
            contract("td,tf->df", keys_all, up_cot),
            contract("td,tf->df", target_all, back_cot),
        )
    )
    if cells > 1:
        direct = jnp.where(lax.axis_index("tok") < CELL, direct, 0.0)
    grads = grads + direct

    shaped = grads.reshape(3, cells, CELL, rep_size, rows, cols)
    if cells > 1:
        shaped = lax.psum_scatter(
            shaped, "tok", scatter_dimension=1, tiled=True, axis_index_groups=cell_groups
        )
    shaped = shaped[:, 0]
    if rep_size == 2:
        keep = jnp.where(rep == 0, shaped[:, :, 0], shaped[:, :, 1])
        give = jnp.where(rep == 0, shaped[:, :, 1], shaped[:, :, 0])
        shaped = keep + lax.ppermute(give, "rep", SWAP)
    else:
        shaped = lax.psum_scatter(shaped, "rep", scatter_dimension=2)
    spots = [shaped[:, spot] for spot in range(CELL)]
    returned = [
        lax.ppermute(pick(spots, list(range(CELL)), came[turn]), PLACE, flipped(pairs[turn]))
        for turn in range(ROUNDS)
    ]
    home_piece = pick(spots, list(range(CELL)), place)
    home_other = lax.ppermute(home_piece, PLACE, flipped(local_pairs))

    def choose(turn):
        return jnp.where(turn == 0, returned[0], jnp.where(turn == 1, returned[1], returned[2]))

    low = jnp.where(at_home, jnp.where(core == 0, home_piece, home_other), choose(turn0))
    high = jnp.where(at_home, jnp.where(core == 0, home_other, home_piece), choose(turn1))
    owned = jnp.concatenate((low, high), axis=2)

    key_part = (
        contract("tf,df->td", gate_back, step_cot[0])
        + contract("tf,df->td", up_back, step_cot[1])
        + contract("tf,df->td", gate_cot, gate)
        + contract("tf,df->td", up_cot, up)
    )
    target_part = contract("tf,df->td", hidden, step_cot[2]) + contract(
        "tf,df->td", back_cot, down
    )
    settled = scatter(jnp.stack((key_part, target_part)))
    key_grad, target_grad = settled[0], settled[1]
    value_grad = -step[:, None] * target_grad
    step_grad = -jnp.sum(value_rows[0, 0] * target_grad, axis=1)
    logit_grad = step_grad * factor * jax.nn.sigmoid(step_logits[0, 0])
    return (
        query_grad[0][None, None],
        key_grad[None, None],
        value_grad[None, None],
        logit_grad[None, None],
        owned[0][None],
        owned[1][None],
        owned[2][None],
    )


def solution(mesh):
    tokens = P(("groups", "rep"), "head", "tok", None)
    logits = P(("groups", "rep"), "head", "tok")
    weight = P("head", ("tok", "rep"), None)
    grad = P(("groups", "head"), ("tok", "rep"), None)
    return jax.shard_map(
        per_device,
        mesh=mesh,
        in_specs=(tokens, tokens, tokens, logits, tokens, weight, weight, weight),
        out_specs=(tokens, tokens, tokens, logits, grad, grad, grad),
        check_vma=False,
    )
```

```python
import functools
import math

import jax
import jax.numpy as jnp
from jax import lax
from jax.experimental import pallas as pl
from jax.experimental.pallas import tpu as pltpu
from jax.sharding import PartitionSpec as P

EPSILON = 1e-06
CELL = 4
ROUNDS = CELL - 1
PLACE = ("tok", "head")
SWAP = [(0, 1), (1, 0)]
F32 = jnp.float32
BF16 = jnp.bfloat16
NN = ((1,), (0,))
NT = ((1,), (1,))
ANY = pl.BlockSpec(memory_space=pl.ANY)
VMEM = pl.BlockSpec(memory_space=pltpu.VMEM)


def home_of(head):
    return (CELL - 1) // 2 + head


def source_of(head, turn):
    return (home_of(head) + 1 + (turn + 2 * (1 - head)) % ROUNDS) % CELL


def routes(cells):
    rounds = []
    for turn in range(ROUNDS):
        pairs = []
        for cell in range(cells):
            here = []
            for head in range(2):
                for core in range(2):
                    origin = cell * CELL + source_of(head, turn + core)
                    home = cell * CELL + home_of(head)
                    here.append((origin * 2 + head, home * 2 + core))
            everyone = range(cell * CELL * 2, (cell + 1) * CELL * 2)
            idle = sorted(set(everyone) - {first for first, _ in here})
            free = sorted(set(everyone) - {second for _, second in here})
            pairs += here + list(zip(idle, free))
        rounds.append(pairs)
    return rounds


def flipped(pairs):
    return [(second, first) for first, second in pairs]


def split(value):
    high = value.astype(BF16)
    return high, (value - high.astype(F32)).astype(BF16)


def dot3(left, right, form):
    def one(first, second):
        return lax.dot_general(first, second, (form, ((), ())), preferred_element_type=F32)

    return one(left[0], right[0]) + (one(left[0], right[1]) + one(left[1], right[0]))


def position():
    place = lax.rem(lax.axis_index("tok"), CELL)
    core = lax.axis_index("head")
    return place, core


def spot_of(place, core, slot):
    if slot == ROUNDS:
        return place
    head = place - home_of(0)
    return lax.rem(place + 1 + lax.rem(slot + core + 2 * (1 - head) + ROUNDS, ROUNDS), CELL)


def halves_sent(place, core):
    ahead = lax.rem(place - home_of(0) - core - 1 + 2 * CELL, CELL)
    turn0 = lax.rem(ahead + 1 - core, ROUNDS)
    turn1 = lax.rem(turn0 + ROUNDS - 1, ROUNDS)
    return turn0, turn1


def run_copies(copies):
    for copy in copies:
        copy.start()
    for copy in copies:
        copy.wait()


def pack_weights_kernel(gate, up, down, *rest):
    outs, sems = rest[:-1], rest[-1]
    place, core = position()
    _, turn1 = halves_sent(place, core)
    cols = outs[0].shape[2]
    copies = []
    for piece, out in enumerate(outs):
        if piece < ROUNDS:
            part = jnp.where(turn1 == piece, 1, 0)
        else:
            part = core if piece == ROUNDS else 1 - core
        begin = pl.multiple_of(part * cols, cols)
        for which, ref in enumerate((gate, up, down)):
            copies.append(
                pltpu.make_async_copy(
                    ref.at[:, pl.ds(begin, cols)], out.at[which], sems.at[piece, which]
                )
            )
    run_copies(copies)


def pack_rows_kernel(scaled, half, *refs):
    if scaled:
        first, second, scale, *rest = refs
        *outs, held, sems, load_sem = rest
        load = pltpu.make_async_copy(second, held, load_sem)
        load.start()
    else:
        first, second, *rest = refs
        *outs, sems = rest
    place, core = position()
    _, turn1 = halves_sent(place, core)

    def copies_of(which, ref):
        copies = []
        for piece in range(ROUNDS):
            begin = pl.multiple_of(jnp.where(turn1 == piece, half, 0), half)
            copies.append(
                pltpu.make_async_copy(
                    ref.at[pl.ds(begin, half)],
                    outs[piece].at[pl.ds(which * half, half)],
                    sems.at[piece, which],
                )
            )
        copies.append(
            pltpu.make_async_copy(
                ref, outs[ROUNDS].at[pl.ds(which * 2 * half, 2 * half)], sems.at[ROUNDS, which]
            )
        )
        return copies

    early = copies_of(0, first)
    for copy in early:
        copy.start()
    if scaled:
        load.wait()
        held[...] = held[...] * scale[...]
        late = copies_of(1, held)
    else:
        late = copies_of(1, second)
    for copy in late:
        copy.start()
    for copy in early + late:
        copy.wait()


def fetch_rows(near, far, own, got, buffers, sems):
    half = near[0].shape[0] // 2
    place, core = position()
    mine = core == place - home_of(0)
    for block in range(ROUNDS):
        for which in range(2):
            rows = pl.ds(which * half, half)
            for side, group in enumerate((near, far)):
                pltpu.make_async_copy(
                    group[block].at[rows],
                    buffers[which].at[block, pl.ds(side * half, half)],
                    sems.at[block, which * 2 + side],
                ).start()

    def local(source):
        for which in range(2):
            for side in range(2):
                pltpu.make_async_copy(
                    source.at[pl.ds((which * 2 + side) * half, half)],
                    buffers[which].at[ROUNDS, pl.ds(side * half, half)],
                    sems.at[ROUNDS, which * 2 + side],
                ).start()

    @pl.when(mine)
    def _():
        local(own)

    @pl.when(jnp.logical_not(mine))
    def _():
        local(got)


def wait_rows(buffers, block, sems):
    half = buffers[0].shape[1] // 2
    for part in range(4):
        view = buffers[part // 2].at[block, pl.ds((part % 2) * half, half)]
        pltpu.make_async_copy(view, view, sems.at[block, part]).wait()


def row_starts(cells, reps, rows):
    place, core = position()
    rep = lax.axis_index("rep")
    starts = {}
    for cell in range(cells):
        for shift in range(reps):
            owner_rep = lax.rem(rep - shift + reps, reps)
            for slot in range(CELL):
                spot = spot_of(place, core, slot)
                begin = ((cell * CELL + spot) * reps + owner_rep) * rows
                starts[cell, shift, slot] = pl.multiple_of(begin, rows)
    return starts


def silu_parts(pre):
    sigma = jax.nn.sigmoid(pre)
    rest = 1.0 - sigma
    return sigma, pre * sigma, sigma * (1.0 + pre * rest)


def store_split(ref, index, value):
    high, low = split(value)
    ref[(0,) + index] = high
    ref[(1,) + index] = low


def pair_of(ref, *index):
    return ref[(0,) + index], ref[(1,) + index]


def inner_kernel(cells, reps, *refs):
    pieces = CELL * reps if cells == 1 else 1
    parts, refs = refs[:pieces], refs[pieces:]
    near, far, (own, got), refs = refs[:3], refs[3:6], refs[6:8], refs[8:]
    weights, gates, ups, backs, steps, *scratch = refs
    keys, targets, wide, turned, acts, row_sems, weight_sems = scratch
    rows = parts[0].shape[-2]
    starts = row_starts(cells, reps, rows)
    copies = []
    for number, ((cell, shift, slot), begin) in enumerate(starts.items()):
        source = parts[shift * CELL + slot] if cells == 1 else parts[0].at[cell, shift * CELL + slot]
        copies.append(
            pltpu.make_async_copy(
                source, weights.at[:, pl.ds(begin, rows)], weight_sems.at[number]
            )
        )
    for copy in copies:
        copy.start()
    fetch_rows(near, far, own, got, (keys, targets), row_sems)
    for copy in copies:
        copy.wait()
    for which in range(3):
        store_split(wide, (which,), weights[which])
    size = keys.shape[1]

    @pl.loop(0, CELL)
    def _(block):
        wait_rows((keys, targets), block, row_sems)
        where = pl.ds(pl.multiple_of(block * size, size), size)
        key, target = split(keys[block]), split(targets[block])
        gate_pre = dot3(key, pair_of(wide, 0), NN)
        up_pre = dot3(key, pair_of(wide, 1), NN)
        back = dot3(target, pair_of(wide, 2), NN)
        gates[where] = gate_pre
        ups[where] = up_pre
        backs[where] = back
        _, act, slope = silu_parts(gate_pre)
        store_split(acts, (0, where), back * up_pre * slope)
        store_split(acts, (1, where), back * act)
        store_split(acts, (2, where), act * up_pre)
        for part in range(2):
            turned[part, 0, :, where] = key[part].T
            turned[part, 1, :, where] = target[part].T

    for which in range(3):
        steps[which] = dot3(pair_of(turned, which // 2), pair_of(acts, which), NN)


def renew_kernel(weights, steps, high, low):
    for which in range(3):
        weight = weights[which]
        moved = weight - steps[which]
        old = jnp.mean(weight * weight, axis=0, keepdims=True) + EPSILON
        new = jnp.mean(moved * moved, axis=0, keepdims=True) + EPSILON
        high[which], low[which] = split(moved * (jnp.sqrt(old) / jnp.sqrt(new)))


def read_kernel(*refs):
    near, far, (own, got, high, low), refs = refs[:3], refs[3:6], refs[6:10], refs[10:]
    (totals, near_out, far_out, local_out), scratch = (
        (refs[0], refs[1:4], refs[4:7], refs[7]),
        refs[8:],
    )
    queries, cots, turned, acts, sent, row_sems, out_sems = scratch
    fetch_rows(near, far, own, got, (queries, cots), row_sems)
    size = queries.shape[1]
    half = size // 2

    def weight(which):
        return high[which], low[which]

    def outgoing(block):
        if block < ROUNDS:
            return [
                (sent.at[block, pl.ds(0, half)], near_out[block]),
                (sent.at[block, pl.ds(half, half)], far_out[block]),
            ]
        return [(sent.at[block], local_out)]

    @pl.loop(0, CELL)
    def _(block):
        wait_rows((queries, cots), block, row_sems)
        where = pl.ds(pl.multiple_of(block * size, size), size)
        query, cot = split(queries[block]), split(cots[block])
        gate_pre = dot3(query, weight(0), NN)
        up_pre = dot3(query, weight(1), NN)
        back = dot3(cot, weight(2), NN)
        _, act, slope = silu_parts(gate_pre)
        gate_back = split(back * up_pre * slope)
        up_back = split(back * act)
        for part in range(2):
            acts[part, 0, where] = gate_back[part]
            acts[part, 1, where] = up_back[part]
            turned[part, 0, :, where] = query[part].T
            turned[part, 1, :, where] = cot[part].T
        store_split(acts, (2, where), act * up_pre)
        sent[block] = dot3(gate_back, weight(0), NT) + dot3(up_back, weight(1), NT)
        for number in range(CELL):

            @pl.when(block == number)
            def _():
                for side, (source, out) in enumerate(outgoing(number)):
                    pltpu.make_async_copy(source, out, out_sems.at[number, side]).start()

    for which in range(3):
        totals[which] = dot3(pair_of(turned, which // 2), pair_of(acts, which), NN)
    for block in range(CELL):
        for side, (source, out) in enumerate(outgoing(block)):
            pltpu.make_async_copy(source, out, out_sems.at[block, side]).wait()


def backward_kernel(cells, reps, *refs):
    near, far, (own, got), refs = refs[:3], refs[3:6], refs[6:8], refs[8:]
    (weights, steps, totals, gates, ups, backs), refs = refs[:6], refs[6:]
    near_out, far_out, local_out, refs = refs[:3], refs[3:6], refs[6], refs[7:]
    pieces, scratch = refs[:reps], refs[reps:]
    keys, targets, wide, cots, turned, acts, grads, sent, row_sems, out_sems, grad_sems = scratch
    fetch_rows(near, far, own, got, (keys, targets), row_sems)
    size = keys.shape[1]
    half = size // 2
    width = weights.shape[1]
    scale = 1.0 / width
    for which in range(3):
        weight, total = weights[which], totals[which]
        moved = weight - steps[which]
        old = jnp.mean(weight * weight, axis=0, keepdims=True) + EPSILON
        new = jnp.mean(moved * moved, axis=0, keepdims=True) + EPSILON
        ratio = jnp.sqrt(old) / jnp.sqrt(new)
        ratio_cot = jnp.sum(total * moved, axis=0, keepdims=True) * scale
        moved_cot = ratio * (total - moved * (ratio_cot / new))
        direct = moved_cot + weight * (ratio_cot * ratio / old)
        if cells > 1:
            direct = direct * jnp.where(lax.axis_index("tok") < CELL, 1.0, 0.0)
        grads[which] = direct
        store_split(wide, (which,), weight)
        store_split(cots, (which,), -moved_cot)

    def outgoing(block):
        if block < ROUNDS:
            return [
                (sent.at[which, block, pl.ds(side * half, half)],
                 (near_out, far_out)[side][block].at[pl.ds(which * half, half)])
                for which in range(2)
                for side in range(2)
            ]
        return [
            (sent.at[which, block], local_out.at[pl.ds(which * size, size)]) for which in range(2)
        ]

    @pl.loop(0, CELL)
    def _(block):
        wait_rows((keys, targets), block, row_sems)
        where = pl.ds(pl.multiple_of(block * size, size), size)
        key, target = split(keys[block]), split(targets[block])
        gate_back_cot = dot3(key, pair_of(cots, 0), NN)
        up_back_cot = dot3(key, pair_of(cots, 1), NN)
        hidden_cot = dot3(target, pair_of(cots, 2), NN)
        gate_pre, up_pre, back = gates[where], ups[where], backs[where]
        sigma, act, slope = silu_parts(gate_pre)
        bend = sigma * (1.0 - sigma) * (2.0 + gate_pre * (1.0 - 2.0 * sigma))
        mixed = gate_back_cot * slope
        back_cot = split(mixed * up_pre + up_back_cot * act)
        up_cot = split(mixed * back + hidden_cot * act)
        gate_cot = split(
            gate_back_cot * back * up_pre * bend
            + (up_back_cot * back + hidden_cot * up_pre) * slope
        )
        for part in range(2):
            acts[part, 0, where] = gate_cot[part]
            acts[part, 1, where] = up_cot[part]
            acts[part, 2, where] = back_cot[part]
            turned[part, 0, :, where] = key[part].T
            turned[part, 1, :, where] = target[part].T
        sent[0, block] = (
            dot3(gate_cot, pair_of(wide, 0), NT)
            + dot3(up_cot, pair_of(wide, 1), NT)
            + dot3(split(back * up_pre * slope), pair_of(cots, 0), NT)
            + dot3(split(back * act), pair_of(cots, 1), NT)
        )
        sent[1, block] = dot3(back_cot, pair_of(wide, 2), NT) + dot3(
            split(act * up_pre), pair_of(cots, 2), NT
        )
        for number in range(CELL):

            @pl.when(block == number)
            def _():
                for side, (source, out) in enumerate(outgoing(number)):
                    pltpu.make_async_copy(source, out, out_sems.at[number, side]).start()

    for which in range(3):
        grads[which] += dot3(pair_of(turned, which // 2), pair_of(acts, which), NN)
    rows = pieces[0].shape[-2]
    copies = []
    place, core = position()
    rep = lax.axis_index("rep")
    number = 0
    for cell in range(cells):
        for shift in range(reps):
            owner_rep = lax.rem(rep + shift, reps)
            for slot in range(CELL):
                spot = spot_of(place, core, slot)
                begin = pl.multiple_of(((cell * CELL + spot) * reps + owner_rep) * rows, rows)
                copies.append(
                    pltpu.make_async_copy(
                        grads.at[:, pl.ds(begin, rows)],
                        pieces[shift].at[cell, slot],
                        grad_sems.at[number],
                    )
                )
                number += 1
    run_copies(copies)
    for block in range(CELL):
        for side, (source, out) in enumerate(outgoing(block)):
            pltpu.make_async_copy(source, out, out_sems.at[block, side]).wait()


def call(kernel, inputs, in_specs, outs, out_specs, scratch, flops=0):
    moved = sum(math.prod(value.shape) * value.dtype.itemsize for value in list(inputs) + list(outs))
    return pl.pallas_call(
        kernel,
        out_shape=outs,
        in_specs=in_specs,
        out_specs=out_specs,
        scratch_shapes=scratch,
        cost_estimate=pl.CostEstimate(flops=flops, bytes_accessed=moved, transcendentals=0),
        compiler_params=pltpu.CompilerParams(vmem_limit_bytes=48 << 20),
    )(*inputs)


def per_device(
    query_rows, key_rows, value_rows, step_logits, read_cotangent, fast_gate, fast_up, fast_down
):
    tokens_here, depth = key_rows.shape[2:]
    half = tokens_here // 2
    tok_size = lax.axis_size("tok")
    reps = lax.axis_size("rep")
    cells = tok_size // CELL
    assert tok_size % CELL == 0 and lax.axis_size("head") == 2
    factor = 1.0 / (8.0 * math.sqrt(tokens_here * tok_size))
    pairs = routes(cells)
    place, core = position()
    turn0, turn1 = halves_sent(place, core)
    at_home = place == home_of(0) + core
    cell_groups = [[cell * CELL + spot for cell in range(cells)] for spot in range(CELL)]
    rows, width = fast_gate.shape[1:]
    cols = width // 2
    shape = jax.ShapeDtypeStruct
    dma = pltpu.SemaphoreType.DMA

    def shifted(shift, sign):
        return [(rep, (rep + sign * shift) % reps) for rep in range(reps)]

    step = jax.nn.softplus(step_logits[0, 0]) * factor

    packed = call(
        pack_weights_kernel,
        (fast_gate[0], fast_up[0], fast_down[0]),
        [ANY] * 3,
        [shape((3, rows, cols), F32)] * (ROUNDS + 2),
        [ANY] * (ROUNDS + 2),
        [dma((ROUNDS + 2, 3))],
    )
    slots = [lax.ppermute(packed[turn], PLACE, pairs[turn]) for turn in range(ROUNDS)]
    other = lax.ppermute(packed[ROUNDS + 1], "head", SWAP)
    owner = core == place - home_of(0)
    slots.append(jnp.where(owner, packed[ROUNDS], other))
    parts = list(slots)
    for shift in range(1, reps):
        parts += [lax.ppermute(piece, "rep", shifted(shift, 1)) for piece in slots]
    if cells > 1:
        parts = [lax.all_gather(jnp.stack(parts), "tok", axis_index_groups=cell_groups)]

    def gather(first, second, scale):
        outs = [shape((2 * half, depth), F32)] * ROUNDS + [shape((4 * half, depth), F32)]
        scratch = [dma((CELL, 2))]
        inputs, specs = [first, second], [ANY, ANY]
        if scale is not None:
            inputs, specs = inputs + [scale], specs + [VMEM]
            scratch = [pltpu.VMEM((2 * half, depth), F32)] + scratch + [dma]
        packed = call(
            functools.partial(pack_rows_kernel, scale is not None, half),
            inputs,
            specs,
            outs,
            [ANY] * CELL,
            scratch,
        )
        near = [lax.ppermute(packed[turn], PLACE, pairs[turn]) for turn in range(ROUNDS)]
        got = lax.ppermute(packed[ROUNDS], "head", SWAP)
        far = [lax.ppermute(piece, "head", SWAP) for piece in near]
        return near + far + [packed[ROUNDS], got]

    def scatter(near, far, local):
        back = []
        for turn in range(ROUNDS):
            total = near[turn] + lax.ppermute(far[turn], "head", SWAP)
            back.append(lax.ppermute(total, PLACE, flipped(pairs[turn])))
        local = local + lax.ppermute(local, "head", SWAP)

        def choose(turn):
            return jnp.where(turn == 0, back[0], jnp.where(turn == 1, back[1], back[2]))

        low, high = choose(turn0), choose(turn1)
        found = []
        for which in range(low.shape[0] // half):
            span = slice(which * half, (which + 1) * half)
            remote = jnp.concatenate((low[span], high[span]))
            here = local[which * 2 * half : (which + 1) * 2 * half]
            found.append(jnp.where(at_home, here, remote))
        return found

    inner_rows = gather(key_rows[0, 0], value_rows[0, 0], -step[:, None])
    read_rows = gather(query_rows[0, 0], read_cotangent[0, 0], None)

    size = 2 * half
    count = CELL * size
    square = shape((3, width, cols), F32)
    tall = shape((count, cols), F32)
    product = 6 * count * width * cols
    buffers = [pltpu.VMEM((CELL, size, depth), F32)] * 2
    turned = pltpu.VMEM((2, 2, depth, count), BF16)
    acts = pltpu.VMEM((2, 3, count, cols), BF16)
    split_square = pltpu.VMEM((2, 3, width, cols), BF16)
    weights, gates, ups, backs, steps = call(
        functools.partial(inner_kernel, cells, reps),
        parts + inner_rows,
        [ANY] * (len(parts) + 8),
        [square, tall, tall, tall, square],
        [VMEM] * 5,
        buffers
        + [split_square, turned, acts, dma((CELL, 4)), dma((cells * reps * CELL,))],
        6 * product,
    )
    if cells > 1:
        steps = lax.psum(steps, "tok", axis_index_groups=cell_groups)
    narrow = shape((3, width, cols), BF16)
    high, low = call(
        renew_kernel, (weights, steps), [VMEM] * 2, [narrow, narrow], [VMEM] * 2, []
    )
    piece = shape((half, depth), F32)
    read = call(
        read_kernel,
        read_rows + [high, low],
        [ANY] * 8 + [VMEM] * 2,
        [square] + [piece] * 6 + [shape((size, depth), F32)],
        [VMEM] + [ANY] * 7,
        buffers
        + [turned, acts, pltpu.VMEM((CELL, size, depth), F32), dma((CELL, 4)), dma((CELL, 2))],
        8 * product,
    )
    totals = read[0]
    if cells > 1:
        totals = lax.psum(totals, "tok", axis_index_groups=cell_groups)
    piece = shape((size, depth), F32)
    final = call(
        functools.partial(backward_kernel, cells, reps),
        inner_rows + [weights, steps, totals, gates, ups, backs],
        [ANY] * 8 + [VMEM] * 6,
        [piece] * 6
        + [shape((2 * size, depth), F32)]
        + [shape((cells, CELL, 3, rows, cols), F32)] * reps,
        [ANY] * (7 + reps),
        buffers
        + [
            split_square,
            split_square,
            turned,
            acts,
            pltpu.VMEM((3, width, cols), F32),
            pltpu.VMEM((2, CELL, size, depth), F32),
            dma((CELL, 4)),
            dma((CELL, 4)),
            dma((cells * reps * CELL,)),
        ],
        12 * product,
    )
    (query_grad,) = scatter(read[1:4], read[4:7], read[7])
    key_grad, target_grad = scatter(final[0:3], final[3:6], final[6])

    given = list(final[7:])
    if cells > 1:
        given = [
            lax.psum_scatter(value, "tok", scatter_dimension=0, tiled=True, axis_index_groups=cell_groups)
            for value in given
        ]
    total = given[0][0]
    for shift in range(1, reps):
        total = total + lax.ppermute(given[shift][0], "rep", shifted(shift, 1))
    returned = [
        lax.ppermute(total[turn], PLACE, flipped(pairs[turn])) for turn in range(ROUNDS)
    ]
    home_piece = total[ROUNDS]
    home_other = lax.ppermute(home_piece, "head", SWAP)

    def choose(turn):
        return jnp.where(turn == 0, returned[0], jnp.where(turn == 1, returned[1], returned[2]))

    left = jnp.where(at_home, jnp.where(core == 0, home_piece, home_other), choose(turn0))
    right = jnp.where(at_home, jnp.where(core == 0, home_other, home_piece), choose(turn1))
    owned = jnp.concatenate((left, right), axis=2)

    value_grad = -step[:, None] * target_grad
    step_grad = -jnp.sum(value_rows[0, 0] * target_grad, axis=1)
    logit_grad = step_grad * factor * jax.nn.sigmoid(step_logits[0, 0])
    return (
        query_grad[None, None],
        key_grad[None, None],
        value_grad[None, None],
        logit_grad[None, None],
        owned[0][None],
        owned[1][None],
        owned[2][None],
    )


def solution(mesh):
    tokens = P(("groups", "rep"), "head", "tok", None)
    logits = P(("groups", "rep"), "head", "tok")
    weight = P("head", ("tok", "rep"), None)
    grad = P(("groups", "head"), ("tok", "rep"), None)
    return jax.shard_map(
        per_device,
        mesh=mesh,
        in_specs=(tokens, tokens, tokens, logits, tokens, weight, weight, weight),
        out_specs=(tokens, tokens, tokens, logits, grad, grad, grad),
        check_vma=False,
    )
```

```python
import functools
import math

import jax
import jax.numpy as jnp
from jax import lax
from jax.experimental import pallas as pl
from jax.experimental.pallas import tpu as pltpu
from jax.sharding import PartitionSpec as P

EPSILON = 1e-06
CELL = 4
ROUNDS = CELL - 1
PLACE = ("tok", "head")
SWAP = [(0, 1), (1, 0)]
F32 = jnp.float32
BF16 = jnp.bfloat16
NN = ((1,), (0,))
NT = ((1,), (1,))
HBM = pl.BlockSpec(memory_space=pltpu.MemorySpace.HBM)
VMEM = pl.BlockSpec(memory_space=pltpu.VMEM)


def home_of(head):
    return (CELL - 1) // 2 + head


def source_of(head, turn):
    return (home_of(head) + 1 + (turn + 2 * (1 - head)) % ROUNDS) % CELL


def routes(cells):
    rounds = []
    for turn in range(ROUNDS):
        pairs = []
        for cell in range(cells):
            here = []
            for head in range(2):
                for core in range(2):
                    origin = cell * CELL + source_of(head, turn + core)
                    home = cell * CELL + home_of(head)
                    here.append((origin * 2 + head, home * 2 + core))
            everyone = range(cell * CELL * 2, (cell + 1) * CELL * 2)
            idle = sorted(set(everyone) - {first for first, _ in here})
            free = sorted(set(everyone) - {second for _, second in here})
            pairs += here + list(zip(idle, free))
        rounds.append(pairs)
    return rounds


def flipped(pairs):
    return [(second, first) for first, second in pairs]


def split(value):
    high = value.astype(BF16)
    return high, (value - high.astype(F32)).astype(BF16)


def dot3(left, right, form):
    def one(first, second):
        return lax.dot_general(first, second, (form, ((), ())), preferred_element_type=F32)

    return one(left[0], right[0]) + (one(left[0], right[1]) + one(left[1], right[0]))


def position():
    place = lax.rem(lax.axis_index("tok"), CELL)
    core = lax.axis_index("head")
    return place, core


def spot_of(place, core, slot):
    if slot == ROUNDS:
        return place
    head = place - home_of(0)
    return lax.rem(place + 1 + lax.rem(slot + core + 2 * (1 - head) + ROUNDS, ROUNDS), CELL)


def halves_sent(place, core):
    ahead = lax.rem(place - home_of(0) - core - 1 + 2 * CELL, CELL)
    turn0 = lax.rem(ahead + 1 - core, ROUNDS)
    turn1 = lax.rem(turn0 + ROUNDS - 1, ROUNDS)
    return turn0, turn1


def run_copies(copies):
    for copy in copies:
        copy.start()
    for copy in copies:
        copy.wait()


def pack_weights_kernel(gate, up, down, *rest):
    outs, sems = rest[:-1], rest[-1]
    place, core = position()
    _, turn1 = halves_sent(place, core)
    cols = outs[0].shape[2]
    copies = []
    for piece, out in enumerate(outs):
        if piece < ROUNDS:
            part = jnp.where(turn1 == piece, 1, 0)
        else:
            part = core if piece == ROUNDS else 1 - core
        begin = pl.multiple_of(part * cols, cols)
        for which, ref in enumerate((gate, up, down)):
            copies.append(
                pltpu.make_async_copy(
                    ref.at[:, pl.ds(begin, cols)], out.at[which], sems.at[piece, which]
                )
            )
    run_copies(copies)


def collect_kernel(first, second, third, own, got, out, sems):
    place, core = position()
    mine = core == place - home_of(0)
    copies = [
        pltpu.make_async_copy(piece, out.at[slot], sems.at[slot])
        for slot, piece in enumerate((first, second, third))
    ]
    for copy in copies:
        copy.start()

    @pl.when(mine)
    def _():
        pltpu.make_async_copy(own, out.at[ROUNDS], sems.at[ROUNDS]).start()

    @pl.when(jnp.logical_not(mine))
    def _():
        pltpu.make_async_copy(got, out.at[ROUNDS], sems.at[ROUNDS]).start()

    for copy in copies:
        copy.wait()
    pltpu.make_async_copy(own, out.at[ROUNDS], sems.at[ROUNDS]).wait()


def pack_rows_kernel(scaled, half, *refs):
    if scaled:
        first, second, scale, *rest = refs
        *outs, held, sems, load_sem = rest
        load = pltpu.make_async_copy(second, held, load_sem)
        load.start()
    else:
        first, second, *rest = refs
        *outs, sems = rest
    place, core = position()
    _, turn1 = halves_sent(place, core)

    def copies_of(which, ref):
        copies = []
        for piece in range(ROUNDS):
            begin = pl.multiple_of(jnp.where(turn1 == piece, half, 0), half)
            copies.append(
                pltpu.make_async_copy(
                    ref.at[pl.ds(begin, half)],
                    outs[piece].at[pl.ds(which * half, half)],
                    sems.at[piece, which],
                )
            )
        copies.append(
            pltpu.make_async_copy(
                ref, outs[ROUNDS].at[pl.ds(which * 2 * half, 2 * half)], sems.at[ROUNDS, which]
            )
        )
        return copies

    early = copies_of(0, first)
    for copy in early:
        copy.start()
    if scaled:
        load.wait()
        held[...] = held[...] * scale[...]
        late = copies_of(1, held)
    else:
        late = copies_of(1, second)
    for copy in late:
        copy.start()
    for copy in early + late:
        copy.wait()


def fetch_rows(near, far, own, got, buffers, sems):
    half = near[0].shape[0] // 2
    place, core = position()
    mine = core == place - home_of(0)
    for block in range(ROUNDS):
        for which in range(2):
            rows = pl.ds(which * half, half)
            for side, group in enumerate((near, far)):
                pltpu.make_async_copy(
                    group[block].at[rows],
                    buffers[which].at[block, pl.ds(side * half, half)],
                    sems.at[block, which * 2 + side],
                ).start()

    def local(source):
        for which in range(2):
            for side in range(2):
                pltpu.make_async_copy(
                    source.at[pl.ds((which * 2 + side) * half, half)],
                    buffers[which].at[ROUNDS, pl.ds(side * half, half)],
                    sems.at[ROUNDS, which * 2 + side],
                ).start()

    @pl.when(mine)
    def _():
        local(own)

    @pl.when(jnp.logical_not(mine))
    def _():
        local(got)


def wait_rows(buffers, block, sems):
    half = buffers[0].shape[1] // 2
    for part in range(4):
        view = buffers[part // 2].at[block, pl.ds((part % 2) * half, half)]
        pltpu.make_async_copy(view, view, sems.at[block, part]).wait()


def row_starts(cells, reps, rows):
    place, core = position()
    rep = lax.axis_index("rep")
    starts = {}
    for cell in range(cells):
        for shift in range(reps):
            owner_rep = lax.rem(rep - shift + reps, reps)
            for slot in range(CELL):
                spot = spot_of(place, core, slot)
                begin = ((cell * CELL + spot) * reps + owner_rep) * rows
                starts[cell, shift, slot] = pl.multiple_of(begin, rows)
    return starts


def silu_parts(pre):
    sigma = jax.nn.sigmoid(pre)
    rest = 1.0 - sigma
    return sigma, pre * sigma, sigma * (1.0 + pre * rest)


def store_split(ref, index, value):
    high, low = split(value)
    ref[(0,) + index] = high
    ref[(1,) + index] = low


def pair_of(ref, *index):
    return ref[(0,) + index], ref[(1,) + index]


def inner_kernel(cells, reps, *refs):
    pieces = reps if cells == 1 else 1
    parts, refs = refs[:pieces], refs[pieces:]
    near, far, (own, got), refs = refs[:3], refs[3:6], refs[6:8], refs[8:]
    weights, gates, ups, backs, steps, *scratch = refs
    keys, targets, wide, turned, acts, row_sems, weight_sems = scratch
    rows = parts[0].shape[-2]
    starts = row_starts(cells, reps, rows)
    copies = []
    for number, ((cell, shift, slot), begin) in enumerate(starts.items()):
        source = parts[shift].at[slot] if cells == 1 else parts[0].at[cell, shift, slot]
        copies.append(
            pltpu.make_async_copy(
                source, weights.at[:, pl.ds(begin, rows)], weight_sems.at[number]
            )
        )
    for copy in copies:
        copy.start()
    fetch_rows(near, far, own, got, (keys, targets), row_sems)
    for copy in copies:
        copy.wait()
    for which in range(3):
        store_split(wide, (which,), weights[which])
    size = keys.shape[1]

    @pl.loop(0, CELL)
    def _(block):
        wait_rows((keys, targets), block, row_sems)
        where = pl.ds(pl.multiple_of(block * size, size), size)
        key, target = split(keys[block]), split(targets[block])
        gate_pre = dot3(key, pair_of(wide, 0), NN)
        up_pre = dot3(key, pair_of(wide, 1), NN)
        back = dot3(target, pair_of(wide, 2), NN)
        gates[where] = gate_pre
        ups[where] = up_pre
        backs[where] = back
        _, act, slope = silu_parts(gate_pre)
        store_split(acts, (0, where), back * up_pre * slope)
        store_split(acts, (1, where), back * act)
        store_split(acts, (2, where), act * up_pre)
        for part in range(2):
            turned[part, 0, :, where] = key[part].T
            turned[part, 1, :, where] = target[part].T

    for which in range(3):
        steps[which] = dot3(pair_of(turned, which // 2), pair_of(acts, which), NN)


def renew_kernel(weights, steps, high, low):
    for which in range(3):
        weight = weights[which]
        moved = weight - steps[which]
        old = jnp.mean(weight * weight, axis=0, keepdims=True) + EPSILON
        new = jnp.mean(moved * moved, axis=0, keepdims=True) + EPSILON
        high[which], low[which] = split(moved * (jnp.sqrt(old) / jnp.sqrt(new)))


def read_kernel(*refs):
    near, far, (own, got, high, low), refs = refs[:3], refs[3:6], refs[6:10], refs[10:]
    totals, near_out, far_out, scratch = refs[0], refs[1:4], refs[4], refs[5:]
    queries, cots, turned, acts, sent, row_sems, out_sems = scratch
    fetch_rows(near, far, own, got, (queries, cots), row_sems)
    size = queries.shape[1]
    half = size // 2

    def weight(which):
        return high[which], low[which]

    def outgoing(block):
        if block < ROUNDS:
            return [
                (sent.at[block, pl.ds(0, half)], near_out[block]),
                (sent.at[block, pl.ds(half, half)], far_out.at[pl.ds(block * half, half)]),
            ]
        return [(sent.at[block], far_out.at[pl.ds(ROUNDS * half, size)])]

    @pl.loop(0, CELL)
    def _(block):
        wait_rows((queries, cots), block, row_sems)
        where = pl.ds(pl.multiple_of(block * size, size), size)
        query, cot = split(queries[block]), split(cots[block])
        gate_pre = dot3(query, weight(0), NN)
        up_pre = dot3(query, weight(1), NN)
        back = dot3(cot, weight(2), NN)
        _, act, slope = silu_parts(gate_pre)
        gate_back = split(back * up_pre * slope)
        up_back = split(back * act)
        for part in range(2):
            acts[part, 0, where] = gate_back[part]
            acts[part, 1, where] = up_back[part]
            turned[part, 0, :, where] = query[part].T
            turned[part, 1, :, where] = cot[part].T
        store_split(acts, (2, where), act * up_pre)
        sent[block] = dot3(gate_back, weight(0), NT) + dot3(up_back, weight(1), NT)
        for number in range(CELL):

            @pl.when(block == number)
            def _():
                for side, (source, out) in enumerate(outgoing(number)):
                    pltpu.make_async_copy(source, out, out_sems.at[number, side]).start()

    for which in range(3):
        totals[which] = dot3(pair_of(turned, which // 2), pair_of(acts, which), NN)
    for block in range(CELL):
        for side, (source, out) in enumerate(outgoing(block)):
            pltpu.make_async_copy(source, out, out_sems.at[block, side]).wait()


def weight_grad_kernel(cells, reps, *refs):
    near, far, (own, got), refs = refs[:3], refs[3:6], refs[6:8], refs[8:]
    (weights, steps, totals, gates, ups, backs), refs = refs[:6], refs[6:]
    (cots, acts), pieces, scratch = refs[:2], refs[2 : 2 + reps], refs[2 + reps :]
    keys, targets, turned, grads, row_sems, grad_sems = scratch
    fetch_rows(near, far, own, got, (keys, targets), row_sems)
    size = keys.shape[1]
    scale = 1.0 / weights.shape[1]
    for which in range(3):
        weight, total = weights[which], totals[which]
        moved = weight - steps[which]
        old = jnp.mean(weight * weight, axis=0, keepdims=True) + EPSILON
        new = jnp.mean(moved * moved, axis=0, keepdims=True) + EPSILON
        ratio = jnp.sqrt(old) / jnp.sqrt(new)
        ratio_cot = jnp.sum(total * moved, axis=0, keepdims=True) * scale
        moved_cot = ratio * (total - moved * (ratio_cot / new))
        direct = moved_cot + weight * (ratio_cot * ratio / old)
        if cells > 1:
            direct = direct * jnp.where(lax.axis_index("tok") < CELL, 1.0, 0.0)
        grads[which] = direct
        store_split(cots, (which,), -moved_cot)

    @pl.loop(0, CELL)
    def _(block):
        wait_rows((keys, targets), block, row_sems)
        where = pl.ds(pl.multiple_of(block * size, size), size)
        key, target = split(keys[block]), split(targets[block])
        gate_back_cot = dot3(key, pair_of(cots, 0), NN)
        up_back_cot = dot3(key, pair_of(cots, 1), NN)
        hidden_cot = dot3(target, pair_of(cots, 2), NN)
        gate_pre, up_pre, back = gates[where], ups[where], backs[where]
        sigma, act, slope = silu_parts(gate_pre)
        bend = sigma * (1.0 - sigma) * (2.0 + gate_pre * (1.0 - 2.0 * sigma))
        mixed = gate_back_cot * slope
        store_split(
            acts,
            (0, where),
            gate_back_cot * back * up_pre * bend
            + (up_back_cot * back + hidden_cot * up_pre) * slope,
        )
        store_split(acts, (1, where), mixed * back + hidden_cot * act)
        store_split(acts, (2, where), mixed * up_pre + up_back_cot * act)
        for part in range(2):
            turned[part, 0, :, where] = key[part].T
            turned[part, 1, :, where] = target[part].T

    for which in range(3):
        grads[which] += dot3(pair_of(turned, which // 2), pair_of(acts, which), NN)
    rows = pieces[0].shape[-2]
    copies = []
    place, core = position()
    rep = lax.axis_index("rep")
    for cell in range(cells):
        for shift in range(reps):
            owner_rep = lax.rem(rep + shift, reps)
            for slot in range(CELL):
                spot = spot_of(place, core, slot)
                begin = pl.multiple_of(((cell * CELL + spot) * reps + owner_rep) * rows, rows)
                copies.append(
                    pltpu.make_async_copy(
                        grads.at[:, pl.ds(begin, rows)],
                        pieces[shift].at[cell, slot],
                        grad_sems.at[len(copies)],
                    )
                )
    run_copies(copies)


def token_grad_kernel(first, last, *refs):
    (weights, cots, acts, gates, ups, backs), refs = refs[:6], refs[6:]
    rounds = min(last, ROUNDS) - first
    near_out, far_out, (wide, sent, out_sems) = refs[:rounds], refs[rounds], refs[rounds + 1 :]
    size = sent.shape[2]
    half = size // 2
    for which in range(3):
        store_split(wide, (which,), weights[which])

    def outgoing(number):
        if number < rounds:
            near = [
                (sent.at[which, number, pl.ds(0, half)], near_out[number].at[pl.ds(which * half, half)])
                for which in range(2)
            ]
            far = [
                (
                    sent.at[which, number, pl.ds(half, half)],
                    far_out.at[pl.ds(number * size + which * half, half)],
                )
                for which in range(2)
            ]
            return near + far
        return [
            (sent.at[which, number], far_out.at[pl.ds((rounds + which) * size, size)])
            for which in range(2)
        ]

    @pl.loop(0, last - first)
    def _(number):
        where = pl.ds(pl.multiple_of((first + number) * size, size), size)
        gate_pre, up_pre, back = gates[where], ups[where], backs[where]
        _, act, slope = silu_parts(gate_pre)
        sent[0, number] = (
            dot3(pair_of(acts, 0, where), pair_of(wide, 0), NT)
            + dot3(pair_of(acts, 1, where), pair_of(wide, 1), NT)
            + dot3(split(back * up_pre * slope), pair_of(cots, 0), NT)
            + dot3(split(back * act), pair_of(cots, 1), NT)
        )
        sent[1, number] = dot3(pair_of(acts, 2, where), pair_of(wide, 2), NT) + dot3(
            split(act * up_pre), pair_of(cots, 2), NT
        )
        for each in range(last - first):

            @pl.when(number == each)
            def _():
                for side, (source, out) in enumerate(outgoing(each)):
                    pltpu.make_async_copy(source, out, out_sems.at[each, side]).start()

    for each in range(last - first):
        for side, (source, out) in enumerate(outgoing(each)):
            pltpu.make_async_copy(source, out, out_sems.at[each, side]).wait()


def call(kernel, inputs, in_specs, outs, out_specs, scratch, flops=0):
    moved = sum(math.prod(value.shape) * value.dtype.itemsize for value in list(inputs) + list(outs))
    return pl.pallas_call(
        kernel,
        out_shape=outs,
        in_specs=in_specs,
        out_specs=out_specs,
        scratch_shapes=scratch,
        cost_estimate=pl.CostEstimate(flops=flops, bytes_accessed=moved, transcendentals=0),
        compiler_params=pltpu.CompilerParams(vmem_limit_bytes=26 << 20),
    )(*inputs)


def per_device(
    query_rows, key_rows, value_rows, step_logits, read_cotangent, fast_gate, fast_up, fast_down
):
    tokens_here, depth = key_rows.shape[2:]
    half = tokens_here // 2
    tok_size = lax.axis_size("tok")
    reps = lax.axis_size("rep")
    cells = tok_size // CELL
    assert tok_size % CELL == 0 and lax.axis_size("head") == 2
    factor = 1.0 / (8.0 * math.sqrt(tokens_here * tok_size))
    pairs = routes(cells)
    place, core = position()
    turn0, turn1 = halves_sent(place, core)
    at_home = place == home_of(0) + core
    cell_groups = [[cell * CELL + spot for cell in range(cells)] for spot in range(CELL)]
    rows, width = fast_gate.shape[1:]
    cols = width // 2
    shape = jax.ShapeDtypeStruct
    dma = pltpu.SemaphoreType.DMA

    def shifted(shift, sign):
        return [(rep, (rep + sign * shift) % reps) for rep in range(reps)]

    step = jax.nn.softplus(step_logits[0, 0]) * factor

    packed = call(
        pack_weights_kernel,
        (fast_gate[0], fast_up[0], fast_down[0]),
        [HBM] * 3,
        [shape((3, rows, cols), F32)] * (ROUNDS + 2),
        [HBM] * (ROUNDS + 2),
        [dma((ROUNDS + 2, 3))],
    )
    slots = [lax.ppermute(packed[turn], PLACE, pairs[turn]) for turn in range(ROUNDS)]
    other = lax.ppermute(packed[ROUNDS + 1], "head", SWAP)
    (together,) = call(
        collect_kernel,
        slots + [packed[ROUNDS], other],
        [HBM] * 5,
        [shape((CELL, 3, rows, cols), F32)],
        [HBM],
        [dma((CELL,))],
    )
    parts = [together]
    for shift in range(1, reps):
        parts.append(lax.ppermute(together, "rep", shifted(shift, 1)))
    if cells > 1:
        parts = [lax.all_gather(jnp.stack(parts), "tok", axis_index_groups=cell_groups)]

    def gather(first, second, scale):
        outs = [shape((2 * half, depth), F32)] * ROUNDS + [shape((4 * half, depth), F32)]
        scratch = [dma((CELL, 2))]
        inputs, specs = [first, second], [HBM, HBM]
        if scale is not None:
            inputs, specs = inputs + [scale], specs + [VMEM]
            scratch = [pltpu.VMEM((2 * half, depth), F32)] + scratch + [dma]
        packed = call(
            functools.partial(pack_rows_kernel, scale is not None, half),
            inputs,
            specs,
            outs,
            [HBM] * CELL,
            scratch,
        )
        near = [lax.ppermute(packed[turn], PLACE, pairs[turn]) for turn in range(ROUNDS)]
        got = lax.ppermute(packed[ROUNDS], "head", SWAP)
        return near, [packed[ROUNDS], got]

    def spread(near, local):
        return near + [lax.ppermute(piece, "head", SWAP) for piece in near] + local

    def hand_back(near, far, first):
        across = lax.ppermute(far, "head", SWAP)
        length = near[0].shape[0]
        back = []
        for number, part in enumerate(near):
            total = part + across[number * length : (number + 1) * length]
            back.append(lax.ppermute(total, PLACE, flipped(pairs[first + number])))
        return back, far[len(near) * length :] + across[len(near) * length :]

    def settle(back, local):
        def choose(turn):
            return jnp.where(turn == 0, back[0], jnp.where(turn == 1, back[1], back[2]))

        low, high = choose(turn0), choose(turn1)
        found = []
        for which in range(low.shape[0] // half):
            span = slice(which * half, (which + 1) * half)
            remote = jnp.concatenate((low[span], high[span]))
            here = local[which * 2 * half : (which + 1) * 2 * half]
            found.append(jnp.where(at_home, here, remote))
        return found

    inner_near, inner_local = gather(key_rows[0, 0], value_rows[0, 0], -step[:, None])
    read_near, read_local = gather(query_rows[0, 0], read_cotangent[0, 0], None)
    inner_rows = spread(inner_near, inner_local)

    size = 2 * half
    count = CELL * size
    square = shape((3, width, cols), F32)
    tall = shape((count, cols), F32)
    product = 6 * count * width * cols
    buffers = [pltpu.VMEM((CELL, size, depth), F32)] * 2
    turned = pltpu.VMEM((2, 2, depth, count), BF16)
    acts = pltpu.VMEM((2, 3, count, cols), BF16)
    split_square = pltpu.VMEM((2, 3, width, cols), BF16)
    weights, gates, ups, backs, steps = call(
        functools.partial(inner_kernel, cells, reps),
        parts + inner_rows,
        [HBM] * (len(parts) + 8),
        [square, tall, tall, tall, square],
        [VMEM] * 5,
        buffers
        + [split_square, turned, acts, dma((CELL, 4)), dma((cells * reps * CELL,))],
        6 * product,
    )
    if cells > 1:
        steps = lax.psum(steps, "tok", axis_index_groups=cell_groups)
    narrow = shape((3, width, cols), BF16)
    high, low = call(
        renew_kernel, (weights, steps), [VMEM] * 2, [narrow, narrow], [VMEM] * 2, []
    )
    *read_near, high = lax.optimization_barrier((*read_near, high))
    read_rows = spread(list(read_near), read_local)
    piece = shape((half, depth), F32)
    read = call(
        read_kernel,
        read_rows + [high, low],
        [HBM] * 8 + [VMEM] * 2,
        [square] + [piece] * ROUNDS + [shape((ROUNDS * half + size, depth), F32)],
        [VMEM] + [HBM] * (ROUNDS + 1),
        buffers
        + [turned, acts, pltpu.VMEM((CELL, size, depth), F32), dma((CELL, 4)), dma((CELL, 2))],
        8 * product,
    )
    totals = read[0]
    if cells > 1:
        totals = lax.psum(totals, "tok", axis_index_groups=cell_groups)
    cots, acts_cot, *given = call(
        functools.partial(weight_grad_kernel, cells, reps),
        inner_rows + [weights, steps, totals, gates, ups, backs],
        [HBM] * 8 + [VMEM] * 6,
        [shape((2, 3, width, cols), BF16), shape((2, 3, count, cols), BF16)]
        + [shape((cells, CELL, 3, rows, cols), F32)] * reps,
        [VMEM] * 2 + [HBM] * reps,
        buffers
        + [
            turned,
            pltpu.VMEM((3, width, cols), F32),
            dma((CELL, 4)),
            dma((cells * reps * CELL,)),
        ],
        6 * product,
    )
    query_back, query_local = hand_back(read[1:4], read[4], 0)
    middle = 2
    piece = shape((size, depth), F32)
    back = []
    for first, last in ((0, middle), (middle, CELL)):
        rounds = min(last, ROUNDS) - first
        over = size * (2 * (last - first) - rounds)
        out = call(
            functools.partial(token_grad_kernel, first, last),
            [weights, cots, acts_cot, gates, ups, backs],
            [VMEM] * 6,
            [piece] * rounds + [shape((over, depth), F32)],
            [HBM] * (rounds + 1),
            [split_square, pltpu.VMEM((2, last - first, size, depth), F32), dma((last - first, 4))],
            6 * product * (last - first) // CELL,
        )
        returned, local = hand_back(out[:rounds], out[rounds], first)
        back += returned
    (query_grad,) = settle(query_back, query_local)
    key_grad, target_grad = settle(back, local)

    if cells > 1:
        given = [
            lax.psum_scatter(value, "tok", scatter_dimension=0, tiled=True, axis_index_groups=cell_groups)
            for value in given
        ]
    total = given[0][0]
    for shift in range(1, reps):
        total = total + lax.ppermute(given[shift][0], "rep", shifted(shift, 1))
    returned = [
        lax.ppermute(total[turn], PLACE, flipped(pairs[turn])) for turn in range(ROUNDS)
    ]
    home_piece = total[ROUNDS]
    home_other = lax.ppermute(home_piece, "head", SWAP)

    def choose(turn):
        return jnp.where(turn == 0, returned[0], jnp.where(turn == 1, returned[1], returned[2]))

    left = jnp.where(at_home, jnp.where(core == 0, home_piece, home_other), choose(turn0))
    right = jnp.where(at_home, jnp.where(core == 0, home_other, home_piece), choose(turn1))
    owned = jnp.concatenate((left, right), axis=2)

    value_grad = -step[:, None] * target_grad
    step_grad = -jnp.sum(value_rows[0, 0] * target_grad, axis=1)
    logit_grad = step_grad * factor * jax.nn.sigmoid(step_logits[0, 0])
    return (
        query_grad[None, None],
        key_grad[None, None],
        value_grad[None, None],
        logit_grad[None, None],
        owned[0][None],
        owned[1][None],
        owned[2][None],
    )


def solution(mesh):
    tokens = P(("groups", "rep"), "head", "tok", None)
    logits = P(("groups", "rep"), "head", "tok")
    weight = P("head", ("tok", "rep"), None)
    grad = P(("groups", "head"), ("tok", "rep"), None)
    return jax.shard_map(
        per_device,
        mesh=mesh,
        in_specs=(tokens, tokens, tokens, logits, tokens, weight, weight, weight),
        out_specs=(tokens, tokens, tokens, logits, grad, grad, grad),
        check_vma=False,
    )
```

```python
import functools
import math

import jax
import jax.numpy as jnp
from jax import lax
from jax.experimental import pallas as pl
from jax.experimental.pallas import tpu as pltpu
from jax.sharding import PartitionSpec as P

EPSILON = 1e-06
CELL = 4
ROUNDS = CELL - 1
PLACE = ("tok", "head")
SWAP = [(0, 1), (1, 0)]
F32 = jnp.float32
BF16 = jnp.bfloat16
NN = ((1,), (0,))
NT = ((1,), (1,))
HBM = pl.BlockSpec(memory_space=pltpu.MemorySpace.HBM)
VMEM = pl.BlockSpec(memory_space=pltpu.VMEM)


def home_of(head):
    return (CELL - 1) // 2 + head


def source_of(head, turn):
    return (home_of(head) + 1 + (turn + 2 * (1 - head)) % ROUNDS) % CELL


def routes(cells):
    rounds = []
    for turn in range(ROUNDS):
        pairs = []
        for cell in range(cells):
            here = []
            for head in range(2):
                for core in range(2):
                    origin = cell * CELL + source_of(head, turn + core)
                    home = cell * CELL + home_of(head)
                    here.append((origin * 2 + head, home * 2 + core))
            everyone = range(cell * CELL * 2, (cell + 1) * CELL * 2)
            idle = sorted(set(everyone) - {first for first, _ in here})
            free = sorted(set(everyone) - {second for _, second in here})
            pairs += here + list(zip(idle, free))
        rounds.append(pairs)
    return rounds


def flipped(pairs):
    return [(second, first) for first, second in pairs]


def split(value):
    high = value.astype(BF16)
    return high, (value - high.astype(F32)).astype(BF16)


def dot3(left, right, form):
    def one(first, second):
        return lax.dot_general(first, second, (form, ((), ())), preferred_element_type=F32)

    return one(left[0], right[0]) + (one(left[0], right[1]) + one(left[1], right[0]))


def position():
    place = lax.rem(lax.axis_index("tok"), CELL)
    core = lax.axis_index("head")
    return place, core


def spot_of(place, core, slot):
    if slot == ROUNDS:
        return place
    head = place - home_of(0)
    return lax.rem(place + 1 + lax.rem(slot + core + 2 * (1 - head) + ROUNDS, ROUNDS), CELL)


def halves_sent(place, core):
    ahead = lax.rem(place - home_of(0) - core - 1 + 2 * CELL, CELL)
    turn0 = lax.rem(ahead + 1 - core, ROUNDS)
    turn1 = lax.rem(turn0 + ROUNDS - 1, ROUNDS)
    return turn0, turn1


def run_copies(copies):
    for copy in copies:
        copy.start()
    for copy in copies:
        copy.wait()


def pack_weights_kernel(gate, up, down, *rest):
    outs, sems = rest[:-1], rest[-1]
    place, core = position()
    _, turn1 = halves_sent(place, core)
    cols = outs[0].shape[2]
    copies = []
    for piece, out in enumerate(outs):
        if piece < ROUNDS:
            part = jnp.where(turn1 == piece, 1, 0)
        else:
            part = core if piece == ROUNDS else 1 - core
        begin = pl.multiple_of(part * cols, cols)
        for which, ref in enumerate((gate, up, down)):
            copies.append(
                pltpu.make_async_copy(
                    ref.at[:, pl.ds(begin, cols)], out.at[which], sems.at[piece, which]
                )
            )
    run_copies(copies)


def collect_kernel(first, second, third, own, got, out, sems):
    place, core = position()
    mine = core == place - home_of(0)
    copies = [
        pltpu.make_async_copy(piece, out.at[slot], sems.at[slot])
        for slot, piece in enumerate((first, second, third))
    ]
    for copy in copies:
        copy.start()

    @pl.when(mine)
    def _():
        pltpu.make_async_copy(own, out.at[ROUNDS], sems.at[ROUNDS]).start()

    @pl.when(jnp.logical_not(mine))
    def _():
        pltpu.make_async_copy(got, out.at[ROUNDS], sems.at[ROUNDS]).start()

    for copy in copies:
        copy.wait()
    pltpu.make_async_copy(own, out.at[ROUNDS], sems.at[ROUNDS]).wait()


def pack_rows_kernel(scaled, half, *refs):
    if scaled:
        first, second, scale, *rest = refs
        *outs, held, sems, load_sem = rest
        load = pltpu.make_async_copy(second, held, load_sem)
        load.start()
    else:
        first, second, *rest = refs
        *outs, sems = rest
    place, core = position()
    _, turn1 = halves_sent(place, core)

    def copies_of(which, ref):
        copies = []
        for piece in range(ROUNDS):
            begin = pl.multiple_of(jnp.where(turn1 == piece, half, 0), half)
            copies.append(
                pltpu.make_async_copy(
                    ref.at[pl.ds(begin, half)],
                    outs[piece].at[pl.ds(which * half, half)],
                    sems.at[piece, which],
                )
            )
        copies.append(
            pltpu.make_async_copy(
                ref, outs[ROUNDS].at[pl.ds(which * 2 * half, 2 * half)], sems.at[ROUNDS, which]
            )
        )
        return copies

    early = copies_of(0, first)
    for copy in early:
        copy.start()
    if scaled:
        load.wait()
        held[...] = held[...] * scale[...]
        late = copies_of(1, held)
    else:
        late = copies_of(1, second)
    for copy in late:
        copy.start()
    for copy in early + late:
        copy.wait()


def fetch_rows(near, far, own, got, buffers, sems):
    half = buffers[0].shape[1] // 2
    place, core = position()
    mine = core == place - home_of(0)
    last = len(near)
    for block in range(last):
        for which in range(2):
            rows = pl.ds(which * half, half)
            for side, group in enumerate((near, far)):
                pltpu.make_async_copy(
                    group[block].at[rows],
                    buffers[which].at[block, pl.ds(side * half, half)],
                    sems.at[block, which * 2 + side],
                ).start()

    def local(source):
        for which in range(2):
            for side in range(2):
                pltpu.make_async_copy(
                    source.at[pl.ds((which * 2 + side) * half, half)],
                    buffers[which].at[last, pl.ds(side * half, half)],
                    sems.at[last, which * 2 + side],
                ).start()

    if own is None:
        return

    @pl.when(mine)
    def _():
        local(own)

    @pl.when(jnp.logical_not(mine))
    def _():
        local(got)


def wait_rows(buffers, block, sems):
    half = buffers[0].shape[1] // 2
    for part in range(4):
        view = buffers[part // 2].at[block, pl.ds((part % 2) * half, half)]
        pltpu.make_async_copy(view, view, sems.at[block, part]).wait()


def row_starts(cells, reps, rows):
    place, core = position()
    rep = lax.axis_index("rep")
    starts = {}
    for cell in range(cells):
        for shift in range(reps):
            owner_rep = lax.rem(rep - shift + reps, reps)
            for slot in range(CELL):
                spot = spot_of(place, core, slot)
                begin = ((cell * CELL + spot) * reps + owner_rep) * rows
                starts[cell, shift, slot] = pl.multiple_of(begin, rows)
    return starts


def silu_parts(pre):
    sigma = jax.nn.sigmoid(pre)
    rest = 1.0 - sigma
    return sigma, pre * sigma, sigma * (1.0 + pre * rest)


def store_split(ref, index, value):
    high, low = split(value)
    ref[(0,) + index] = high
    ref[(1,) + index] = low


def pair_of(ref, *index):
    return ref[(0,) + index], ref[(1,) + index]


def inner_kernel(cells, reps, *refs):
    pieces = reps if cells == 1 else 1
    parts, refs = refs[:pieces], refs[pieces:]
    near, far, (own, got), refs = refs[:3], refs[3:6], refs[6:8], refs[8:]
    weights, gates, ups, backs, turned, steps, *scratch = refs
    keys, targets, wide, acts, row_sems, weight_sems = scratch
    rows = parts[0].shape[-2]
    starts = row_starts(cells, reps, rows)
    copies = []
    for number, ((cell, shift, slot), begin) in enumerate(starts.items()):
        source = parts[shift].at[slot] if cells == 1 else parts[0].at[cell, shift, slot]
        copies.append(
            pltpu.make_async_copy(
                source, weights.at[:, pl.ds(begin, rows)], weight_sems.at[number]
            )
        )
    for copy in copies:
        copy.start()
    fetch_rows(near, far, own, got, (keys, targets), row_sems)
    for copy in copies:
        copy.wait()
    for which in range(3):
        store_split(wide, (which,), weights[which])
    size = keys.shape[1]

    @pl.loop(0, CELL)
    def _(block):
        wait_rows((keys, targets), block, row_sems)
        where = pl.ds(pl.multiple_of(block * size, size), size)
        key, target = split(keys[block]), split(targets[block])
        gate_pre = dot3(key, pair_of(wide, 0), NN)
        up_pre = dot3(key, pair_of(wide, 1), NN)
        back = dot3(target, pair_of(wide, 2), NN)
        gates[where] = gate_pre
        ups[where] = up_pre
        backs[where] = back
        _, act, slope = silu_parts(gate_pre)
        store_split(acts, (0, where), back * up_pre * slope)
        store_split(acts, (1, where), back * act)
        store_split(acts, (2, where), act * up_pre)
        for part in range(2):
            turned[part, 0, :, where] = key[part].T
            turned[part, 1, :, where] = target[part].T

    for which in range(3):
        steps[which] = dot3(pair_of(turned, which // 2), pair_of(acts, which), NN)


def renew_kernel(weights, steps, high, low):
    for which in range(3):
        weight = weights[which]
        moved = weight - steps[which]
        old = jnp.mean(weight * weight, axis=0, keepdims=True) + EPSILON
        new = jnp.mean(moved * moved, axis=0, keepdims=True) + EPSILON
        high[which], low[which] = split(moved * (jnp.sqrt(old) / jnp.sqrt(new)))


def read_kernel(*refs):
    near, far, (own, got, high, low), refs = refs[:3], refs[3:6], refs[6:10], refs[10:]
    totals, near_out, far_out, scratch = refs[0], refs[1:4], refs[4], refs[5:]
    queries, cots, turned, acts, sent, row_sems, out_sems = scratch
    fetch_rows(near, far, own, got, (queries, cots), row_sems)
    size = queries.shape[1]
    half = size // 2

    def weight(which):
        return high[which], low[which]

    def outgoing(block):
        if block < ROUNDS:
            return [
                (sent.at[block, pl.ds(0, half)], near_out[block]),
                (sent.at[block, pl.ds(half, half)], far_out.at[pl.ds(block * half, half)]),
            ]
        return [(sent.at[block], far_out.at[pl.ds(ROUNDS * half, size)])]

    @pl.loop(0, CELL)
    def _(block):
        wait_rows((queries, cots), block, row_sems)
        where = pl.ds(pl.multiple_of(block * size, size), size)
        query, cot = split(queries[block]), split(cots[block])
        gate_pre = dot3(query, weight(0), NN)
        up_pre = dot3(query, weight(1), NN)
        back = dot3(cot, weight(2), NN)
        _, act, slope = silu_parts(gate_pre)
        gate_back = split(back * up_pre * slope)
        up_back = split(back * act)
        for part in range(2):
            acts[part, 0, where] = gate_back[part]
            acts[part, 1, where] = up_back[part]
            turned[part, 0, :, where] = query[part].T
            turned[part, 1, :, where] = cot[part].T
        store_split(acts, (2, where), act * up_pre)
        sent[block] = dot3(gate_back, weight(0), NT) + dot3(up_back, weight(1), NT)
        for number in range(CELL):

            @pl.when(block == number)
            def _():
                for side, (source, out) in enumerate(outgoing(number)):
                    pltpu.make_async_copy(source, out, out_sems.at[number, side]).start()

    for which in range(3):
        totals[which] = dot3(pair_of(turned, which // 2), pair_of(acts, which), NN)
    for block in range(CELL):
        for side, (source, out) in enumerate(outgoing(block)):
            pltpu.make_async_copy(source, out, out_sems.at[block, side]).wait()


def renew_back_kernel(cells, weights, steps, totals, cots, direct):
    scale = 1.0 / weights.shape[1]
    for which in range(3):
        weight, total = weights[which], totals[which]
        moved = weight - steps[which]
        old = jnp.mean(weight * weight, axis=0, keepdims=True) + EPSILON
        new = jnp.mean(moved * moved, axis=0, keepdims=True) + EPSILON
        ratio = jnp.sqrt(old) / jnp.sqrt(new)
        ratio_cot = jnp.sum(total * moved, axis=0, keepdims=True) * scale
        moved_cot = ratio * (total - moved * (ratio_cot / new))
        grad = moved_cot + weight * (ratio_cot * ratio / old)
        if cells > 1:
            grad = grad * jnp.where(lax.axis_index("tok") < CELL, 1.0, 0.0)
        direct[which] = grad
        store_split(cots, (which,), -moved_cot)


def token_grad_kernel(first, last, *refs):
    rounds = min(last, ROUNDS) - first
    near, far, refs = refs[:rounds], refs[rounds : 2 * rounds], refs[2 * rounds :]
    own, got = None, None
    if last > ROUNDS:
        (own, got), refs = refs[:2], refs[2:]
    (weights, cots, gates, ups, backs), refs = refs[:5], refs[5:]
    acts, near_out, far_out, scratch = refs[0], refs[1 : 1 + rounds], refs[1 + rounds], refs[2 + rounds :]
    keys, targets, wide, sent, row_sems, out_sems = scratch
    fetch_rows(near, far, own, got, (keys, targets), row_sems)
    size = sent.shape[2]
    half = size // 2
    for which in range(3):
        store_split(wide, (which,), weights[which])

    def outgoing(number):
        if number < rounds:
            near = [
                (sent.at[which, number, pl.ds(0, half)], near_out[number].at[pl.ds(which * half, half)])
                for which in range(2)
            ]
            far = [
                (
                    sent.at[which, number, pl.ds(half, half)],
                    far_out.at[pl.ds(number * size + which * half, half)],
                )
                for which in range(2)
            ]
            return near + far
        return [
            (sent.at[which, number], far_out.at[pl.ds((rounds + which) * size, size)])
            for which in range(2)
        ]

    @pl.loop(0, last - first)
    def _(number):
        wait_rows((keys, targets), number, row_sems)
        where = pl.ds(pl.multiple_of((first + number) * size, size), size)
        here = pl.ds(pl.multiple_of(number * size, size), size)
        key, target = split(keys[number]), split(targets[number])
        gate_back_cot = dot3(key, pair_of(cots, 0), NN)
        up_back_cot = dot3(key, pair_of(cots, 1), NN)
        hidden_cot = dot3(target, pair_of(cots, 2), NN)
        gate_pre, up_pre, back = gates[where], ups[where], backs[where]
        sigma, act, slope = silu_parts(gate_pre)
        bend = sigma * (1.0 - sigma) * (2.0 + gate_pre * (1.0 - 2.0 * sigma))
        mixed = gate_back_cot * slope
        gate_cot = split(
            gate_back_cot * back * up_pre * bend
            + (up_back_cot * back + hidden_cot * up_pre) * slope
        )
        up_cot = split(mixed * back + hidden_cot * act)
        back_cot = split(mixed * up_pre + up_back_cot * act)
        for part in range(2):
            acts[part, 0, here] = gate_cot[part]
            acts[part, 1, here] = up_cot[part]
            acts[part, 2, here] = back_cot[part]
        sent[0, number] = (
            dot3(gate_cot, pair_of(wide, 0), NT)
            + dot3(up_cot, pair_of(wide, 1), NT)
            + dot3(split(back * up_pre * slope), pair_of(cots, 0), NT)
            + dot3(split(back * act), pair_of(cots, 1), NT)
        )
        sent[1, number] = dot3(back_cot, pair_of(wide, 2), NT) + dot3(
            split(act * up_pre), pair_of(cots, 2), NT
        )
        for each in range(last - first):

            @pl.when(number == each)
            def _():
                for side, (source, out) in enumerate(outgoing(each)):
                    pltpu.make_async_copy(source, out, out_sems.at[each, side]).start()

    for each in range(last - first):
        for side, (source, out) in enumerate(outgoing(each)):
            pltpu.make_async_copy(source, out, out_sems.at[each, side]).wait()


def weight_grad_kernel(cells, reps, turned, direct, *refs):
    parts, pieces, (grads, grad_sems) = refs[: -reps - 2], refs[-reps - 2 : -2], refs[-2:]
    for which in range(3):
        total = direct[which]
        begin = 0
        for acts in parts:
            span = pl.ds(begin, acts.shape[2])
            begin += acts.shape[2]
            left = turned[0, which // 2, :, span], turned[1, which // 2, :, span]
            total = total + dot3(left, pair_of(acts, which), NN)
        grads[which] = total
    rows = pieces[0].shape[-2]
    copies = []
    place, core = position()
    rep = lax.axis_index("rep")
    for cell in range(cells):
        for shift in range(reps):
            owner_rep = lax.rem(rep + shift, reps)
            for slot in range(CELL):
                spot = spot_of(place, core, slot)
                begin = pl.multiple_of(((cell * CELL + spot) * reps + owner_rep) * rows, rows)
                copies.append(
                    pltpu.make_async_copy(
                        grads.at[:, pl.ds(begin, rows)],
                        pieces[shift].at[cell, slot],
                        grad_sems.at[len(copies)],
                    )
                )
    run_copies(copies)


def call(kernel, inputs, in_specs, outs, out_specs, scratch, flops=0, grant=26):
    moved = sum(math.prod(value.shape) * value.dtype.itemsize for value in list(inputs) + list(outs))
    return pl.pallas_call(
        kernel,
        out_shape=outs,
        in_specs=in_specs,
        out_specs=out_specs,
        scratch_shapes=scratch,
        cost_estimate=pl.CostEstimate(flops=flops, bytes_accessed=moved, transcendentals=0),
        compiler_params=pltpu.CompilerParams(vmem_limit_bytes=grant << 20),
    )(*inputs)


def per_device(
    query_rows, key_rows, value_rows, step_logits, read_cotangent, fast_gate, fast_up, fast_down
):
    tokens_here, depth = key_rows.shape[2:]
    half = tokens_here // 2
    tok_size = lax.axis_size("tok")
    reps = lax.axis_size("rep")
    cells = tok_size // CELL
    assert tok_size % CELL == 0 and lax.axis_size("head") == 2
    factor = 1.0 / (8.0 * math.sqrt(tokens_here * tok_size))
    pairs = routes(cells)
    place, core = position()
    turn0, turn1 = halves_sent(place, core)
    at_home = place == home_of(0) + core
    cell_groups = [[cell * CELL + spot for cell in range(cells)] for spot in range(CELL)]
    rows, width = fast_gate.shape[1:]
    cols = width // 2
    shape = jax.ShapeDtypeStruct
    dma = pltpu.SemaphoreType.DMA

    def shifted(shift, sign):
        return [(rep, (rep + sign * shift) % reps) for rep in range(reps)]

    step = jax.nn.softplus(step_logits[0, 0]) * factor

    packed = call(
        pack_weights_kernel,
        (fast_gate[0], fast_up[0], fast_down[0]),
        [HBM] * 3,
        [shape((3, rows, cols), F32)] * (ROUNDS + 2),
        [HBM] * (ROUNDS + 2),
        [dma((ROUNDS + 2, 3))],
        grant=60,
    )
    packed = list(packed)
    packed[0], value_first = lax.optimization_barrier((packed[0], value_rows[0, 0]))
    slots = [lax.ppermute(packed[turn], PLACE, pairs[turn]) for turn in range(ROUNDS)]
    slots[0], other = lax.optimization_barrier((slots[0], packed[ROUNDS + 1]))
    other = lax.ppermute(other, "head", SWAP)
    (together,) = call(
        collect_kernel,
        slots + [packed[ROUNDS], other],
        [HBM] * 5,
        [shape((CELL, 3, rows, cols), F32)],
        [HBM],
        [dma((CELL,))],
    )
    parts = [together]
    for shift in range(1, reps):
        parts.append(lax.ppermute(together, "rep", shifted(shift, 1)))
    if cells > 1:
        parts = [lax.all_gather(jnp.stack(parts), "tok", axis_index_groups=cell_groups)]

    def gather(first, second, scale):
        outs = [shape((2 * half, depth), F32)] * ROUNDS + [shape((4 * half, depth), F32)]
        scratch = [dma((CELL, 2))]
        inputs, specs = [first, second], [HBM, HBM]
        if scale is not None:
            inputs, specs = inputs + [scale], specs + [VMEM]
            scratch = [pltpu.VMEM((2 * half, depth), F32)] + scratch + [dma]
        packed = call(
            functools.partial(pack_rows_kernel, scale is not None, half),
            inputs,
            specs,
            outs,
            [HBM] * CELL,
            scratch,
            grant=60 if scale is not None else 26,
        )
        near = [lax.ppermute(packed[turn], PLACE, pairs[turn]) for turn in range(ROUNDS)]
        near[0], local = lax.optimization_barrier((near[0], packed[ROUNDS]))
        return near, [local, lax.ppermute(local, "head", SWAP)]

    def spread(near, local):
        return near + [lax.ppermute(piece, "head", SWAP) for piece in near] + local

    def combine(near, far):
        across = lax.ppermute(far, "head", SWAP)
        length = near[0].shape[0]
        found = [
            part + across[number * length : (number + 1) * length]
            for number, part in enumerate(near)
        ]
        return found, far[len(near) * length :] + across[len(near) * length :]

    def hand_back(totals, first):
        return [
            lax.ppermute(total, PLACE, flipped(pairs[first + number]))
            for number, total in enumerate(totals)
        ]

    def settle(back, local):
        def choose(turn):
            return jnp.where(turn == 0, back[0], jnp.where(turn == 1, back[1], back[2]))

        low, high = choose(turn0), choose(turn1)
        found = []
        for which in range(low.shape[0] // half):
            span = slice(which * half, (which + 1) * half)
            remote = jnp.concatenate((low[span], high[span]))
            here = local[which * 2 * half : (which + 1) * 2 * half]
            found.append(jnp.where(at_home, here, remote))
        return found

    inner_near, inner_local = gather(key_rows[0, 0], value_first, -step[:, None])
    inner_near[0], queries = lax.optimization_barrier((inner_near[0], query_rows[0, 0]))
    read_near, read_local = gather(queries, read_cotangent[0, 0], None)
    inner_rows = spread(inner_near, inner_local)

    size = 2 * half
    count = CELL * size
    square = shape((3, width, cols), F32)
    tall = shape((count, cols), F32)
    product = 6 * count * width * cols
    buffers = [pltpu.VMEM((CELL, size, depth), F32)] * 2
    turned = pltpu.VMEM((2, 2, depth, count), BF16)
    acts = pltpu.VMEM((2, 3, count, cols), BF16)
    split_square = pltpu.VMEM((2, 3, width, cols), BF16)
    weights, gates, ups, backs, key_turned, steps = call(
        functools.partial(inner_kernel, cells, reps),
        parts + inner_rows,
        [HBM] * (len(parts) + 8),
        [square, tall, tall, tall, shape((2, 2, depth, count), BF16), square],
        [VMEM] * 6,
        buffers + [split_square, acts, dma((CELL, 4)), dma((cells * reps * CELL,))],
        6 * product,
    )
    if cells > 1:
        steps = lax.psum(steps, "tok", axis_index_groups=cell_groups)
    narrow = shape((3, width, cols), BF16)
    high, low = call(
        renew_kernel, (weights, steps), [VMEM] * 2, [narrow, narrow], [VMEM] * 2, []
    )
    *read_near, high = lax.optimization_barrier((*read_near, high))
    read_rows = spread(list(read_near), read_local)
    piece = shape((half, depth), F32)
    read = call(
        read_kernel,
        read_rows + [high, low],
        [HBM] * 8 + [VMEM] * 2,
        [square] + [piece] * ROUNDS + [shape((ROUNDS * half + size, depth), F32)],
        [VMEM] + [HBM] * (ROUNDS + 1),
        buffers
        + [turned, acts, pltpu.VMEM((CELL, size, depth), F32), dma((CELL, 4)), dma((CELL, 2))],
        8 * product,
    )
    totals = read[0]
    if cells > 1:
        totals = lax.psum(totals, "tok", axis_index_groups=cell_groups)
    cots, direct = call(
        functools.partial(renew_back_kernel, cells),
        [weights, steps, totals],
        [VMEM] * 3,
        [shape((2, 3, width, cols), BF16), square],
        [VMEM] * 2,
        [],
    )
    middle = 2

    def token_grads(first, last, cots):
        rounds = min(last, ROUNDS) - first
        span = slice(first, first + rounds)
        inputs = inner_rows[:ROUNDS][span] + inner_rows[ROUNDS : 2 * ROUNDS][span]
        if last > ROUNDS:
            inputs = inputs + inner_rows[2 * ROUNDS :]
        blocks = last - first
        acts, *outs = call(
            functools.partial(token_grad_kernel, first, last),
            inputs + [weights, cots, gates, ups, backs],
            [HBM] * len(inputs) + [VMEM] * 5,
            [shape((2, 3, blocks * size, cols), BF16)]
            + [shape((size, depth), F32)] * rounds
            + [shape((size * (2 * blocks - rounds), depth), F32)],
            [VMEM] + [HBM] * (rounds + 1),
            [pltpu.VMEM((blocks, size, depth), F32)] * 2
            + [
                split_square,
                pltpu.VMEM((2, blocks, size, depth), F32),
                dma((blocks, 4)),
                dma((blocks, 4)),
            ],
            9 * product * blocks // CELL,
        )
        return acts, outs[:rounds], outs[rounds]

    acts_first, near_first, far_first = token_grads(0, middle, cots)
    query_totals, query_local = combine(read[1:4], read[4])
    cots, *query_totals = lax.optimization_barrier((cots, *query_totals))
    query_back = hand_back(query_totals, 0)
    acts_last, near_last, far_last = token_grads(middle, CELL, cots)
    acts_last, *near_first = lax.optimization_barrier((acts_last, *near_first))
    totals_first, _ = combine(near_first, far_first)
    acts_last, *totals_first = lax.optimization_barrier((acts_last, *totals_first))
    back = hand_back(totals_first, 0)
    given = call(
        functools.partial(weight_grad_kernel, cells, reps),
        [key_turned, direct, acts_first, acts_last],
        [VMEM] * 4,
        [shape((cells, CELL, 3, rows, cols), F32)] * reps,
        [HBM] * reps,
        [pltpu.VMEM((3, width, cols), F32), dma((cells * reps * CELL,))],
        3 * product,
    )
    given = list(given)
    far_last, given[0], *query_back = lax.optimization_barrier((far_last, given[0], *query_back))
    totals_last, local = combine(near_last, far_last)
    given[0], *totals_last = lax.optimization_barrier((given[0], *totals_last))
    back += hand_back(totals_last, middle)
    (query_grad,) = settle(query_back, query_local)
    key_grad, target_grad = settle(back, local)

    if cells > 1:
        given = [
            lax.psum_scatter(value, "tok", scatter_dimension=0, tiled=True, axis_index_groups=cell_groups)
            for value in given
        ]
    total = given[0][0]
    for shift in range(1, reps):
        total = total + lax.ppermute(given[shift][0], "rep", shifted(shift, 1))
    returned = [
        lax.ppermute(total[turn], PLACE, flipped(pairs[turn])) for turn in range(ROUNDS)
    ]
    home_piece = total[ROUNDS]
    home_other = lax.ppermute(home_piece, "head", SWAP)

    def choose(turn):
        return jnp.where(turn == 0, returned[0], jnp.where(turn == 1, returned[1], returned[2]))

    left = jnp.where(at_home, jnp.where(core == 0, home_piece, home_other), choose(turn0))
    right = jnp.where(at_home, jnp.where(core == 0, home_other, home_piece), choose(turn1))
    owned = jnp.concatenate((left, right), axis=2)

    value_grad = -step[:, None] * target_grad
    step_grad = -jnp.sum(value_rows[0, 0] * target_grad, axis=1)
    logit_grad = step_grad * factor * jax.nn.sigmoid(step_logits[0, 0])
    return (
        query_grad[None, None],
        key_grad[None, None],
        value_grad[None, None],
        logit_grad[None, None],
        owned[0][None],
        owned[1][None],
        owned[2][None],
    )


def solution(mesh):
    tokens = P(("groups", "rep"), "head", "tok", None)
    logits = P(("groups", "rep"), "head", "tok")
    weight = P("head", ("tok", "rep"), None)
    grad = P(("groups", "head"), ("tok", "rep"), None)
    return jax.shard_map(
        per_device,
        mesh=mesh,
        in_specs=(tokens, tokens, tokens, logits, tokens, weight, weight, weight),
        out_specs=(tokens, tokens, tokens, logits, grad, grad, grad),
        check_vma=False,
    )
```

```python
import functools
import math

import jax
import jax.numpy as jnp
from jax import lax
from jax.experimental import pallas as pl
from jax.experimental.pallas import tpu as pltpu
from jax.sharding import PartitionSpec as P

EPSILON = 1e-06
CELL = 4
ROUNDS = CELL - 1
PLACE = ("tok", "head")
SWAP = [(0, 1), (1, 0)]
F32 = jnp.float32
BF16 = jnp.bfloat16
NN = ((1,), (0,))
NT = ((1,), (1,))
HBM = pl.BlockSpec(memory_space=pltpu.MemorySpace.HBM)
VMEM = pl.BlockSpec(memory_space=pltpu.VMEM)


def home_of(head):
    return (CELL - 1) // 2 + head


def source_of(head, turn):
    return (home_of(head) + 1 + (turn + 2 * (1 - head)) % ROUNDS) % CELL


def routes(cells):
    rounds = []
    for turn in range(ROUNDS):
        pairs = []
        for cell in range(cells):
            here = []
            for head in range(2):
                for core in range(2):
                    origin = cell * CELL + source_of(head, turn + core)
                    home = cell * CELL + home_of(head)
                    here.append((origin * 2 + head, home * 2 + core))
            everyone = range(cell * CELL * 2, (cell + 1) * CELL * 2)
            idle = sorted(set(everyone) - {first for first, _ in here})
            free = sorted(set(everyone) - {second for _, second in here})
            pairs += here + list(zip(idle, free))
        rounds.append(pairs)
    return rounds


def flipped(pairs):
    return [(second, first) for first, second in pairs]


def split(value):
    high = value.astype(BF16)
    return high, (value - high.astype(F32)).astype(BF16)


def dot3(left, right, form):
    def one(first, second):
        return lax.dot_general(first, second, (form, ((), ())), preferred_element_type=F32)

    return one(left[0], right[0]) + (one(left[0], right[1]) + one(left[1], right[0]))


def position():
    place = lax.rem(lax.axis_index("tok"), CELL)
    core = lax.axis_index("head")
    return place, core


def spot_of(place, core, slot):
    if slot == ROUNDS:
        return place
    head = place - home_of(0)
    return lax.rem(place + 1 + lax.rem(slot + core + 2 * (1 - head) + ROUNDS, ROUNDS), CELL)


def halves_sent(place, core):
    ahead = lax.rem(place - home_of(0) - core - 1 + 2 * CELL, CELL)
    turn0 = lax.rem(ahead + 1 - core, ROUNDS)
    turn1 = lax.rem(turn0 + ROUNDS - 1, ROUNDS)
    return turn0, turn1


def run_copies(copies):
    for copy in copies:
        copy.start()
    for copy in copies:
        copy.wait()


def pack_weights_kernel(gate, up, down, *rest):
    outs, sems = rest[:-1], rest[-1]
    place, core = position()
    _, turn1 = halves_sent(place, core)
    cols = outs[0].shape[2]
    copies = []
    for piece, out in enumerate(outs):
        if piece < ROUNDS:
            part = jnp.where(turn1 == piece, 1, 0)
        else:
            part = core if piece == ROUNDS else 1 - core
        begin = pl.multiple_of(part * cols, cols)
        for which, ref in enumerate((gate, up, down)):
            copies.append(
                pltpu.make_async_copy(
                    ref.at[:, pl.ds(begin, cols)], out.at[which], sems.at[piece, which]
                )
            )
    run_copies(copies)


def collect_kernel(first, second, third, own, got, out, sems):
    place, core = position()
    mine = core == place - home_of(0)
    copies = [
        pltpu.make_async_copy(piece, out.at[slot], sems.at[slot])
        for slot, piece in enumerate((first, second, third))
    ]
    for copy in copies:
        copy.start()

    @pl.when(mine)
    def _():
        pltpu.make_async_copy(own, out.at[ROUNDS], sems.at[ROUNDS]).start()

    @pl.when(jnp.logical_not(mine))
    def _():
        pltpu.make_async_copy(got, out.at[ROUNDS], sems.at[ROUNDS]).start()

    for copy in copies:
        copy.wait()
    pltpu.make_async_copy(own, out.at[ROUNDS], sems.at[ROUNDS]).wait()


def pack_rows_kernel(scaled, half, *refs):
    if scaled:
        first, second, scale, *outs, held, sems = refs
    else:
        first, second, *outs, sems = refs
    place, core = position()
    _, turn1 = halves_sent(place, core)

    def copies_of(which, ref):
        copies = []
        for piece in range(ROUNDS):
            begin = pl.multiple_of(jnp.where(turn1 == piece, half, 0), half)
            copies.append(
                pltpu.make_async_copy(
                    ref.at[pl.ds(begin, half)],
                    outs[piece].at[pl.ds(which * half, half)],
                    sems.at[piece, which],
                )
            )
        copies.append(
            pltpu.make_async_copy(
                ref, outs[ROUNDS].at[pl.ds(which * 2 * half, 2 * half)], sems.at[ROUNDS, which]
            )
        )
        return copies

    early = copies_of(0, first)
    for copy in early:
        copy.start()
    if scaled:
        held[...] = second[...] * scale[...]
        late = copies_of(1, held)
    else:
        late = copies_of(1, second)
    for copy in late:
        copy.start()
    for copy in early + late:
        copy.wait()


def fetch_rows(near, far, own, got, buffers, sems):
    half = buffers[0].shape[1] // 2
    place, core = position()
    mine = core == place - home_of(0)
    last = len(near)
    for block in range(last):
        for which in range(2):
            rows = pl.ds(which * half, half)
            for side, group in enumerate((near, far)):
                pltpu.make_async_copy(
                    group[block].at[rows],
                    buffers[which].at[block, pl.ds(side * half, half)],
                    sems.at[block, which * 2 + side],
                ).start()

    def local(source):
        for which in range(2):
            for side in range(2):
                pltpu.make_async_copy(
                    source.at[pl.ds((which * 2 + side) * half, half)],
                    buffers[which].at[last, pl.ds(side * half, half)],
                    sems.at[last, which * 2 + side],
                ).start()

    if own is None:
        return

    @pl.when(mine)
    def _():
        local(own)

    @pl.when(jnp.logical_not(mine))
    def _():
        local(got)


def wait_rows(buffers, block, sems):
    half = buffers[0].shape[1] // 2
    for part in range(4):
        view = buffers[part // 2].at[block, pl.ds((part % 2) * half, half)]
        pltpu.make_async_copy(view, view, sems.at[block, part]).wait()


def row_starts(cells, reps, rows):
    place, core = position()
    rep = lax.axis_index("rep")
    starts = {}
    for cell in range(cells):
        for shift in range(reps):
            owner_rep = lax.rem(rep - shift + reps, reps)
            for slot in range(CELL):
                spot = spot_of(place, core, slot)
                begin = ((cell * CELL + spot) * reps + owner_rep) * rows
                starts[cell, shift, slot] = pl.multiple_of(begin, rows)
    return starts


def silu_parts(pre):
    sigma = jax.nn.sigmoid(pre)
    rest = 1.0 - sigma
    return sigma, pre * sigma, sigma * (1.0 + pre * rest)


def store_split(ref, index, value):
    high, low = split(value)
    ref[(0,) + index] = high
    ref[(1,) + index] = low


def pair_of(ref, *index):
    return ref[(0,) + index], ref[(1,) + index]


def inner_kernel(cells, reps, *refs):
    pieces = reps if cells == 1 else 1
    parts, refs = refs[:pieces], refs[pieces:]
    near, far, (own, got), refs = refs[:3], refs[3:6], refs[6:8], refs[8:]
    weights, gates, ups, backs, turned, steps, *scratch = refs
    keys, targets, wide, acts, row_sems, weight_sems = scratch
    rows = parts[0].shape[-2]
    starts = row_starts(cells, reps, rows)
    copies = []
    for number, ((cell, shift, slot), begin) in enumerate(starts.items()):
        source = parts[shift].at[slot] if cells == 1 else parts[0].at[cell, shift, slot]
        copies.append(
            pltpu.make_async_copy(
                source, weights.at[:, pl.ds(begin, rows)], weight_sems.at[number]
            )
        )
    for copy in copies:
        copy.start()
    fetch_rows(near, far, own, got, (keys, targets), row_sems)
    for copy in copies:
        copy.wait()
    for which in range(3):
        store_split(wide, (which,), weights[which])
    size = keys.shape[1]

    @pl.loop(0, CELL)
    def _(block):
        wait_rows((keys, targets), block, row_sems)
        where = pl.ds(pl.multiple_of(block * size, size), size)
        key, target = split(keys[block]), split(targets[block])
        gate_pre = dot3(key, pair_of(wide, 0), NN)
        up_pre = dot3(key, pair_of(wide, 1), NN)
        back = dot3(target, pair_of(wide, 2), NN)
        gates[where] = gate_pre
        ups[where] = up_pre
        backs[where] = back
        _, act, slope = silu_parts(gate_pre)
        store_split(acts, (0, where), back * up_pre * slope)
        store_split(acts, (1, where), back * act)
        store_split(acts, (2, where), act * up_pre)
        for part in range(2):
            turned[part, 0, :, where] = key[part].T
            turned[part, 1, :, where] = target[part].T

    for which in range(3):
        steps[which] = dot3(pair_of(turned, which // 2), pair_of(acts, which), NN)


def renew_kernel(weights, steps, high, low):
    for which in range(3):
        weight = weights[which]
        moved = weight - steps[which]
        old = jnp.mean(weight * weight, axis=0, keepdims=True) + EPSILON
        new = jnp.mean(moved * moved, axis=0, keepdims=True) + EPSILON
        high[which], low[which] = split(moved * (jnp.sqrt(old) / jnp.sqrt(new)))


def read_kernel(*refs):
    near, far, (own, got, high, low), refs = refs[:3], refs[3:6], refs[6:10], refs[10:]
    totals, near_out, far_out, scratch = refs[0], refs[1:4], refs[4], refs[5:]
    queries, cots, turned, acts, sent, row_sems, out_sems = scratch
    fetch_rows(near, far, own, got, (queries, cots), row_sems)
    size = queries.shape[1]
    half = size // 2

    def weight(which):
        return high[which], low[which]

    def outgoing(block):
        if block < ROUNDS:
            return [
                (sent.at[block, pl.ds(0, half)], near_out[block]),
                (sent.at[block, pl.ds(half, half)], far_out.at[pl.ds(block * half, half)]),
            ]
        return [(sent.at[block], far_out.at[pl.ds(ROUNDS * half, size)])]

    @pl.loop(0, CELL)
    def _(block):
        wait_rows((queries, cots), block, row_sems)
        where = pl.ds(pl.multiple_of(block * size, size), size)
        query, cot = split(queries[block]), split(cots[block])
        gate_pre = dot3(query, weight(0), NN)
        up_pre = dot3(query, weight(1), NN)
        back = dot3(cot, weight(2), NN)
        _, act, slope = silu_parts(gate_pre)
        gate_back = split(back * up_pre * slope)
        up_back = split(back * act)
        for part in range(2):
            acts[part, 0, where] = gate_back[part]
            acts[part, 1, where] = up_back[part]
            turned[part, 0, :, where] = query[part].T
            turned[part, 1, :, where] = cot[part].T
        store_split(acts, (2, where), act * up_pre)
        sent[block] = dot3(gate_back, weight(0), NT) + dot3(up_back, weight(1), NT)
        for number in range(CELL):

            @pl.when(block == number)
            def _():
                for side, (source, out) in enumerate(outgoing(number)):
                    pltpu.make_async_copy(source, out, out_sems.at[number, side]).start()

    for which in range(3):
        totals[which] = dot3(pair_of(turned, which // 2), pair_of(acts, which), NN)
    for block in range(CELL):
        for side, (source, out) in enumerate(outgoing(block)):
            pltpu.make_async_copy(source, out, out_sems.at[block, side]).wait()


def renew_back_kernel(cells, weights, steps, totals, cots, direct):
    scale = 1.0 / weights.shape[1]
    for which in range(3):
        weight, total = weights[which], totals[which]
        moved = weight - steps[which]
        old = jnp.mean(weight * weight, axis=0, keepdims=True) + EPSILON
        new = jnp.mean(moved * moved, axis=0, keepdims=True) + EPSILON
        ratio = jnp.sqrt(old) / jnp.sqrt(new)
        ratio_cot = jnp.sum(total * moved, axis=0, keepdims=True) * scale
        moved_cot = ratio * (total - moved * (ratio_cot / new))
        grad = moved_cot + weight * (ratio_cot * ratio / old)
        if cells > 1:
            grad = grad * jnp.where(lax.axis_index("tok") < CELL, 1.0, 0.0)
        direct[which] = grad
        store_split(cots, (which,), -moved_cot)


def token_grad_kernel(first, last, *refs):
    rounds = min(last, ROUNDS) - first
    near, far, refs = refs[:rounds], refs[rounds : 2 * rounds], refs[2 * rounds :]
    own, got = None, None
    if last > ROUNDS:
        (own, got), refs = refs[:2], refs[2:]
    (weights, cots, gates, ups, backs), refs = refs[:5], refs[5:]
    acts, near_out, far_out, scratch = refs[0], refs[1 : 1 + rounds], refs[1 + rounds], refs[2 + rounds :]
    keys, targets, wide, sent, row_sems, out_sems = scratch
    fetch_rows(near, far, own, got, (keys, targets), row_sems)
    size = sent.shape[2]
    half = size // 2
    for which in range(3):
        store_split(wide, (which,), weights[which])

    def outgoing(number):
        if number < rounds:
            near = [
                (sent.at[which, number, pl.ds(0, half)], near_out[number].at[pl.ds(which * half, half)])
                for which in range(2)
            ]
            far = [
                (
                    sent.at[which, number, pl.ds(half, half)],
                    far_out.at[pl.ds(number * size + which * half, half)],
                )
                for which in range(2)
            ]
            return near + far
        return [
            (sent.at[which, number], far_out.at[pl.ds((rounds + which) * size, size)])
            for which in range(2)
        ]

    @pl.loop(0, last - first)
    def _(number):
        wait_rows((keys, targets), number, row_sems)
        where = pl.ds(pl.multiple_of((first + number) * size, size), size)
        here = pl.ds(pl.multiple_of(number * size, size), size)
        key, target = split(keys[number]), split(targets[number])
        gate_back_cot = dot3(key, pair_of(cots, 0), NN)
        up_back_cot = dot3(key, pair_of(cots, 1), NN)
        hidden_cot = dot3(target, pair_of(cots, 2), NN)
        gate_pre, up_pre, back = gates[where], ups[where], backs[where]
        sigma, act, slope = silu_parts(gate_pre)
        bend = sigma * (1.0 - sigma) * (2.0 + gate_pre * (1.0 - 2.0 * sigma))
        mixed = gate_back_cot * slope
        gate_cot = split(
            gate_back_cot * back * up_pre * bend
            + (up_back_cot * back + hidden_cot * up_pre) * slope
        )
        up_cot = split(mixed * back + hidden_cot * act)
        back_cot = split(mixed * up_pre + up_back_cot * act)
        for part in range(2):
            acts[part, 0, here] = gate_cot[part]
            acts[part, 1, here] = up_cot[part]
            acts[part, 2, here] = back_cot[part]
        sent[0, number] = (
            dot3(gate_cot, pair_of(wide, 0), NT)
            + dot3(up_cot, pair_of(wide, 1), NT)
            + dot3(split(back * up_pre * slope), pair_of(cots, 0), NT)
            + dot3(split(back * act), pair_of(cots, 1), NT)
        )
        sent[1, number] = dot3(back_cot, pair_of(wide, 2), NT) + dot3(
            split(act * up_pre), pair_of(cots, 2), NT
        )
        for each in range(last - first):

            @pl.when(number == each)
            def _():
                for side, (source, out) in enumerate(outgoing(each)):
                    pltpu.make_async_copy(source, out, out_sems.at[each, side]).start()

    for each in range(last - first):
        for side, (source, out) in enumerate(outgoing(each)):
            pltpu.make_async_copy(source, out, out_sems.at[each, side]).wait()


def weight_grad_kernel(cells, reps, turned, direct, *refs):
    parts, pieces, (grads, grad_sems) = refs[: -reps - 2], refs[-reps - 2 : -2], refs[-2:]
    for which in range(3):
        total = direct[which]
        begin = 0
        for acts in parts:
            span = pl.ds(begin, acts.shape[2])
            begin += acts.shape[2]
            left = turned[0, which // 2, :, span], turned[1, which // 2, :, span]
            total = total + dot3(left, pair_of(acts, which), NN)
        grads[which] = total
    rows = pieces[0].shape[-2]
    copies = []
    place, core = position()
    rep = lax.axis_index("rep")
    for cell in range(cells):
        for shift in range(reps):
            owner_rep = lax.rem(rep + shift, reps)
            for slot in range(CELL):
                spot = spot_of(place, core, slot)
                begin = pl.multiple_of(((cell * CELL + spot) * reps + owner_rep) * rows, rows)
                copies.append(
                    pltpu.make_async_copy(
                        grads.at[:, pl.ds(begin, rows)],
                        pieces[shift].at[cell, slot],
                        grad_sems.at[len(copies)],
                    )
                )
    run_copies(copies)


def call(kernel, inputs, in_specs, outs, out_specs, scratch, flops=0):
    moved = sum(math.prod(value.shape) * value.dtype.itemsize for value in list(inputs) + list(outs))
    return pl.pallas_call(
        kernel,
        out_shape=outs,
        in_specs=in_specs,
        out_specs=out_specs,
        scratch_shapes=scratch,
        cost_estimate=pl.CostEstimate(flops=flops, bytes_accessed=moved, transcendentals=0),
        compiler_params=pltpu.CompilerParams(vmem_limit_bytes=26 << 20),
    )(*inputs)


def per_device(
    query_rows, key_rows, value_rows, step_logits, read_cotangent, fast_gate, fast_up, fast_down
):
    tokens_here, depth = key_rows.shape[2:]
    half = tokens_here // 2
    tok_size = lax.axis_size("tok")
    reps = lax.axis_size("rep")
    cells = tok_size // CELL
    assert tok_size % CELL == 0 and lax.axis_size("head") == 2
    factor = 1.0 / (8.0 * math.sqrt(tokens_here * tok_size))
    pairs = routes(cells)
    place, core = position()
    turn0, turn1 = halves_sent(place, core)
    at_home = place == home_of(0) + core
    cell_groups = [[cell * CELL + spot for cell in range(cells)] for spot in range(CELL)]
    rows, width = fast_gate.shape[1:]
    cols = width // 2
    shape = jax.ShapeDtypeStruct
    dma = pltpu.SemaphoreType.DMA

    def shifted(shift, sign):
        return [(rep, (rep + sign * shift) % reps) for rep in range(reps)]

    step = jax.nn.softplus(step_logits[0, 0]) * factor

    packed = call(
        pack_weights_kernel,
        (fast_gate[0], fast_up[0], fast_down[0]),
        [VMEM] * 3,
        [shape((3, rows, cols), F32)] * (ROUNDS + 2),
        [HBM] * (ROUNDS + 2),
        [dma((ROUNDS + 2, 3))],
    )
    packed = list(packed)
    packed[0], value_first = lax.optimization_barrier((packed[0], value_rows[0, 0]))
    slots = [lax.ppermute(packed[turn], PLACE, pairs[turn]) for turn in range(ROUNDS)]
    slots[0], other = lax.optimization_barrier((slots[0], packed[ROUNDS + 1]))
    other = lax.ppermute(other, "head", SWAP)
    (together,) = call(
        collect_kernel,
        slots + [packed[ROUNDS], other],
        [HBM] * 5,
        [shape((CELL, 3, rows, cols), F32)],
        [HBM],
        [dma((CELL,))],
    )
    parts = [together]
    for shift in range(1, reps):
        parts.append(lax.ppermute(together, "rep", shifted(shift, 1)))
    if cells > 1:
        parts = [lax.all_gather(jnp.stack(parts), "tok", axis_index_groups=cell_groups)]

    def gather(first, second, scale):
        outs = [shape((2 * half, depth), F32)] * ROUNDS + [shape((4 * half, depth), F32)]
        scratch = [dma((CELL, 2))]
        inputs, specs = [first, second], [VMEM, VMEM]
        if scale is not None:
            inputs, specs = inputs + [scale], specs + [VMEM]
            scratch = [pltpu.VMEM((2 * half, depth), F32)] + scratch
        packed = call(
            functools.partial(pack_rows_kernel, scale is not None, half),
            inputs,
            specs,
            outs,
            [HBM] * CELL,
            scratch,
        )
        near = [lax.ppermute(packed[turn], PLACE, pairs[turn]) for turn in range(ROUNDS)]
        return near, packed[ROUNDS]

    def spread(near, local):
        far = [lax.ppermute(piece, "head", SWAP) for piece in near]
        return near + far + [local, lax.ppermute(local, "head", SWAP)]

    def combine(near, far):
        across = lax.ppermute(far, "head", SWAP)
        length = near[0].shape[0]
        found = [
            part + across[number * length : (number + 1) * length]
            for number, part in enumerate(near)
        ]
        return found, far[len(near) * length :] + across[len(near) * length :]

    def hand_back(totals, first):
        return [
            lax.ppermute(total, PLACE, flipped(pairs[first + number]))
            for number, total in enumerate(totals)
        ]

    def settle(back, local):
        def choose(turn):
            return jnp.where(turn == 0, back[0], jnp.where(turn == 1, back[1], back[2]))

        low, high = choose(turn0), choose(turn1)
        found = []
        for which in range(low.shape[0] // half):
            span = slice(which * half, (which + 1) * half)
            remote = jnp.concatenate((low[span], high[span]))
            here = local[which * 2 * half : (which + 1) * 2 * half]
            found.append(jnp.where(at_home, here, remote))
        return found

    inner_near, inner_local = gather(key_rows[0, 0], value_first, -step[:, None])
    inner_near[0], inner_local, queries = lax.optimization_barrier(
        (inner_near[0], inner_local, query_rows[0, 0])
    )
    read_near, read_local = gather(queries, read_cotangent[0, 0], None)
    inner_rows = spread(inner_near, inner_local)

    size = 2 * half
    count = CELL * size
    square = shape((3, width, cols), F32)
    tall = shape((count, cols), F32)
    product = 6 * count * width * cols
    buffers = [pltpu.VMEM((CELL, size, depth), F32)] * 2
    turned = pltpu.VMEM((2, 2, depth, count), BF16)
    acts = pltpu.VMEM((2, 3, count, cols), BF16)
    split_square = pltpu.VMEM((2, 3, width, cols), BF16)
    weights, gates, ups, backs, key_turned, steps = call(
        functools.partial(inner_kernel, cells, reps),
        parts + inner_rows,
        [HBM] * (len(parts) + 8),
        [square, tall, tall, tall, shape((2, 2, depth, count), BF16), square],
        [VMEM] * 6,
        buffers + [split_square, acts, dma((CELL, 4)), dma((cells * reps * CELL,))],
        6 * product,
    )
    if cells > 1:
        steps = lax.psum(steps, "tok", axis_index_groups=cell_groups)
    narrow = shape((3, width, cols), BF16)
    high, low = call(
        renew_kernel, (weights, steps), [VMEM] * 2, [narrow, narrow], [VMEM] * 2, []
    )
    *read_near, read_local, high = lax.optimization_barrier((*read_near, read_local, high))
    read_rows = spread(list(read_near), read_local)
    piece = shape((half, depth), F32)
    read = call(
        read_kernel,
        read_rows + [high, low],
        [HBM] * 8 + [VMEM] * 2,
        [square] + [piece] * ROUNDS + [shape((ROUNDS * half + size, depth), F32)],
        [VMEM] + [HBM] * (ROUNDS + 1),
        buffers
        + [turned, acts, pltpu.VMEM((CELL, size, depth), F32), dma((CELL, 4)), dma((CELL, 2))],
        8 * product,
    )
    totals = read[0]
    if cells > 1:
        totals = lax.psum(totals, "tok", axis_index_groups=cell_groups)
    cots, direct = call(
        functools.partial(renew_back_kernel, cells),
        [weights, steps, totals],
        [VMEM] * 3,
        [shape((2, 3, width, cols), BF16), square],
        [VMEM] * 2,
        [],
    )
    middle = 2

    def token_grads(first, last, cots):
        rounds = min(last, ROUNDS) - first
        span = slice(first, first + rounds)
        inputs = inner_rows[:ROUNDS][span] + inner_rows[ROUNDS : 2 * ROUNDS][span]
        if last > ROUNDS:
            inputs = inputs + inner_rows[2 * ROUNDS :]
        blocks = last - first
        acts, *outs = call(
            functools.partial(token_grad_kernel, first, last),
            inputs + [weights, cots, gates, ups, backs],
            [HBM] * len(inputs) + [VMEM] * 5,
            [shape((2, 3, blocks * size, cols), BF16)]
            + [shape((size, depth), F32)] * rounds
            + [shape((size * (2 * blocks - rounds), depth), F32)],
            [VMEM] + [HBM] * (rounds + 1),
            [pltpu.VMEM((blocks, size, depth), F32)] * 2
            + [
                split_square,
                pltpu.VMEM((2, blocks, size, depth), F32),
                dma((blocks, 4)),
                dma((blocks, 4)),
            ],
            9 * product * blocks // CELL,
        )
        return acts, outs[:rounds], outs[rounds]

    acts_first, near_first, far_first = token_grads(0, middle, cots)
    query_totals, query_local = combine(read[1:4], read[4])
    cots, *query_totals = lax.optimization_barrier((cots, *query_totals))
    query_back = hand_back(query_totals, 0)
    acts_last, near_last, far_last = token_grads(middle, CELL, cots)
    acts_last, *near_first = lax.optimization_barrier((acts_last, *near_first))
    totals_first, _ = combine(near_first, far_first)
    acts_last, *totals_first = lax.optimization_barrier((acts_last, *totals_first))
    back = hand_back(totals_first, 0)
    given = call(
        functools.partial(weight_grad_kernel, cells, reps),
        [key_turned, direct, acts_first, acts_last],
        [VMEM] * 4,
        [shape((cells, CELL, 3, rows, cols), F32)] * reps,
        [HBM] * reps,
        [pltpu.VMEM((3, width, cols), F32), dma((cells * reps * CELL,))],
        3 * product,
    )
    given = list(given)
    far_last, given[0], *query_back = lax.optimization_barrier((far_last, given[0], *query_back))
    totals_last, local = combine(near_last, far_last)
    given[0], *totals_last = lax.optimization_barrier((given[0], *totals_last))
    (query_grad,) = settle(query_back, query_local)
    given[0], query_grad = lax.optimization_barrier((given[0], query_grad))

    if cells > 1:
        given = [
            lax.psum_scatter(value, "tok", scatter_dimension=0, tiled=True, axis_index_groups=cell_groups)
            for value in given
        ]
    total = given[0][0]
    for shift in range(1, reps):
        total = total + lax.ppermute(given[shift][0], "rep", shifted(shift, 1))
    total, *back = lax.optimization_barrier((total, *back))
    back += hand_back(totals_last, middle)
    key_grad, target_grad = settle(back, local)
    returned = [
        lax.ppermute(total[turn], PLACE, flipped(pairs[turn])) for turn in range(ROUNDS)
    ]
    home_piece = total[ROUNDS]
    home_other = lax.ppermute(home_piece, "head", SWAP)

    def choose(turn):
        return jnp.where(turn == 0, returned[0], jnp.where(turn == 1, returned[1], returned[2]))

    left = jnp.where(at_home, jnp.where(core == 0, home_piece, home_other), choose(turn0))
    right = jnp.where(at_home, jnp.where(core == 0, home_other, home_piece), choose(turn1))
    owned = jnp.concatenate((left, right), axis=2)

    value_grad = -step[:, None] * target_grad
    step_grad = -jnp.sum(value_rows[0, 0] * target_grad, axis=1)
    logit_grad = step_grad * factor * jax.nn.sigmoid(step_logits[0, 0])
    return (
        query_grad[None, None],
        key_grad[None, None],
        value_grad[None, None],
        logit_grad[None, None],
        owned[0][None],
        owned[1][None],
        owned[2][None],
    )


def solution(mesh):
    tokens = P(("groups", "rep"), "head", "tok", None)
    logits = P(("groups", "rep"), "head", "tok")
    weight = P("head", ("tok", "rep"), None)
    grad = P(("groups", "head"), ("tok", "rep"), None)
    return jax.shard_map(
        per_device,
        mesh=mesh,
        in_specs=(tokens, tokens, tokens, logits, tokens, weight, weight, weight),
        out_specs=(tokens, tokens, tokens, logits, grad, grad, grad),
        check_vma=False,
    )
```

```python
import functools
import math

import jax
import jax.numpy as jnp
from jax import lax
from jax.experimental import pallas as pl
from jax.experimental.pallas import tpu as pltpu
from jax.sharding import PartitionSpec as P

EPSILON = 1e-06
CELL = 4
ROUNDS = CELL - 1
PLACE = ("tok", "head")
SWAP = [(0, 1), (1, 0)]
F32 = jnp.float32
BF16 = jnp.bfloat16
NN = ((1,), (0,))
NT = ((1,), (1,))
HBM = pl.BlockSpec(memory_space=pltpu.MemorySpace.HBM)
VMEM = pl.BlockSpec(memory_space=pltpu.VMEM)


def home_of(head):
    return (CELL - 1) // 2 + head


def source_of(head, turn):
    return (home_of(head) + 1 + (turn + 2 * (1 - head)) % ROUNDS) % CELL


def routes(cells):
    rounds = []
    for turn in range(ROUNDS):
        pairs = []
        for cell in range(cells):
            here = []
            for head in range(2):
                for core in range(2):
                    origin = cell * CELL + source_of(head, turn + core)
                    home = cell * CELL + home_of(head)
                    here.append((origin * 2 + head, home * 2 + core))
            everyone = range(cell * CELL * 2, (cell + 1) * CELL * 2)
            idle = sorted(set(everyone) - {first for first, _ in here})
            free = sorted(set(everyone) - {second for _, second in here})
            pairs += here + list(zip(idle, free))
        rounds.append(pairs)
    return rounds


def flipped(pairs):
    return [(second, first) for first, second in pairs]


def split(value):
    high = value.astype(BF16)
    return high, (value - high.astype(F32)).astype(BF16)


def dot3(left, right, form):
    def one(first, second):
        return lax.dot_general(first, second, (form, ((), ())), preferred_element_type=F32)

    return one(left[0], right[0]) + (one(left[0], right[1]) + one(left[1], right[0]))


def position():
    place = lax.rem(lax.axis_index("tok"), CELL)
    core = lax.axis_index("head")
    return place, core


def spot_of(place, core, slot):
    if slot == ROUNDS:
        return place
    head = place - home_of(0)
    return lax.rem(place + 1 + lax.rem(slot + core + 2 * (1 - head) + ROUNDS, ROUNDS), CELL)


def halves_sent(place, core):
    ahead = lax.rem(place - home_of(0) - core - 1 + 2 * CELL, CELL)
    turn0 = lax.rem(ahead + 1 - core, ROUNDS)
    turn1 = lax.rem(turn0 + ROUNDS - 1, ROUNDS)
    return turn0, turn1


def run_copies(copies):
    for copy in copies:
        copy.start()
    for copy in copies:
        copy.wait()


def weight_rows(rows):
    return rows * 3 // 2 if rows % 16 == 0 else rows * 2


def weight_blocks(rows, cols):
    blocks = [(0, 0, rows, 0, 0), (1, 0, rows, 0, cols)]
    if rows % 16 == 0:
        return blocks + [(2, 0, rows // 2, rows, 0), (2, rows // 2, rows // 2, rows, cols)]
    return blocks + [(2, 0, rows, rows, 0)]


def pack_kernel(half, with_weights, *refs):
    if with_weights:
        first, second, scale, gate, up, down, *outs, held, sems, weight_sems = refs
    else:
        first, second, *outs, sems = refs
    place, core = position()
    _, turn1 = halves_sent(place, core)

    def copies_of(which, ref):
        copies = []
        for piece in range(ROUNDS):
            begin = pl.multiple_of(jnp.where(turn1 == piece, half, 0), half)
            copies.append(
                pltpu.make_async_copy(
                    ref.at[pl.ds(begin, half)],
                    outs[piece].at[pl.ds(which * half, half)],
                    sems.at[piece, which],
                )
            )
        copies.append(
            pltpu.make_async_copy(
                ref, outs[ROUNDS].at[pl.ds(which * 2 * half, 2 * half)], sems.at[ROUNDS, which]
            )
        )
        return copies

    copies = copies_of(0, first)
    if with_weights:
        rows, width = gate.shape
        cols = width // 2
        for piece, out in enumerate(outs):
            if piece < ROUNDS:
                part, top = jnp.where(turn1 == piece, 1, 0), 2 * half
            elif piece == ROUNDS:
                part, top = 1 - core, 4 * half
            else:
                part, top = core, 0
            begin = pl.multiple_of(part * cols, cols)
            for number, (which, start, size, row, col) in enumerate(weight_blocks(rows, cols)):
                copies.append(
                    pltpu.make_async_copy(
                        (gate, up, down)[which].at[pl.ds(start, size), pl.ds(begin, cols)],
                        out.at[pl.ds(top + row, size), pl.ds(col, cols)],
                        weight_sems.at[piece, number],
                    )
                )
    for copy in copies:
        copy.start()
    if with_weights:
        held[...] = second[...] * scale[...]
    late = copies_of(1, held if with_weights else second)
    for copy in late:
        copy.start()
    for copy in copies + late:
        copy.wait()


def fetch_rows(near, far, own, got, buffers, sems):
    half = buffers[0].shape[1] // 2
    place, core = position()
    mine = core == place - home_of(0)
    last = len(near)
    for block in range(last):
        for which in range(2):
            rows = pl.ds(which * half, half)
            for side, group in enumerate((near, far)):
                pltpu.make_async_copy(
                    group[block].at[rows],
                    buffers[which].at[block, pl.ds(side * half, half)],
                    sems.at[block, which * 2 + side],
                ).start()

    def local(source):
        for which in range(2):
            for side in range(2):
                pltpu.make_async_copy(
                    source.at[pl.ds((which * 2 + side) * half, half)],
                    buffers[which].at[last, pl.ds(side * half, half)],
                    sems.at[last, which * 2 + side],
                ).start()

    if own is None:
        return

    @pl.when(mine)
    def _():
        local(own)

    @pl.when(jnp.logical_not(mine))
    def _():
        local(got)


def wait_rows(buffers, block, sems):
    half = buffers[0].shape[1] // 2
    for part in range(4):
        view = buffers[part // 2].at[block, pl.ds((part % 2) * half, half)]
        pltpu.make_async_copy(view, view, sems.at[block, part]).wait()


def row_starts(cells, reps, rows):
    place, core = position()
    rep = lax.axis_index("rep")
    starts = {}
    for cell in range(cells):
        for shift in range(reps):
            owner_rep = lax.rem(rep - shift + reps, reps)
            for slot in range(CELL):
                spot = spot_of(place, core, slot)
                begin = ((cell * CELL + spot) * reps + owner_rep) * rows
                starts[cell, shift, slot] = pl.multiple_of(begin, rows)
    return starts


def silu_parts(pre):
    sigma = jax.nn.sigmoid(pre)
    rest = 1.0 - sigma
    return sigma, pre * sigma, sigma * (1.0 + pre * rest)


def store_split(ref, index, value):
    high, low = split(value)
    ref[(0,) + index] = high
    ref[(1,) + index] = low


def pair_of(ref, *index):
    return ref[(0,) + index], ref[(1,) + index]


def inner_kernel(cells, reps, *refs):
    pieces = reps if cells == 1 else 1
    parts, refs = refs[:pieces], refs[pieces:]
    near, far, (own, got), refs = refs[:3], refs[3:6], refs[6:8], refs[8:]
    weights, gates, ups, backs, turned, steps, *scratch = refs
    keys, targets, wide, acts, row_sems, weight_sems = scratch
    rows, cols = weights.shape[1] // (cells * reps * CELL), weights.shape[2]
    copies = []
    for (cell, shift, slot), begin in row_starts(cells, reps, rows).items():
        source = parts[shift].at[slot] if cells == 1 else parts[0].at[cell, shift, slot]
        for which, start, size, row, col in weight_blocks(rows, cols):
            copies.append(
                pltpu.make_async_copy(
                    source.at[pl.ds(row, size), pl.ds(col, cols)],
                    weights.at[which, pl.ds(pl.multiple_of(begin + start, size), size)],
                    weight_sems.at[len(copies)],
                )
            )
    for copy in copies:
        copy.start()
    fetch_rows(near, far, own, got, (keys, targets), row_sems)
    for copy in copies:
        copy.wait()
    for which in range(3):
        store_split(wide, (which,), weights[which])
    size = keys.shape[1]

    @pl.loop(0, CELL)
    def _(block):
        wait_rows((keys, targets), block, row_sems)
        where = pl.ds(pl.multiple_of(block * size, size), size)
        key, target = split(keys[block]), split(targets[block])
        gate_pre = dot3(key, pair_of(wide, 0), NN)
        up_pre = dot3(key, pair_of(wide, 1), NN)
        back = dot3(target, pair_of(wide, 2), NN)
        gates[where] = gate_pre
        ups[where] = up_pre
        backs[where] = back
        _, act, slope = silu_parts(gate_pre)
        store_split(acts, (0, where), back * up_pre * slope)
        store_split(acts, (1, where), back * act)
        store_split(acts, (2, where), act * up_pre)
        for part in range(2):
            turned[part, 0, :, where] = key[part].T
            turned[part, 1, :, where] = target[part].T

    for which in range(3):
        steps[which] = dot3(pair_of(turned, which // 2), pair_of(acts, which), NN)


def renew_kernel(weights, steps, high, low):
    for which in range(3):
        weight = weights[which]
        moved = weight - steps[which]
        old = jnp.mean(weight * weight, axis=0, keepdims=True) + EPSILON
        new = jnp.mean(moved * moved, axis=0, keepdims=True) + EPSILON
        high[which], low[which] = split(moved * (jnp.sqrt(old) / jnp.sqrt(new)))


def read_kernel(*refs):
    near, far, (own, got, high, low), refs = refs[:3], refs[3:6], refs[6:10], refs[10:]
    totals, near_out, far_out, scratch = refs[0], refs[1:4], refs[4], refs[5:]
    queries, cots, turned, acts, sent, row_sems, out_sems = scratch
    fetch_rows(near, far, own, got, (queries, cots), row_sems)
    size = queries.shape[1]
    half = size // 2

    def weight(which):
        return high[which], low[which]

    def outgoing(block):
        if block < ROUNDS:
            return [
                (sent.at[block, pl.ds(0, half)], near_out[block]),
                (sent.at[block, pl.ds(half, half)], far_out.at[pl.ds(block * half, half)]),
            ]
        return [(sent.at[block], far_out.at[pl.ds(ROUNDS * half, size)])]

    @pl.loop(0, CELL)
    def _(block):
        wait_rows((queries, cots), block, row_sems)
        where = pl.ds(pl.multiple_of(block * size, size), size)
        query, cot = split(queries[block]), split(cots[block])
        gate_pre = dot3(query, weight(0), NN)
        up_pre = dot3(query, weight(1), NN)
        back = dot3(cot, weight(2), NN)
        _, act, slope = silu_parts(gate_pre)
        gate_back = split(back * up_pre * slope)
        up_back = split(back * act)
        for part in range(2):
            acts[part, 0, where] = gate_back[part]
            acts[part, 1, where] = up_back[part]
            turned[part, 0, :, where] = query[part].T
            turned[part, 1, :, where] = cot[part].T
        store_split(acts, (2, where), act * up_pre)
        sent[block] = dot3(gate_back, weight(0), NT) + dot3(up_back, weight(1), NT)
        for number in range(CELL):

            @pl.when(block == number)
            def _():
                for side, (source, out) in enumerate(outgoing(number)):
                    pltpu.make_async_copy(source, out, out_sems.at[number, side]).start()

    for which in range(3):
        totals[which] = dot3(pair_of(turned, which // 2), pair_of(acts, which), NN)
    for block in range(CELL):
        for side, (source, out) in enumerate(outgoing(block)):
            pltpu.make_async_copy(source, out, out_sems.at[block, side]).wait()


def renew_back_kernel(cells, weights, steps, totals, cots, direct):
    scale = 1.0 / weights.shape[1]
    for which in range(3):
        weight, total = weights[which], totals[which]
        moved = weight - steps[which]
        old = jnp.mean(weight * weight, axis=0, keepdims=True) + EPSILON
        new = jnp.mean(moved * moved, axis=0, keepdims=True) + EPSILON
        ratio = jnp.sqrt(old) / jnp.sqrt(new)
        ratio_cot = jnp.sum(total * moved, axis=0, keepdims=True) * scale
        moved_cot = ratio * (total - moved * (ratio_cot / new))
        grad = moved_cot + weight * (ratio_cot * ratio / old)
        if cells > 1:
            grad = grad * jnp.where(lax.axis_index("tok") < CELL, 1.0, 0.0)
        direct[which] = grad
        store_split(cots, (which,), -moved_cot)


def write_grads(cells, reps, turned, direct, parts, pieces, grads, grad_sems):
    for which in range(3):
        total = direct[which]
        begin = 0
        for acts in parts:
            span = pl.ds(begin, acts.shape[2])
            begin += acts.shape[2]
            left = turned[0, which // 2, :, span], turned[1, which // 2, :, span]
            total = total + dot3(left, pair_of(acts, which), NN)
        grads[which] = total
    rows = pieces[0].shape[-2]
    copies = []
    place, core = position()
    rep = lax.axis_index("rep")
    for cell in range(cells):
        for shift in range(reps):
            owner_rep = lax.rem(rep + shift, reps)
            for slot in range(CELL):
                spot = spot_of(place, core, slot)
                begin = pl.multiple_of(((cell * CELL + spot) * reps + owner_rep) * rows, rows)
                copies.append(
                    pltpu.make_async_copy(
                        grads.at[:, pl.ds(begin, rows)],
                        pieces[shift].at[cell, slot],
                        grad_sems.at[len(copies)],
                    )
                )
    run_copies(copies)


def token_grad_kernel(cells, reps, first, last, *refs):
    rounds = min(last, ROUNDS) - first
    near, far, refs = refs[:rounds], refs[rounds : 2 * rounds], refs[2 * rounds :]
    own, got, final = None, None, last > ROUNDS
    if final:
        (own, got, turned, direct, before), refs = refs[:5], refs[5:]
    (weights, cots, gates, ups, backs), refs = refs[:5], refs[5:]
    near_out, far_out, refs = refs[:rounds], refs[rounds], refs[rounds + 1 :]
    if final:
        pieces, (acts, grads, grad_sems), refs = refs[:reps], refs[reps : reps + 3], refs[reps + 3 :]
    else:
        acts, refs = refs[0], refs[1:]
    keys, targets, wide, sent, row_sems, out_sems = refs
    fetch_rows(near, far, own, got, (keys, targets), row_sems)
    size = sent.shape[2]
    half = size // 2
    for which in range(3):
        store_split(wide, (which,), weights[which])

    def outgoing(number):
        if number < rounds:
            near = [
                (sent.at[which, number, pl.ds(0, half)], near_out[number].at[pl.ds(which * half, half)])
                for which in range(2)
            ]
            far = [
                (
                    sent.at[which, number, pl.ds(half, half)],
                    far_out.at[pl.ds(number * size + which * half, half)],
                )
                for which in range(2)
            ]
            return near + far
        return [
            (sent.at[which, number], far_out.at[pl.ds((rounds + which) * size, size)])
            for which in range(2)
        ]

    @pl.loop(0, last - first)
    def _(number):
        wait_rows((keys, targets), number, row_sems)
        where = pl.ds(pl.multiple_of((first + number) * size, size), size)
        here = pl.ds(pl.multiple_of(number * size, size), size)
        key, target = split(keys[number]), split(targets[number])
        gate_back_cot = dot3(key, pair_of(cots, 0), NN)
        up_back_cot = dot3(key, pair_of(cots, 1), NN)
        hidden_cot = dot3(target, pair_of(cots, 2), NN)
        gate_pre, up_pre, back = gates[where], ups[where], backs[where]
        sigma, act, slope = silu_parts(gate_pre)
        bend = sigma * (1.0 - sigma) * (2.0 + gate_pre * (1.0 - 2.0 * sigma))
        mixed = gate_back_cot * slope
        gate_cot = split(
            gate_back_cot * back * up_pre * bend
            + (up_back_cot * back + hidden_cot * up_pre) * slope
        )
        up_cot = split(mixed * back + hidden_cot * act)
        back_cot = split(mixed * up_pre + up_back_cot * act)
        for part in range(2):
            acts[part, 0, here] = gate_cot[part]
            acts[part, 1, here] = up_cot[part]
            acts[part, 2, here] = back_cot[part]
        sent[0, number] = (
            dot3(gate_cot, pair_of(wide, 0), NT)
            + dot3(up_cot, pair_of(wide, 1), NT)
            + dot3(split(back * up_pre * slope), pair_of(cots, 0), NT)
            + dot3(split(back * act), pair_of(cots, 1), NT)
        )
        sent[1, number] = dot3(back_cot, pair_of(wide, 2), NT) + dot3(
            split(act * up_pre), pair_of(cots, 2), NT
        )
        for each in range(last - first):

            @pl.when(number == each)
            def _():
                for side, (source, out) in enumerate(outgoing(each)):
                    pltpu.make_async_copy(source, out, out_sems.at[each, side]).start()

    if final:
        write_grads(cells, reps, turned, direct, (before, acts), pieces, grads, grad_sems)
    for each in range(last - first):
        for side, (source, out) in enumerate(outgoing(each)):
            pltpu.make_async_copy(source, out, out_sems.at[each, side]).wait()


def call(kernel, inputs, in_specs, outs, out_specs, scratch, flops=0):
    moved = sum(math.prod(value.shape) * value.dtype.itemsize for value in list(inputs) + list(outs))
    return pl.pallas_call(
        kernel,
        out_shape=outs,
        in_specs=in_specs,
        out_specs=out_specs,
        scratch_shapes=scratch,
        cost_estimate=pl.CostEstimate(flops=flops, bytes_accessed=moved, transcendentals=0),
        compiler_params=pltpu.CompilerParams(vmem_limit_bytes=26 << 20),
    )(*inputs)


def per_device(
    query_rows, key_rows, value_rows, step_logits, read_cotangent, fast_gate, fast_up, fast_down
):
    tokens_here, depth = key_rows.shape[2:]
    half = tokens_here // 2
    tok_size = lax.axis_size("tok")
    reps = lax.axis_size("rep")
    cells = tok_size // CELL
    assert tok_size % CELL == 0 and lax.axis_size("head") == 2
    factor = 1.0 / (8.0 * math.sqrt(tokens_here * tok_size))
    pairs = routes(cells)
    place, core = position()
    turn0, turn1 = halves_sent(place, core)
    at_home = place == home_of(0) + core
    cell_groups = [[cell * CELL + spot for cell in range(cells)] for spot in range(CELL)]
    rows, width = fast_gate.shape[1:]
    cols = width // 2
    shape = jax.ShapeDtypeStruct
    dma = pltpu.SemaphoreType.DMA

    def shifted(shift, sign):
        return [(rep, (rep + sign * shift) % reps) for rep in range(reps)]

    step = jax.nn.softplus(step_logits[0, 0]) * factor

    weight_count = weight_rows(rows)

    def gather(first, second, *rest):
        extra = weight_count if rest else 0
        outs = [shape((2 * half + extra, depth), F32)] * ROUNDS
        outs.append(shape((4 * half + extra, depth), F32))
        scratch = [dma((CELL, 2))]
        if rest:
            outs.append(shape((extra, depth), F32))
            scratch = [pltpu.VMEM((2 * half, depth), F32)] + scratch + [dma((CELL + 1, 4))]
        inputs = [first, second, *rest]
        packed = call(
            functools.partial(pack_kernel, half, bool(rest)),
            inputs,
            [VMEM] * len(inputs),
            outs,
            [HBM] * len(outs),
            scratch,
        )
        near = [lax.ppermute(packed[turn], PLACE, pairs[turn]) for turn in range(ROUNDS)]
        return near, *packed[ROUNDS:]

    def spread(near, local):
        far = [lax.ppermute(piece, "head", SWAP) for piece in near]
        return near + far + [local, lax.ppermute(local, "head", SWAP)]

    def combine(near, far):
        across = lax.ppermute(far, "head", SWAP)
        length = near[0].shape[0]
        found = [
            part + across[number * length : (number + 1) * length]
            for number, part in enumerate(near)
        ]
        return found, far[len(near) * length :] + across[len(near) * length :]

    def hand_back(totals, first):
        return [
            lax.ppermute(total, PLACE, flipped(pairs[first + number]))
            for number, total in enumerate(totals)
        ]

    def settle(back, local):
        def choose(turn):
            return jnp.where(turn == 0, back[0], jnp.where(turn == 1, back[1], back[2]))

        low, high = choose(turn0), choose(turn1)
        found = []
        for which in range(low.shape[0] // half):
            span = slice(which * half, (which + 1) * half)
            remote = jnp.concatenate((low[span], high[span]))
            here = local[which * 2 * half : (which + 1) * 2 * half]
            found.append(jnp.where(at_home, here, remote))
        return found

    inner_near, inner_local, kept = gather(
        key_rows[0, 0],
        value_rows[0, 0],
        -step[:, None],
        fast_gate[0],
        fast_up[0],
        fast_down[0],
    )
    inner_near = list(lax.optimization_barrier(tuple(inner_near)))
    inner_rows = spread(inner_near, inner_local)
    inner_rows[-1], queries = lax.optimization_barrier((inner_rows[-1], query_rows[0, 0]))
    read_near, read_local = gather(queries, read_cotangent[0, 0])
    slots = [piece[2 * half :] for piece in inner_near]
    slots.append(jnp.where(core == place - home_of(0), kept, inner_rows[-1][4 * half :]))
    together = jnp.stack(slots)
    parts = [together]
    for shift in range(1, reps):
        parts.append(lax.ppermute(together, "rep", shifted(shift, 1)))
    if cells > 1:
        parts = [lax.all_gather(jnp.stack(parts), "tok", axis_index_groups=cell_groups)]

    size = 2 * half
    count = CELL * size
    square = shape((3, width, cols), F32)
    tall = shape((count, cols), F32)
    product = 6 * count * width * cols
    buffers = [pltpu.VMEM((CELL, size, depth), F32)] * 2
    turned = pltpu.VMEM((2, 2, depth, count), BF16)
    acts = pltpu.VMEM((2, 3, count, cols), BF16)
    split_square = pltpu.VMEM((2, 3, width, cols), BF16)
    weights, gates, ups, backs, key_turned, steps = call(
        functools.partial(inner_kernel, cells, reps),
        parts + inner_rows,
        [HBM] * (len(parts) + 8),
        [square, tall, tall, tall, shape((2, 2, depth, count), BF16), square],
        [VMEM] * 6,
        buffers + [split_square, acts, dma((CELL, 4)), dma((cells * reps * CELL * 4,))],
        6 * product,
    )
    if cells > 1:
        steps = lax.psum(steps, "tok", axis_index_groups=cell_groups)
    narrow = shape((3, width, cols), BF16)
    high, low = call(
        renew_kernel, (weights, steps), [VMEM] * 2, [narrow, narrow], [VMEM] * 2, []
    )
    *read_near, read_local, high = lax.optimization_barrier((*read_near, read_local, high))
    read_rows = spread(list(read_near), read_local)
    piece = shape((half, depth), F32)
    read = call(
        read_kernel,
        read_rows + [high, low],
        [HBM] * 8 + [VMEM] * 2,
        [square] + [piece] * ROUNDS + [shape((ROUNDS * half + size, depth), F32)],
        [VMEM] + [HBM] * (ROUNDS + 1),
        buffers
        + [turned, acts, pltpu.VMEM((CELL, size, depth), F32), dma((CELL, 4)), dma((CELL, 2))],
        8 * product,
    )
    totals = read[0]
    if cells > 1:
        totals = lax.psum(totals, "tok", axis_index_groups=cell_groups)
    cots, direct = call(
        functools.partial(renew_back_kernel, cells),
        [weights, steps, totals],
        [VMEM] * 3,
        [shape((2, 3, width, cols), BF16), square],
        [VMEM] * 2,
        [],
    )
    middle = 2

    def token_grads(first, last, cots, *more):
        rounds = min(last, ROUNDS) - first
        span = slice(first, first + rounds)
        inputs = inner_rows[:ROUNDS][span] + inner_rows[ROUNDS : 2 * ROUNDS][span]
        if more:
            inputs = inputs + inner_rows[2 * ROUNDS :]
        blocks = last - first
        specs = [HBM] * len(inputs) + [VMEM] * (len(more) + 5)
        outs = [shape((size, depth), F32)] * rounds
        outs.append(shape((size * (2 * blocks - rounds), depth), F32))
        acts = (2, 3, blocks * size, cols)
        if more:
            outs += [shape((cells, CELL, 3, rows, cols), F32)] * reps
            scratch = [
                pltpu.VMEM(acts, BF16),
                pltpu.VMEM((3, width, cols), F32),
                dma((cells * reps * CELL,)),
            ]
            out_specs = [HBM] * len(outs)
        else:
            out_specs = [HBM] * len(outs) + [VMEM]
            outs.append(shape(acts, BF16))
            scratch = []
        outs = call(
            functools.partial(token_grad_kernel, cells, reps, first, last),
            inputs + [*more, weights, cots, gates, ups, backs],
            specs,
            outs,
            out_specs,
            scratch
            + [pltpu.VMEM((blocks, size, depth), F32)] * 2
            + [
                split_square,
                pltpu.VMEM((2, blocks, size, depth), F32),
                dma((blocks, 4)),
                dma((blocks, 4)),
            ],
            9 * product * blocks // CELL + (3 * product if more else 0),
        )
        return outs[:rounds], outs[rounds], list(outs[rounds + 1 :])

    near_first, far_first, (acts_first,) = token_grads(0, middle, cots)
    query_totals, query_local = combine(read[1:4], read[4])
    cots, *query_totals = lax.optimization_barrier((cots, *query_totals))
    query_back = hand_back(query_totals, 0)
    near_last, far_last, given = token_grads(middle, CELL, cots, key_turned, direct, acts_first)
    far_last, *rest = lax.optimization_barrier((far_last, *near_first, *query_back))
    near_first, query_back = rest[:-ROUNDS], rest[-ROUNDS:]
    totals_first, _ = combine(near_first, far_first)
    back = hand_back(totals_first, 0)
    totals_last, local = combine(near_last, far_last)
    back += hand_back(totals_last, middle)
    given[0], *back = lax.optimization_barrier((given[0], *back))
    (query_grad,) = settle(query_back, query_local)
    key_grad, target_grad = settle(back, local)

    if cells > 1:
        given = [
            lax.psum_scatter(value, "tok", scatter_dimension=0, tiled=True, axis_index_groups=cell_groups)
            for value in given
        ]
    total = given[0][0]
    for shift in range(1, reps):
        total = total + lax.ppermute(given[shift][0], "rep", shifted(shift, 1))
    returned = [
        lax.ppermute(total[turn], PLACE, flipped(pairs[turn])) for turn in range(ROUNDS)
    ]
    home_piece = total[ROUNDS]
    home_other = lax.ppermute(home_piece, "head", SWAP)

    def choose(turn):
        return jnp.where(turn == 0, returned[0], jnp.where(turn == 1, returned[1], returned[2]))

    left = jnp.where(at_home, jnp.where(core == 0, home_piece, home_other), choose(turn0))
    right = jnp.where(at_home, jnp.where(core == 0, home_other, home_piece), choose(turn1))
    owned = jnp.concatenate((left, right), axis=2)

    value_grad = -step[:, None] * target_grad
    step_grad = -jnp.sum(value_rows[0, 0] * target_grad, axis=1)
    logit_grad = step_grad * factor * jax.nn.sigmoid(step_logits[0, 0])
    return (
        query_grad[None, None],
        key_grad[None, None],
        value_grad[None, None],
        logit_grad[None, None],
        owned[0][None],
        owned[1][None],
        owned[2][None],
    )


def solution(mesh):
    tokens = P(("groups", "rep"), "head", "tok", None)
    logits = P(("groups", "rep"), "head", "tok")
    weight = P("head", ("tok", "rep"), None)
    grad = P(("groups", "head"), ("tok", "rep"), None)
    return jax.shard_map(
        per_device,
        mesh=mesh,
        in_specs=(tokens, tokens, tokens, logits, tokens, weight, weight, weight),
        out_specs=(tokens, tokens, tokens, logits, grad, grad, grad),
        check_vma=False,
    )
```

```python
import functools
import math

import jax
import jax.numpy as jnp
from jax import lax
from jax.experimental import pallas as pl
from jax.experimental.pallas import tpu as pltpu
from jax.sharding import PartitionSpec as P

EPSILON = 1e-06
CELL = 4
ROUNDS = CELL - 1
PLACE = ("tok", "head")
SWAP = [(0, 1), (1, 0)]
F32 = jnp.float32
BF16 = jnp.bfloat16
NN = ((1,), (0,))
NT = ((1,), (1,))
GROUP = 2
HBM = pl.BlockSpec(memory_space=pltpu.MemorySpace.HBM)
VMEM = pl.BlockSpec(memory_space=pltpu.VMEM)


def home_of(head):
    return (CELL - 1) // 2 + head


def source_of(head, turn):
    return (home_of(head) + 1 + (turn + 2 * (1 - head)) % ROUNDS) % CELL


def routes(cells):
    rounds = []
    for turn in range(ROUNDS):
        pairs = []
        for cell in range(cells):
            here = []
            for head in range(2):
                for core in range(2):
                    origin = cell * CELL + source_of(head, turn + core)
                    home = cell * CELL + home_of(head)
                    here.append((origin * 2 + head, home * 2 + core))
            everyone = range(cell * CELL * 2, (cell + 1) * CELL * 2)
            idle = sorted(set(everyone) - {first for first, _ in here})
            free = sorted(set(everyone) - {second for _, second in here})
            pairs += here + list(zip(idle, free))
        rounds.append(pairs)
    return rounds


def flipped(pairs):
    return [(second, first) for first, second in pairs]


def split(value):
    high = value.astype(BF16)
    return high, (value - high.astype(F32)).astype(BF16)


def dot3(left, right, form):
    def one(first, second):
        return lax.dot_general(first, second, (form, ((), ())), preferred_element_type=F32)

    return one(left[0], right[0]) + (one(left[0], right[1]) + one(left[1], right[0]))


def position():
    place = lax.rem(lax.axis_index("tok"), CELL)
    core = lax.axis_index("head")
    return place, core


def spot_of(place, core, slot):
    if slot == ROUNDS:
        return place
    head = place - home_of(0)
    return lax.rem(place + 1 + lax.rem(slot + core + 2 * (1 - head) + ROUNDS, ROUNDS), CELL)


def halves_sent(place, core):
    ahead = lax.rem(place - home_of(0) - core - 1 + 2 * CELL, CELL)
    turn0 = lax.rem(ahead + 1 - core, ROUNDS)
    turn1 = lax.rem(turn0 + ROUNDS - 1, ROUNDS)
    return turn0, turn1


def run_copies(copies):
    for copy in copies:
        copy.start()
    for copy in copies:
        copy.wait()


def weight_rows(rows):
    return rows * 3 // 2 if rows % 16 == 0 else rows * 2


def weight_blocks(rows, cols):
    blocks = [(0, 0, rows, 0, 0), (1, 0, rows, 0, cols)]
    if rows % 16 == 0:
        return blocks + [(2, 0, rows // 2, rows, 0), (2, rows // 2, rows // 2, rows, cols)]
    return blocks + [(2, 0, rows, rows, 0)]


def pack_kernel(half, with_weights, *refs):
    if with_weights:
        *sources, scale = refs[:6]
        first, second, gate, up, down = refs[-9:-4]
        outs, (load_sems, held, sems, weight_sems) = refs[6:-9], refs[-4:]
        loads = [
            pltpu.make_async_copy(source, there, load_sems.at[number])
            for number, (source, there) in enumerate(zip(sources, (first, second, gate, up, down)))
        ]
        for load in loads:
            load.start()
        loads[0].wait()
    else:
        first, second, *outs, sems = refs
    place, core = position()
    _, turn1 = halves_sent(place, core)

    def copies_of(which, ref):
        copies = []
        for piece in range(ROUNDS):
            begin = pl.multiple_of(jnp.where(turn1 == piece, half, 0), half)
            copies.append(
                pltpu.make_async_copy(
                    ref.at[pl.ds(begin, half)],
                    outs[piece].at[pl.ds(which * half, half)],
                    sems.at[piece, which],
                )
            )
        copies.append(
            pltpu.make_async_copy(
                ref, outs[ROUNDS].at[pl.ds(which * 2 * half, 2 * half)], sems.at[ROUNDS, which]
            )
        )
        return copies

    copies = copies_of(0, first)
    for copy in copies:
        copy.start()
    if with_weights:
        loads[1].wait()
        held[...] = second[...] * scale[...]
    late = copies_of(1, held if with_weights else second)
    for copy in late:
        copy.start()
    if with_weights:
        for load in loads[2:]:
            load.wait()
        rows, width = gate.shape
        cols = width // 2
        for piece, out in enumerate(outs):
            if piece < ROUNDS:
                part, top = jnp.where(turn1 == piece, 1, 0), 2 * half
            elif piece == ROUNDS:
                part, top = 1 - core, 4 * half
            else:
                part, top = core, 0
            begin = pl.multiple_of(part * cols, cols)
            for number, (which, start, size, row, col) in enumerate(weight_blocks(rows, cols)):
                copies.append(
                    pltpu.make_async_copy(
                        (gate, up, down)[which].at[pl.ds(start, size), pl.ds(begin, cols)],
                        out.at[pl.ds(top + row, size), pl.ds(col, cols)],
                        weight_sems.at[piece, number],
                    )
                )
                copies[-1].start()
    for copy in copies + late:
        copy.wait()


def fetch_rows(near, far, own, got, buffers, sems):
    half = buffers[0].shape[1] // 2
    place, core = position()
    mine = core == place - home_of(0)
    last = len(near)
    for block in range(last):
        for which in range(2):
            rows = pl.ds(which * half, half)
            for side, group in enumerate((near, far)):
                pltpu.make_async_copy(
                    group[block].at[rows],
                    buffers[which].at[block, pl.ds(side * half, half)],
                    sems.at[block, which * 2 + side],
                ).start()

    def local(source):
        for which in range(2):
            for side in range(2):
                pltpu.make_async_copy(
                    source.at[pl.ds((which * 2 + side) * half, half)],
                    buffers[which].at[last, pl.ds(side * half, half)],
                    sems.at[last, which * 2 + side],
                ).start()

    if own is None:
        return

    @pl.when(mine)
    def _():
        local(own)

    @pl.when(jnp.logical_not(mine))
    def _():
        local(got)


def take_rows(buffers, group, sems):
    size, depth = buffers[0].shape[1:]
    half = size // 2
    for each in range(GROUP):
        block = group * GROUP + each
        for part in range(4):
            view = buffers[part // 2].at[block, pl.ds((part % 2) * half, half)]
            pltpu.make_async_copy(view, view, sems.at[block, part]).wait()
    first, second = (
        buffer[pl.ds(group * GROUP, GROUP)].reshape(GROUP * size, depth) for buffer in buffers
    )
    return split(first), split(second)


def row_starts(cells, reps, rows):
    place, core = position()
    rep = lax.axis_index("rep")
    starts = {}
    for cell in range(cells):
        for shift in range(reps):
            owner_rep = lax.rem(rep - shift + reps, reps)
            for slot in range(CELL):
                spot = spot_of(place, core, slot)
                begin = ((cell * CELL + spot) * reps + owner_rep) * rows
                starts[cell, shift, slot] = pl.multiple_of(begin, rows)
    return starts


def silu_parts(pre):
    sigma = jax.nn.sigmoid(pre)
    rest = 1.0 - sigma
    return sigma, pre * sigma, sigma * (1.0 + pre * rest)


def store_split(ref, index, value):
    high, low = split(value)
    ref[(0,) + index] = high
    ref[(1,) + index] = low


def pair_of(ref, *index):
    return ref[(0,) + index], ref[(1,) + index]


def inner_kernel(cells, reps, *refs):
    pieces = reps if cells == 1 else 1
    parts, refs = refs[:pieces], refs[pieces:]
    near, far, (own, got), refs = refs[:3], refs[3:6], refs[6:8], refs[8:]
    weights, gates, ups, backs, turned, steps, *scratch = refs
    keys, targets, wide, acts, row_sems, weight_sems = scratch
    rows, cols = weights.shape[1] // (cells * reps * CELL), weights.shape[2]
    copies = []
    for (cell, shift, slot), begin in row_starts(cells, reps, rows).items():
        source = parts[shift].at[slot] if cells == 1 else parts[0].at[cell, shift, slot]
        for which, start, size, row, col in weight_blocks(rows, cols):
            copies.append(
                pltpu.make_async_copy(
                    source.at[pl.ds(row, size), pl.ds(col, cols)],
                    weights.at[which, pl.ds(pl.multiple_of(begin + start, size), size)],
                    weight_sems.at[len(copies)],
                )
            )
    for copy in copies:
        copy.start()
    fetch_rows(near, far, own, got, (keys, targets), row_sems)
    for copy in copies:
        copy.wait()
    for which in range(3):
        store_split(wide, (which,), weights[which])
    size = keys.shape[1] * GROUP

    @pl.loop(0, CELL // GROUP)
    def _(group):
        key, target = take_rows((keys, targets), group, row_sems)
        where = pl.ds(pl.multiple_of(group * size, size), size)
        gate_pre = dot3(key, pair_of(wide, 0), NN)
        up_pre = dot3(key, pair_of(wide, 1), NN)
        back = dot3(target, pair_of(wide, 2), NN)
        gates[where] = gate_pre
        ups[where] = up_pre
        backs[where] = back
        _, act, slope = silu_parts(gate_pre)
        store_split(acts, (0, where), back * up_pre * slope)
        store_split(acts, (1, where), back * act)
        store_split(acts, (2, where), act * up_pre)
        for part in range(2):
            turned[part, 0, :, where] = key[part].T
            turned[part, 1, :, where] = target[part].T

    for which in range(3):
        steps[which] = dot3(pair_of(turned, which // 2), pair_of(acts, which), NN)


def renew_kernel(weights, steps, high, low):
    for which in range(3):
        weight = weights[which]
        moved = weight - steps[which]
        old = jnp.mean(weight * weight, axis=0, keepdims=True) + EPSILON
        new = jnp.mean(moved * moved, axis=0, keepdims=True) + EPSILON
        high[which], low[which] = split(moved * (jnp.sqrt(old) / jnp.sqrt(new)))


def read_kernel(*refs):
    near, far, (own, got, high, low), refs = refs[:3], refs[3:6], refs[6:10], refs[10:]
    totals, near_out, far_out, scratch = refs[0], refs[1:4], refs[4], refs[5:]
    queries, cots, turned, acts, sent, row_sems, out_sems = scratch
    fetch_rows(near, far, own, got, (queries, cots), row_sems)
    size = queries.shape[1]
    half = size // 2

    def weight(which):
        return high[which], low[which]

    def outgoing(block):
        if block < ROUNDS:
            return [
                (sent.at[block, pl.ds(0, half)], near_out[block]),
                (sent.at[block, pl.ds(half, half)], far_out.at[pl.ds(block * half, half)]),
            ]
        return [(sent.at[block], far_out.at[pl.ds(ROUNDS * half, size)])]

    @pl.loop(0, CELL // GROUP)
    def _(group):
        query, cot = take_rows((queries, cots), group, row_sems)
        where = pl.ds(pl.multiple_of(group * GROUP * size, GROUP * size), GROUP * size)
        gate_pre = dot3(query, weight(0), NN)
        up_pre = dot3(query, weight(1), NN)
        back = dot3(cot, weight(2), NN)
        _, act, slope = silu_parts(gate_pre)
        gate_back = split(back * up_pre * slope)
        up_back = split(back * act)
        for part in range(2):
            acts[part, 0, where] = gate_back[part]
            acts[part, 1, where] = up_back[part]
            turned[part, 0, :, where] = query[part].T
            turned[part, 1, :, where] = cot[part].T
        store_split(acts, (2, where), act * up_pre)
        result = dot3(gate_back, weight(0), NT) + dot3(up_back, weight(1), NT)
        sent[pl.ds(group * GROUP, GROUP)] = result.reshape(GROUP, size, result.shape[1])
        for number in range(CELL):

            @pl.when(group == number // GROUP)
            def _():
                for side, (source, out) in enumerate(outgoing(number)):
                    pltpu.make_async_copy(source, out, out_sems.at[number, side]).start()

    for which in range(3):
        totals[which] = dot3(pair_of(turned, which // 2), pair_of(acts, which), NN)
    for block in range(CELL):
        for side, (source, out) in enumerate(outgoing(block)):
            pltpu.make_async_copy(source, out, out_sems.at[block, side]).wait()


def renew_back_kernel(cells, weights, steps, totals, cots, direct):
    scale = 1.0 / weights.shape[1]
    for which in range(3):
        weight, total = weights[which], totals[which]
        moved = weight - steps[which]
        old = jnp.mean(weight * weight, axis=0, keepdims=True) + EPSILON
        new = jnp.mean(moved * moved, axis=0, keepdims=True) + EPSILON
        ratio = jnp.sqrt(old) / jnp.sqrt(new)
        ratio_cot = jnp.sum(total * moved, axis=0, keepdims=True) * scale
        moved_cot = ratio * (total - moved * (ratio_cot / new))
        grad = moved_cot + weight * (ratio_cot * ratio / old)
        if cells > 1:
            grad = grad * jnp.where(lax.axis_index("tok") < CELL, 1.0, 0.0)
        direct[which] = grad
        store_split(cots, (which,), -moved_cot)


def write_grads(cells, reps, turned, direct, parts, pieces, grads, grad_sems):
    for which in range(3):
        total = direct[which]
        begin = 0
        for acts in parts:
            span = pl.ds(begin, acts.shape[2])
            begin += acts.shape[2]
            left = turned[0, which // 2, :, span], turned[1, which // 2, :, span]
            total = total + dot3(left, pair_of(acts, which), NN)
        grads[which] = total
    rows = pieces[0].shape[-2]
    copies = []
    place, core = position()
    rep = lax.axis_index("rep")
    for cell in range(cells):
        for shift in range(reps):
            owner_rep = lax.rem(rep + shift, reps)
            for slot in range(CELL):
                spot = spot_of(place, core, slot)
                begin = pl.multiple_of(((cell * CELL + spot) * reps + owner_rep) * rows, rows)
                copies.append(
                    pltpu.make_async_copy(
                        grads.at[:, pl.ds(begin, rows)],
                        pieces[shift].at[cell, slot],
                        grad_sems.at[len(copies)],
                    )
                )
    run_copies(copies)


def token_grad_kernel(cells, reps, first, last, *refs):
    rounds = min(last, ROUNDS) - first
    near, far, refs = refs[:rounds], refs[rounds : 2 * rounds], refs[2 * rounds :]
    own, got, final = None, None, last > ROUNDS
    if final:
        (own, got, turned, direct, before), refs = refs[:5], refs[5:]
    (weights, cots, gates, ups, backs), refs = refs[:5], refs[5:]
    near_out, far_out, refs = refs[:rounds], refs[rounds], refs[rounds + 1 :]
    if final:
        pieces, (acts, grads, grad_sems), refs = refs[:reps], refs[reps : reps + 3], refs[reps + 3 :]
    else:
        acts, refs = refs[0], refs[1:]
    keys, targets, wide, sent, row_sems, out_sems = refs
    fetch_rows(near, far, own, got, (keys, targets), row_sems)
    size = sent.shape[2]
    half = size // 2
    for which in range(3):
        store_split(wide, (which,), weights[which])

    def outgoing(number):
        if number < rounds:
            near = [
                (sent.at[which, number, pl.ds(0, half)], near_out[number].at[pl.ds(which * half, half)])
                for which in range(2)
            ]
            far = [
                (
                    sent.at[which, number, pl.ds(half, half)],
                    far_out.at[pl.ds(number * size + which * half, half)],
                )
                for which in range(2)
            ]
            return near + far
        return [
            (sent.at[which, number], far_out.at[pl.ds((rounds + which) * size, size)])
            for which in range(2)
        ]

    @pl.loop(0, (last - first) // GROUP)
    def _(group):
        key, target = take_rows((keys, targets), group, row_sems)
        many = GROUP * size
        where = pl.ds(pl.multiple_of(first * size + group * many, many), many)
        here = pl.ds(pl.multiple_of(group * many, many), many)
        there = pl.ds(group * GROUP, GROUP)
        gate_back_cot = dot3(key, pair_of(cots, 0), NN)
        up_back_cot = dot3(key, pair_of(cots, 1), NN)
        hidden_cot = dot3(target, pair_of(cots, 2), NN)
        gate_pre, up_pre, back = gates[where], ups[where], backs[where]
        sigma, act, slope = silu_parts(gate_pre)
        bend = sigma * (1.0 - sigma) * (2.0 + gate_pre * (1.0 - 2.0 * sigma))
        mixed = gate_back_cot * slope
        gate_cot = split(
            gate_back_cot * back * up_pre * bend
            + (up_back_cot * back + hidden_cot * up_pre) * slope
        )
        up_cot = split(mixed * back + hidden_cot * act)
        back_cot = split(mixed * up_pre + up_back_cot * act)
        for part in range(2):
            acts[part, 0, here] = gate_cot[part]
            acts[part, 1, here] = up_cot[part]
            acts[part, 2, here] = back_cot[part]
        key_part = (
            dot3(gate_cot, pair_of(wide, 0), NT)
            + dot3(up_cot, pair_of(wide, 1), NT)
            + dot3(split(back * up_pre * slope), pair_of(cots, 0), NT)
            + dot3(split(back * act), pair_of(cots, 1), NT)
        )
        target_part = dot3(back_cot, pair_of(wide, 2), NT) + dot3(
            split(act * up_pre), pair_of(cots, 2), NT
        )
        sent[0, there] = key_part.reshape(GROUP, size, key_part.shape[1])
        sent[1, there] = target_part.reshape(GROUP, size, target_part.shape[1])
        for each in range(last - first):

            @pl.when(group == each // GROUP)
            def _():
                for side, (source, out) in enumerate(outgoing(each)):
                    pltpu.make_async_copy(source, out, out_sems.at[each, side]).start()

    if final:
        write_grads(cells, reps, turned, direct, (before, acts), pieces, grads, grad_sems)
    for each in range(last - first):
        for side, (source, out) in enumerate(outgoing(each)):
            pltpu.make_async_copy(source, out, out_sems.at[each, side]).wait()


def call(kernel, inputs, in_specs, outs, out_specs, scratch, flops=0, grant=26):
    moved = sum(math.prod(value.shape) * value.dtype.itemsize for value in list(inputs) + list(outs))
    return pl.pallas_call(
        kernel,
        out_shape=outs,
        in_specs=in_specs,
        out_specs=out_specs,
        scratch_shapes=scratch,
        cost_estimate=pl.CostEstimate(flops=flops, bytes_accessed=moved, transcendentals=0),
        compiler_params=pltpu.CompilerParams(vmem_limit_bytes=grant << 20),
    )(*inputs)


def per_device(
    query_rows, key_rows, value_rows, step_logits, read_cotangent, fast_gate, fast_up, fast_down
):
    tokens_here, depth = key_rows.shape[2:]
    half = tokens_here // 2
    tok_size = lax.axis_size("tok")
    reps = lax.axis_size("rep")
    cells = tok_size // CELL
    assert tok_size % CELL == 0 and lax.axis_size("head") == 2
    factor = 1.0 / (8.0 * math.sqrt(tokens_here * tok_size))
    pairs = routes(cells)
    place, core = position()
    turn0, turn1 = halves_sent(place, core)
    at_home = place == home_of(0) + core
    cell_groups = [[cell * CELL + spot for cell in range(cells)] for spot in range(CELL)]
    rows, width = fast_gate.shape[1:]
    cols = width // 2
    shape = jax.ShapeDtypeStruct
    dma = pltpu.SemaphoreType.DMA

    def shifted(shift, sign):
        return [(rep, (rep + sign * shift) % reps) for rep in range(reps)]

    step = jax.nn.softplus(step_logits[0, 0]) * factor

    weight_count = weight_rows(rows)

    def gather(first, second, *rest):
        extra = weight_count if rest else 0
        outs = [shape((2 * half + extra, depth), F32)] * ROUNDS
        outs.append(shape((4 * half + extra, depth), F32))
        scratch = [dma((CELL, 2))]
        if rest:
            outs.append(shape((extra, depth), F32))
            weights_held = [pltpu.VMEM((rows, width), F32)] * 3
            scratch = (
                [pltpu.VMEM((2 * half, depth), F32)] * 2
                + weights_held
                + [dma((5,)), pltpu.VMEM((2 * half, depth), F32)]
                + scratch
                + [dma((CELL + 1, 4))]
            )
        inputs = [first, second, *rest]
        packed = call(
            functools.partial(pack_kernel, half, bool(rest)),
            inputs,
            [HBM] * 5 + [VMEM] if rest else [VMEM] * 2,
            outs,
            [HBM] * len(outs),
            scratch,
            grant=60 if rest else 26,
        )
        near = [lax.ppermute(packed[turn], PLACE, pairs[turn]) for turn in range(ROUNDS)]
        return near, *packed[ROUNDS:]

    def spread(near, local):
        far = [lax.ppermute(piece, "head", SWAP) for piece in near]
        return near + far + [local, lax.ppermute(local, "head", SWAP)]

    def combine(near, far):
        across = lax.ppermute(far, "head", SWAP)
        length = near[0].shape[0]
        found = [
            part + across[number * length : (number + 1) * length]
            for number, part in enumerate(near)
        ]
        return found, far[len(near) * length :] + across[len(near) * length :]

    def hand_back(totals, first):
        return [
            lax.ppermute(total, PLACE, flipped(pairs[first + number]))
            for number, total in enumerate(totals)
        ]

    def settle(back, local):
        def choose(turn):
            return jnp.where(turn == 0, back[0], jnp.where(turn == 1, back[1], back[2]))

        low, high = choose(turn0), choose(turn1)
        found = []
        for which in range(low.shape[0] // half):
            span = slice(which * half, (which + 1) * half)
            remote = jnp.concatenate((low[span], high[span]))
            here = local[which * 2 * half : (which + 1) * 2 * half]
            found.append(jnp.where(at_home, here, remote))
        return found

    inner_near, inner_local, kept = gather(
        key_rows[0, 0],
        value_rows[0, 0],
        fast_gate[0],
        fast_up[0],
        fast_down[0],
        -step[:, None],
    )
    inner_near = list(lax.optimization_barrier(tuple(inner_near)))
    inner_rows = spread(inner_near, inner_local)
    inner_rows[-1], queries = lax.optimization_barrier((inner_rows[-1], query_rows[0, 0]))
    read_near, read_local = gather(queries, read_cotangent[0, 0])
    slots = [piece[2 * half :] for piece in inner_near]
    slots.append(jnp.where(core == place - home_of(0), kept, inner_rows[-1][4 * half :]))
    together = jnp.stack(slots)
    parts = [together]
    for shift in range(1, reps):
        parts.append(lax.ppermute(together, "rep", shifted(shift, 1)))
    if cells > 1:
        parts = [lax.all_gather(jnp.stack(parts), "tok", axis_index_groups=cell_groups)]

    size = 2 * half
    count = CELL * size
    square = shape((3, width, cols), F32)
    tall = shape((count, cols), F32)
    product = 6 * count * width * cols
    buffers = [pltpu.VMEM((CELL, size, depth), F32)] * 2
    turned = pltpu.VMEM((2, 2, depth, count), BF16)
    acts = pltpu.VMEM((2, 3, count, cols), BF16)
    split_square = pltpu.VMEM((2, 3, width, cols), BF16)
    weights, gates, ups, backs, key_turned, steps = call(
        functools.partial(inner_kernel, cells, reps),
        parts + inner_rows,
        [HBM] * (len(parts) + 8),
        [square, tall, tall, tall, shape((2, 2, depth, count), BF16), square],
        [VMEM] * 6,
        buffers + [split_square, acts, dma((CELL, 4)), dma((cells * reps * CELL * 4,))],
        6 * product,
    )
    if cells > 1:
        steps = lax.psum(steps, "tok", axis_index_groups=cell_groups)
    narrow = shape((3, width, cols), BF16)
    high, low = call(
        renew_kernel, (weights, steps), [VMEM] * 2, [narrow, narrow], [VMEM] * 2, []
    )
    *read_near, read_local, high = lax.optimization_barrier((*read_near, read_local, high))
    read_rows = spread(list(read_near), read_local)
    piece = shape((half, depth), F32)
    read = call(
        read_kernel,
        read_rows + [high, low],
        [HBM] * 8 + [VMEM] * 2,
        [square] + [piece] * ROUNDS + [shape((ROUNDS * half + size, depth), F32)],
        [VMEM] + [HBM] * (ROUNDS + 1),
        buffers
        + [turned, acts, pltpu.VMEM((CELL, size, depth), F32), dma((CELL, 4)), dma((CELL, 2))],
        8 * product,
    )
    totals = read[0]
    if cells > 1:
        totals = lax.psum(totals, "tok", axis_index_groups=cell_groups)
    cots, direct = call(
        functools.partial(renew_back_kernel, cells),
        [weights, steps, totals],
        [VMEM] * 3,
        [shape((2, 3, width, cols), BF16), square],
        [VMEM] * 2,
        [],
    )
    middle = 2

    def token_grads(first, last, cots, *more):
        rounds = min(last, ROUNDS) - first
        span = slice(first, first + rounds)
        inputs = inner_rows[:ROUNDS][span] + inner_rows[ROUNDS : 2 * ROUNDS][span]
        if more:
            inputs = inputs + inner_rows[2 * ROUNDS :]
        blocks = last - first
        specs = [HBM] * len(inputs) + [VMEM] * (len(more) + 5)
        outs = [shape((size, depth), F32)] * rounds
        outs.append(shape((size * (2 * blocks - rounds), depth), F32))
        acts = (2, 3, blocks * size, cols)
        if more:
            outs += [shape((cells, CELL, 3, rows, cols), F32)] * reps
            scratch = [
                pltpu.VMEM(acts, BF16),
                pltpu.VMEM((3, width, cols), F32),
                dma((cells * reps * CELL,)),
            ]
            out_specs = [HBM] * len(outs)
        else:
            out_specs = [HBM] * len(outs) + [VMEM]
            outs.append(shape(acts, BF16))
            scratch = []
        outs = call(
            functools.partial(token_grad_kernel, cells, reps, first, last),
            inputs + [*more, weights, cots, gates, ups, backs],
            specs,
            outs,
            out_specs,
            scratch
            + [pltpu.VMEM((blocks, size, depth), F32)] * 2
            + [
                split_square,
                pltpu.VMEM((2, blocks, size, depth), F32),
                dma((blocks, 4)),
                dma((blocks, 4)),
            ],
            9 * product * blocks // CELL + (3 * product if more else 0),
        )
        return outs[:rounds], outs[rounds], list(outs[rounds + 1 :])

    near_first, far_first, (acts_first,) = token_grads(0, middle, cots)
    query_totals, query_local = combine(read[1:4], read[4])
    cots, *query_totals = lax.optimization_barrier((cots, *query_totals))
    query_back = hand_back(query_totals, 0)
    near_last, far_last, given = token_grads(middle, CELL, cots, key_turned, direct, acts_first)
    far_last, *rest = lax.optimization_barrier((far_last, *near_first, *query_back))
    near_first, query_back = rest[:-ROUNDS], rest[-ROUNDS:]
    totals_first, _ = combine(near_first, far_first)
    back = hand_back(totals_first, 0)
    totals_last, local = combine(near_last, far_last)
    back += hand_back(totals_last, middle)
    given[0], *back = lax.optimization_barrier((given[0], *back))
    (query_grad,) = settle(query_back, query_local)
    key_grad, target_grad = settle(back, local)

    if cells > 1:
        given = [
            lax.psum_scatter(value, "tok", scatter_dimension=0, tiled=True, axis_index_groups=cell_groups)
            for value in given
        ]
    total = given[0][0]
    for shift in range(1, reps):
        total = total + lax.ppermute(given[shift][0], "rep", shifted(shift, 1))
    returned = [
        lax.ppermute(total[turn], PLACE, flipped(pairs[turn])) for turn in range(ROUNDS)
    ]
    home_piece = total[ROUNDS]
    home_other = lax.ppermute(home_piece, "head", SWAP)

    def choose(turn):
        return jnp.where(turn == 0, returned[0], jnp.where(turn == 1, returned[1], returned[2]))

    left = jnp.where(at_home, jnp.where(core == 0, home_piece, home_other), choose(turn0))
    right = jnp.where(at_home, jnp.where(core == 0, home_other, home_piece), choose(turn1))
    owned = jnp.concatenate((left, right), axis=2)

    value_grad = -step[:, None] * target_grad
    step_grad = -jnp.sum(value_rows[0, 0] * target_grad, axis=1)
    logit_grad = step_grad * factor * jax.nn.sigmoid(step_logits[0, 0])
    return (
        query_grad[None, None],
        key_grad[None, None],
        value_grad[None, None],
        logit_grad[None, None],
        owned[0][None],
        owned[1][None],
        owned[2][None],
    )


def solution(mesh):
    tokens = P(("groups", "rep"), "head", "tok", None)
    logits = P(("groups", "rep"), "head", "tok")
    weight = P("head", ("tok", "rep"), None)
    grad = P(("groups", "head"), ("tok", "rep"), None)
    return jax.shard_map(
        per_device,
        mesh=mesh,
        in_specs=(tokens, tokens, tokens, logits, tokens, weight, weight, weight),
        out_specs=(tokens, tokens, tokens, logits, grad, grad, grad),
        check_vma=False,
    )
```

```python
import functools
import math

import jax
import jax.numpy as jnp
from jax import lax
from jax.experimental import pallas as pl
from jax.experimental.pallas import tpu as pltpu
from jax.sharding import PartitionSpec as P

EPSILON = 1e-06
CELL = 4
ROUNDS = CELL - 1
PLACE = ("tok", "head")
SWAP = [(0, 1), (1, 0)]
F32 = jnp.float32
BF16 = jnp.bfloat16
NN = ((1,), (0,))
NT = ((1,), (1,))
HBM = pl.BlockSpec(memory_space=pltpu.MemorySpace.HBM)
VMEM = pl.BlockSpec(memory_space=pltpu.VMEM)


def home_of(head):
    return (CELL - 1) // 2 + head


def source_of(head, turn):
    return (home_of(head) + 1 + (turn + 2 * (1 - head)) % ROUNDS) % CELL


def routes(cells):
    rounds = []
    for turn in range(ROUNDS):
        pairs = []
        for cell in range(cells):
            here = []
            for head in range(2):
                for core in range(2):
                    origin = cell * CELL + source_of(head, turn + core)
                    home = cell * CELL + home_of(head)
                    here.append((origin * 2 + head, home * 2 + core))
            everyone = range(cell * CELL * 2, (cell + 1) * CELL * 2)
            idle = sorted(set(everyone) - {first for first, _ in here})
            free = sorted(set(everyone) - {second for _, second in here})
            pairs += here + list(zip(idle, free))
        rounds.append(pairs)
    return rounds


def flipped(pairs):
    return [(second, first) for first, second in pairs]


def split(value):
    high = value.astype(BF16)
    return high, (value - high.astype(F32)).astype(BF16)


def dot3(left, right, form):
    def one(first, second):
        return lax.dot_general(first, second, (form, ((), ())), preferred_element_type=F32)

    return one(left[0], right[0]) + (one(left[0], right[1]) + one(left[1], right[0]))


def position():
    place = lax.rem(lax.axis_index("tok"), CELL)
    core = lax.axis_index("head")
    return place, core


def spot_of(place, core, slot):
    if slot == ROUNDS:
        return place
    head = place - home_of(0)
    return lax.rem(place + 1 + lax.rem(slot + core + 2 * (1 - head) + ROUNDS, ROUNDS), CELL)


def halves_sent(place, core):
    ahead = lax.rem(place - home_of(0) - core - 1 + 2 * CELL, CELL)
    turn0 = lax.rem(ahead + 1 - core, ROUNDS)
    turn1 = lax.rem(turn0 + ROUNDS - 1, ROUNDS)
    return turn0, turn1


def run_copies(copies):
    for copy in copies:
        copy.start()
    for copy in copies:
        copy.wait()


def weight_rows(rows):
    return rows * 3 // 2 if rows % 16 == 0 else rows * 2


def weight_blocks(rows, cols):
    blocks = [(0, 0, rows, 0, 0), (1, 0, rows, 0, cols)]
    if rows % 16 == 0:
        return blocks + [(2, 0, rows // 2, rows, 0), (2, rows // 2, rows // 2, rows, cols)]
    return blocks + [(2, 0, rows, rows, 0)]


def pack_kernel(half, with_weights, *refs):
    if with_weights:
        *sources, scale = refs[:6]
        first, second, gate, up, down = refs[-9:-4]
        outs, (load_sems, held, sems, weight_sems) = refs[6:-9], refs[-4:]
        loads = [
            pltpu.make_async_copy(source, there, load_sems.at[number])
            for number, (source, there) in enumerate(zip(sources, (first, second, gate, up, down)))
        ]
        for load in loads:
            load.start()
        loads[0].wait()
    else:
        first, second, *outs, sems = refs
    place, core = position()
    _, turn1 = halves_sent(place, core)

    def copies_of(which, ref):
        copies = []
        for piece in range(ROUNDS):
            begin = pl.multiple_of(jnp.where(turn1 == piece, half, 0), half)
            copies.append(
                pltpu.make_async_copy(
                    ref.at[pl.ds(begin, half)],
                    outs[piece].at[pl.ds(which * half, half)],
                    sems.at[piece, which],
                )
            )
        copies.append(
            pltpu.make_async_copy(
                ref, outs[ROUNDS].at[pl.ds(which * 2 * half, 2 * half)], sems.at[ROUNDS, which]
            )
        )
        return copies

    copies = copies_of(0, first)
    for copy in copies:
        copy.start()
    if with_weights:
        loads[1].wait()
        held[...] = second[...] * scale[...]
    late = copies_of(1, held if with_weights else second)
    for copy in late:
        copy.start()
    if with_weights:
        for load in loads[2:]:
            load.wait()
        rows, width = gate.shape
        cols = width // 2
        for piece, out in enumerate(outs):
            if piece < ROUNDS:
                part, top = jnp.where(turn1 == piece, 1, 0), 2 * half
            elif piece == ROUNDS:
                part, top = 1 - core, 4 * half
            else:
                part, top = core, 0
            begin = pl.multiple_of(part * cols, cols)
            for number, (which, start, size, row, col) in enumerate(weight_blocks(rows, cols)):
                copies.append(
                    pltpu.make_async_copy(
                        (gate, up, down)[which].at[pl.ds(start, size), pl.ds(begin, cols)],
                        out.at[pl.ds(top + row, size), pl.ds(col, cols)],
                        weight_sems.at[piece, number],
                    )
                )
                copies[-1].start()
    for copy in copies + late:
        copy.wait()


def fetch_rows(rounds, own, got, side, buffers, sems):
    half = buffers[0].shape[0] // CELL
    place, core = position()
    mine = core == place - home_of(0)
    for which in range(2):
        for turn, piece in enumerate(rounds):
            pltpu.make_async_copy(
                piece.at[pl.ds(which * half, half)],
                buffers[which].at[pl.ds(turn * half, half)],
                sems.at[which, turn],
            ).start()

    def local(source):
        for which in range(2):
            pltpu.make_async_copy(
                source.at[pl.ds((which * 2 + side) * half, half)],
                buffers[which].at[pl.ds(ROUNDS * half, half)],
                sems.at[which, ROUNDS],
            ).start()

    @pl.when(mine)
    def _():
        local(own)

    @pl.when(jnp.logical_not(mine))
    def _():
        local(got)


def take_rows(buffers, sems):
    half = buffers[0].shape[0] // CELL
    for which in range(2):
        for chunk in range(CELL):
            view = buffers[which].at[pl.ds(chunk * half, half)]
            pltpu.make_async_copy(view, view, sems.at[which, chunk]).wait()
    return split(buffers[0][...]), split(buffers[1][...])


def row_starts(cells, reps, rows):
    place, core = position()
    rep = lax.axis_index("rep")
    starts = {}
    for cell in range(cells):
        for shift in range(reps):
            owner_rep = lax.rem(rep - shift + reps, reps)
            for slot in range(CELL):
                spot = spot_of(place, core, slot)
                begin = ((cell * CELL + spot) * reps + owner_rep) * rows
                starts[cell, shift, slot] = pl.multiple_of(begin, rows)
    return starts


def silu_parts(pre):
    sigma = jax.nn.sigmoid(pre)
    rest = 1.0 - sigma
    return sigma, pre * sigma, sigma * (1.0 + pre * rest)


def store_split(ref, index, value):
    high, low = split(value)
    ref[(0,) + index] = high
    ref[(1,) + index] = low


def pair_of(ref, *index):
    return ref[(0,) + index], ref[(1,) + index]


def inner_kernel(cells, reps, *refs):
    pieces = reps if cells == 1 else 1
    parts, refs = refs[:pieces], refs[pieces:]
    near, far, (own, got), refs = refs[:3], refs[3:6], refs[6:8], refs[8:]
    weights, gates, ups, backs, turned, steps, *scratch = refs
    keys, targets, wide, acts, row_sems, weight_sems = scratch
    rows, cols = weights.shape[1] // (cells * reps * CELL), weights.shape[2]
    copies = []
    for (cell, shift, slot), begin in row_starts(cells, reps, rows).items():
        source = parts[shift].at[slot] if cells == 1 else parts[0].at[cell, shift, slot]
        for which, start, size, row, col in weight_blocks(rows, cols):
            copies.append(
                pltpu.make_async_copy(
                    source.at[pl.ds(row, size), pl.ds(col, cols)],
                    weights.at[which, pl.ds(pl.multiple_of(begin + start, size), size)],
                    weight_sems.at[len(copies)],
                )
            )
    for copy in copies:
        copy.start()
    for side, rounds in enumerate((near, far)):
        buffers = keys.at[side], targets.at[side]
        fetch_rows(rounds, own, got, side, buffers, row_sems.at[side])
    for copy in copies:
        copy.wait()
    for which in range(3):
        store_split(wide, (which,), weights[which])
    size = keys.shape[1]

    @pl.loop(0, 2)
    def _(side):
        key, target = take_rows((keys.at[side], targets.at[side]), row_sems.at[side])
        where = pl.ds(pl.multiple_of(side * size, size), size)
        gate_pre = dot3(key, pair_of(wide, 0), NN)
        up_pre = dot3(key, pair_of(wide, 1), NN)
        back = dot3(target, pair_of(wide, 2), NN)
        gates[where] = gate_pre
        ups[where] = up_pre
        backs[where] = back
        _, act, slope = silu_parts(gate_pre)
        store_split(acts, (0, where), back * up_pre * slope)
        store_split(acts, (1, where), back * act)
        store_split(acts, (2, where), act * up_pre)
        for part in range(2):
            turned[part, 0, :, where] = key[part].T
            turned[part, 1, :, where] = target[part].T

    for which in range(3):
        steps[which] = dot3(pair_of(turned, which // 2), pair_of(acts, which), NN)


def renew_kernel(weights, steps, high, low):
    for which in range(3):
        weight = weights[which]
        moved = weight - steps[which]
        old = jnp.mean(weight * weight, axis=0, keepdims=True) + EPSILON
        new = jnp.mean(moved * moved, axis=0, keepdims=True) + EPSILON
        high[which], low[which] = split(moved * (jnp.sqrt(old) / jnp.sqrt(new)))


def read_kernel(side, *refs):
    rounds, (own, got, high, low), refs = refs[:3], refs[3:7], refs[7:]
    before, refs = (refs[:2], refs[2:]) if side else ((), refs)
    main, refs = (refs[0], refs[1:]) if side else (None, refs)
    round_out, rest_out = (refs[:3], refs[3]) if side == 0 else (None, refs[0])
    refs = refs[4:] if side == 0 else refs[1:]
    turned, acts, queries, cots, sent, row_sems, out_sems = refs
    half = queries.shape[0] // CELL
    fetch_rows(rounds, own, got, side, (queries, cots), row_sems)

    def weight(which):
        return high[which], low[which]

    query, cot = take_rows((queries, cots), row_sems)
    gate_pre = dot3(query, weight(0), NN)
    up_pre = dot3(query, weight(1), NN)
    back = dot3(cot, weight(2), NN)
    _, act, slope = silu_parts(gate_pre)
    gate_back = split(back * up_pre * slope)
    up_back = split(back * act)
    sent[...] = dot3(gate_back, weight(0), NT) + dot3(up_back, weight(1), NT)
    if side == 0:
        copies = [
            pltpu.make_async_copy(sent.at[pl.ds(turn * half, half)], out, out_sems.at[turn])
            for turn, out in enumerate(round_out)
        ]
        copies.append(
            pltpu.make_async_copy(
                sent.at[pl.ds(ROUNDS * half, half)], rest_out, out_sems.at[ROUNDS]
            )
        )
    else:
        copies = [pltpu.make_async_copy(sent, rest_out, out_sems.at[0])]
    for copy in copies:
        copy.start()
    for part in range(2):
        acts[part, 0] = gate_back[part]
        acts[part, 1] = up_back[part]
        turned[part, 0] = query[part].T
        turned[part, 1] = cot[part].T
    store_split(acts, (2,), act * up_pre)
    if side:
        for which in range(3):
            main[which] = dot3(
                pair_of(before[0], which // 2), pair_of(before[1], which), NN
            ) + dot3(pair_of(turned, which // 2), pair_of(acts, which), NN)
    for copy in copies:
        copy.wait()


def renew_back_kernel(cells, weights, steps, totals, cots, direct):
    scale = 1.0 / weights.shape[1]
    for which in range(3):
        weight, total = weights[which], totals[which]
        moved = weight - steps[which]
        old = jnp.mean(weight * weight, axis=0, keepdims=True) + EPSILON
        new = jnp.mean(moved * moved, axis=0, keepdims=True) + EPSILON
        ratio = jnp.sqrt(old) / jnp.sqrt(new)
        ratio_cot = jnp.sum(total * moved, axis=0, keepdims=True) * scale
        moved_cot = ratio * (total - moved * (ratio_cot / new))
        grad = moved_cot + weight * (ratio_cot * ratio / old)
        if cells > 1:
            grad = grad * jnp.where(lax.axis_index("tok") < CELL, 1.0, 0.0)
        direct[which] = grad
        store_split(cots, (which,), -moved_cot)


def weight_grad_kernel(cells, reps, *refs):
    near, far, (own, got, turned, direct), refs = refs[:3], refs[3:6], refs[6:10], refs[10:]
    (cots, gates, ups, backs), refs = refs[:4], refs[4:]
    acts, pieces, refs = refs[0], refs[1 : 1 + reps], refs[1 + reps :]
    keys, targets, grads, row_sems, grad_sems = refs
    for side, rounds in enumerate((near, far)):
        buffers = keys.at[side], targets.at[side]
        fetch_rows(rounds, own, got, side, buffers, row_sems.at[side])
    size = keys.shape[1]

    @pl.loop(0, 2)
    def _(side):
        key, target = take_rows((keys.at[side], targets.at[side]), row_sems.at[side])
        where = pl.ds(pl.multiple_of(side * size, size), size)
        gate_back_cot = dot3(key, pair_of(cots, 0), NN)
        up_back_cot = dot3(key, pair_of(cots, 1), NN)
        hidden_cot = dot3(target, pair_of(cots, 2), NN)
        gate_pre, up_pre, back = gates[where], ups[where], backs[where]
        sigma, act, slope = silu_parts(gate_pre)
        bend = sigma * (1.0 - sigma) * (2.0 + gate_pre * (1.0 - 2.0 * sigma))
        mixed = gate_back_cot * slope
        store_split(
            acts,
            (0, where),
            gate_back_cot * back * up_pre * bend
            + (up_back_cot * back + hidden_cot * up_pre) * slope,
        )
        store_split(acts, (1, where), mixed * back + hidden_cot * act)
        store_split(acts, (2, where), mixed * up_pre + up_back_cot * act)

    for which in range(3):
        grads[which] = direct[which] + dot3(pair_of(turned, which // 2), pair_of(acts, which), NN)
    rows = pieces[0].shape[-2]
    copies = []
    place, core = position()
    rep = lax.axis_index("rep")
    for cell in range(cells):
        for shift in range(reps):
            owner_rep = lax.rem(rep + shift, reps)
            for slot in range(CELL):
                spot = spot_of(place, core, slot)
                begin = pl.multiple_of(((cell * CELL + spot) * reps + owner_rep) * rows, rows)
                copies.append(
                    pltpu.make_async_copy(
                        grads.at[:, pl.ds(begin, rows)],
                        pieces[shift].at[cell, slot],
                        grad_sems.at[len(copies)],
                    )
                )
    run_copies(copies)


def token_grad_kernel(side, *refs):
    (weights, cots, acts, gates, ups, backs), refs = refs[:6], refs[6:]
    outs, (wide, sent, out_sems) = refs[:-3], refs[-3:]
    size = sent.shape[1]
    half = size // CELL
    for which in range(3):
        store_split(wide, (which,), weights[which])
    where = pl.ds(side * size, size)
    gate_pre, up_pre, back = gates[where], ups[where], backs[where]
    _, act, slope = silu_parts(gate_pre)
    sent[1] = dot3(pair_of(acts, 2, where), pair_of(wide, 2), NT) + dot3(
        split(act * up_pre), pair_of(cots, 2), NT
    )

    def copies_of(which):
        copies = []
        for chunk in range(CELL):
            out = outs[chunk] if side == 0 else outs[0].at[pl.ds(chunk * 2 * half, 2 * half)]
            copies.append(
                pltpu.make_async_copy(
                    sent.at[which, pl.ds(chunk * half, half)],
                    out.at[pl.ds(which * half, half)],
                    out_sems.at[which, chunk],
                )
            )
        return copies

    late = copies_of(1)
    for copy in late:
        copy.start()
    sent[0] = (
        dot3(pair_of(acts, 0, where), pair_of(wide, 0), NT)
        + dot3(pair_of(acts, 1, where), pair_of(wide, 1), NT)
        + dot3(split(back * up_pre * slope), pair_of(cots, 0), NT)
        + dot3(split(back * act), pair_of(cots, 1), NT)
    )
    early = copies_of(0)
    for copy in early:
        copy.start()
    for copy in late + early:
        copy.wait()


def call(kernel, inputs, in_specs, outs, out_specs, scratch, flops=0, grant=26):
    moved = sum(math.prod(value.shape) * value.dtype.itemsize for value in list(inputs) + list(outs))
    return pl.pallas_call(
        kernel,
        out_shape=outs,
        in_specs=in_specs,
        out_specs=out_specs,
        scratch_shapes=scratch,
        cost_estimate=pl.CostEstimate(flops=flops, bytes_accessed=moved, transcendentals=0),
        compiler_params=pltpu.CompilerParams(vmem_limit_bytes=grant << 20),
    )(*inputs)


def per_device(
    query_rows, key_rows, value_rows, step_logits, read_cotangent, fast_gate, fast_up, fast_down
):
    tokens_here, depth = key_rows.shape[2:]
    half = tokens_here // 2
    tok_size = lax.axis_size("tok")
    reps = lax.axis_size("rep")
    cells = tok_size // CELL
    assert tok_size % CELL == 0 and lax.axis_size("head") == 2
    factor = 1.0 / (8.0 * math.sqrt(tokens_here * tok_size))
    pairs = routes(cells)
    place, core = position()
    turn0, turn1 = halves_sent(place, core)
    at_home = place == home_of(0) + core
    cell_groups = [[cell * CELL + spot for cell in range(cells)] for spot in range(CELL)]
    rows, width = fast_gate.shape[1:]
    cols = width // 2
    shape = jax.ShapeDtypeStruct
    dma = pltpu.SemaphoreType.DMA

    def shifted(shift, sign):
        return [(rep, (rep + sign * shift) % reps) for rep in range(reps)]

    step = jax.nn.softplus(step_logits[0, 0]) * factor

    weight_count = weight_rows(rows)

    def gather(first, second, *rest):
        extra = weight_count if rest else 0
        outs = [shape((2 * half + extra, depth), F32)] * ROUNDS
        outs.append(shape((4 * half + extra, depth), F32))
        scratch = [dma((CELL, 2))]
        if rest:
            outs.append(shape((extra, depth), F32))
            weights_held = [pltpu.VMEM((rows, width), F32)] * 3
            scratch = (
                [pltpu.VMEM((2 * half, depth), F32)] * 2
                + weights_held
                + [dma((5,)), pltpu.VMEM((2 * half, depth), F32)]
                + scratch
                + [dma((CELL + 1, 4))]
            )
        inputs = [first, second, *rest]
        packed = call(
            functools.partial(pack_kernel, half, bool(rest)),
            inputs,
            [HBM] * 5 + [VMEM] if rest else [VMEM] * 2,
            outs,
            [HBM] * len(outs),
            scratch,
            grant=60 if rest else 26,
        )
        near = [lax.ppermute(packed[turn], PLACE, pairs[turn]) for turn in range(ROUNDS)]
        return near, *packed[ROUNDS:]

    def spread(near, local):
        far = [lax.ppermute(piece, "head", SWAP) for piece in near]
        return near + far + [local, lax.ppermute(local, "head", SWAP)]

    def hand_back(near, far):
        length = near[0].shape[0]
        totals = [
            part + far[turn * length : (turn + 1) * length]
            for turn, part in enumerate(near[:ROUNDS])
        ]
        return [lax.ppermute(totals[turn], PLACE, flipped(pairs[turn])) for turn in range(ROUNDS)]

    def settle(back, first, second):
        def choose(turn):
            return jnp.where(turn == 0, back[0], jnp.where(turn == 1, back[1], back[2]))

        low = jnp.where(at_home, first, choose(turn0))
        high = jnp.where(at_home, second, choose(turn1))
        return [
            jnp.concatenate((low[at : at + half], high[at : at + half]))
            for at in range(0, low.shape[0], half)
        ]

    inner_near, inner_local, kept = gather(
        key_rows[0, 0],
        value_rows[0, 0],
        fast_gate[0],
        fast_up[0],
        fast_down[0],
        -step[:, None],
    )
    inner_near = list(lax.optimization_barrier(tuple(inner_near)))
    inner_rows = spread(inner_near, inner_local)
    inner_rows[-1], queries = lax.optimization_barrier((inner_rows[-1], query_rows[0, 0]))
    read_near, read_local = gather(queries, read_cotangent[0, 0])
    slots = [piece[2 * half :] for piece in inner_near]
    slots.append(jnp.where(core == place - home_of(0), kept, inner_rows[-1][4 * half :]))
    together = jnp.stack(slots)
    parts = [together]
    for shift in range(1, reps):
        parts.append(lax.ppermute(together, "rep", shifted(shift, 1)))
    if cells > 1:
        parts = [lax.all_gather(jnp.stack(parts), "tok", axis_index_groups=cell_groups)]

    size = CELL * half
    count = 2 * size
    square = shape((3, width, cols), F32)
    tall = shape((count, cols), F32)
    product = 6 * count * width * cols
    buffers = [pltpu.VMEM((size, depth), F32)] * 2
    both = [pltpu.VMEM((2, size, depth), F32)] * 2
    split_square = pltpu.VMEM((2, 3, width, cols), BF16)
    weights, gates, ups, backs, key_turned, steps = call(
        functools.partial(inner_kernel, cells, reps),
        parts + inner_rows,
        [HBM] * (len(parts) + 8),
        [square, tall, tall, tall, shape((2, 2, depth, count), BF16), square],
        [VMEM] * 6,
        both
        + [
            split_square,
            pltpu.VMEM((2, 3, count, cols), BF16),
            dma((2, 2, CELL)),
            dma((cells * reps * CELL * 4,)),
        ],
        6 * product,
    )
    if cells > 1:
        steps = lax.psum(steps, "tok", axis_index_groups=cell_groups)
    narrow = shape((3, width, cols), BF16)
    high, low = call(
        renew_kernel, (weights, steps), [VMEM] * 2, [narrow, narrow], [VMEM] * 2, []
    )
    *read_near, read_local, high = lax.optimization_barrier((*read_near, read_local, high))
    read_rows = spread(list(read_near), read_local)
    piece = shape((half, depth), F32)
    turned = shape((2, 2, depth, size), BF16)
    acts = shape((2, 3, size, cols), BF16)
    read_scratch = buffers + [pltpu.VMEM((size, depth), F32), dma((2, CELL)), dma((CELL,))]
    *query_near, query_first, turned_first, acts_first = call(
        functools.partial(read_kernel, 0),
        read_rows[:ROUNDS] + read_rows[2 * ROUNDS :] + [high, low],
        [HBM] * (ROUNDS + 2) + [VMEM] * 2,
        [piece] * CELL + [turned, acts],
        [HBM] * CELL + [VMEM] * 2,
        read_scratch,
        5 * product // 2,
        18,
    )
    totals, query_far = call(
        functools.partial(read_kernel, 1),
        read_rows[ROUNDS:] + [high, low, turned_first, acts_first],
        [HBM] * (ROUNDS + 2) + [VMEM] * 4,
        [square, shape((size, depth), F32)],
        [VMEM, HBM],
        [pltpu.VMEM(turned.shape, BF16), pltpu.VMEM(acts.shape, BF16)] + read_scratch,
        11 * product // 2,
        18,
    )
    if cells > 1:
        totals = lax.psum(totals, "tok", axis_index_groups=cell_groups)
    cots, direct = call(
        functools.partial(renew_back_kernel, cells),
        [weights, steps, totals],
        [VMEM] * 3,
        [shape((2, 3, width, cols), BF16), square],
        [VMEM] * 2,
        [],
    )
    acts_cot, *given = call(
        functools.partial(weight_grad_kernel, cells, reps),
        inner_rows + [key_turned, direct, cots, gates, ups, backs],
        [HBM] * 8 + [VMEM] * 6,
        [shape((2, 3, count, cols), BF16)] + [shape((cells, CELL, 3, rows, cols), F32)] * reps,
        [VMEM] + [HBM] * reps,
        both
        + [pltpu.VMEM((3, width, cols), F32), dma((2, 2, CELL)), dma((cells * reps * CELL,))],
        6 * product,
        18,
    )

    def token_grads(side, acts):
        piece = shape((2 * half, depth), F32)
        outs = [shape((2 * size, depth), F32)] if side else [piece] * CELL
        return call(
            functools.partial(token_grad_kernel, side),
            [weights, cots, acts, gates, ups, backs],
            [VMEM] * 6,
            outs,
            [HBM] * len(outs),
            [split_square, pltpu.VMEM((2, size, depth), F32), dma((2, CELL))],
            3 * product,
            14,
        )

    def across(value):
        return lax.ppermute(value, "head", SWAP)

    query_got = across(query_far)
    query_low = query_first + across(query_first)
    query_high = (query_far + query_got)[ROUNDS * half :]
    query_got, acts_cot = lax.optimization_barrier((query_got, acts_cot))
    totals_query = [
        part + query_got[turn * half : (turn + 1) * half] for turn, part in enumerate(query_near)
    ]
    acts_cot, *totals_query = lax.optimization_barrier((acts_cot, *totals_query))
    query_back = [
        lax.ppermute(totals_query[turn], PLACE, flipped(pairs[turn])) for turn in range(ROUNDS)
    ]
    (token_far,) = token_grads(1, acts_cot)
    acts_cot, token_far = lax.optimization_barrier((acts_cot, token_far))
    token_got = across(token_far)
    token_near = list(token_grads(0, acts_cot))
    token_near[0], *query_back = lax.optimization_barrier((token_near[0], *query_back))
    back = hand_back(token_near, token_got)
    token_low = token_near[ROUNDS] + across(token_near[ROUNDS])
    token_high = (token_far + token_got)[ROUNDS * 2 * half :]
    given = list(given)
    given[0], *back = lax.optimization_barrier((given[0], *back))
    (query_grad,) = settle(query_back, query_low, query_high)
    key_grad, target_grad = settle(back, token_low, token_high)

    if cells > 1:
        given = [
            lax.psum_scatter(value, "tok", scatter_dimension=0, tiled=True, axis_index_groups=cell_groups)
            for value in given
        ]
    total = given[0][0]
    for shift in range(1, reps):
        total = total + lax.ppermute(given[shift][0], "rep", shifted(shift, 1))
    returned = [
        lax.ppermute(total[turn], PLACE, flipped(pairs[turn])) for turn in range(ROUNDS)
    ]
    home_piece = total[ROUNDS]
    home_other = lax.ppermute(home_piece, "head", SWAP)

    def choose(turn):
        return jnp.where(turn == 0, returned[0], jnp.where(turn == 1, returned[1], returned[2]))

    left = jnp.where(at_home, jnp.where(core == 0, home_piece, home_other), choose(turn0))
    right = jnp.where(at_home, jnp.where(core == 0, home_other, home_piece), choose(turn1))
    owned = jnp.concatenate((left, right), axis=2)

    value_grad = -step[:, None] * target_grad
    step_grad = -jnp.sum(value_rows[0, 0] * target_grad, axis=1)
    logit_grad = step_grad * factor * jax.nn.sigmoid(step_logits[0, 0])
    return (
        query_grad[None, None],
        key_grad[None, None],
        value_grad[None, None],
        logit_grad[None, None],
        owned[0][None],
        owned[1][None],
        owned[2][None],
    )


def solution(mesh):
    tokens = P(("groups", "rep"), "head", "tok", None)
    logits = P(("groups", "rep"), "head", "tok")
    weight = P("head", ("tok", "rep"), None)
    grad = P(("groups", "head"), ("tok", "rep"), None)
    return jax.shard_map(
        per_device,
        mesh=mesh,
        in_specs=(tokens, tokens, tokens, logits, tokens, weight, weight, weight),
        out_specs=(tokens, tokens, tokens, logits, grad, grad, grad),
        check_vma=False,
    )
```

```python
import functools
import math

import jax
import jax.numpy as jnp
from jax import lax
from jax.experimental import pallas as pl
from jax.experimental.pallas import tpu as pltpu
from jax.sharding import PartitionSpec as P

EPSILON = 1e-06
CELL = 4
ROUNDS = CELL - 1
PLACE = ("tok", "head")
SWAP = [(0, 1), (1, 0)]
F32 = jnp.float32
BF16 = jnp.bfloat16
NN = ((1,), (0,))
NT = ((1,), (1,))
GROUP = 2
HBM = pl.BlockSpec(memory_space=pltpu.MemorySpace.HBM)
VMEM = pl.BlockSpec(memory_space=pltpu.VMEM)


def home_of(head):
    return (CELL - 1) // 2 + head


def source_of(head, turn):
    return (home_of(head) + 1 + (turn + 2 * (1 - head)) % ROUNDS) % CELL


def routes(cells):
    rounds = []
    for turn in range(ROUNDS):
        pairs = []
        for cell in range(cells):
            here = []
            for head in range(2):
                for core in range(2):
                    origin = cell * CELL + source_of(head, turn + core)
                    home = cell * CELL + home_of(head)
                    here.append((origin * 2 + head, home * 2 + core))
            everyone = range(cell * CELL * 2, (cell + 1) * CELL * 2)
            idle = sorted(set(everyone) - {first for first, _ in here})
            free = sorted(set(everyone) - {second for _, second in here})
            pairs += here + list(zip(idle, free))
        rounds.append(pairs)
    return rounds


def flipped(pairs):
    return [(second, first) for first, second in pairs]


def split(value):
    high = value.astype(BF16)
    return high, (value - high.astype(F32)).astype(BF16)


def dot3(left, right, form):
    def one(first, second):
        return lax.dot_general(first, second, (form, ((), ())), preferred_element_type=F32)

    return one(left[0], right[0]) + (one(left[0], right[1]) + one(left[1], right[0]))


def position():
    place = lax.rem(lax.axis_index("tok"), CELL)
    core = lax.axis_index("head")
    return place, core


def spot_of(place, core, slot):
    if slot == ROUNDS:
        return place
    head = place - home_of(0)
    return lax.rem(place + 1 + lax.rem(slot + core + 2 * (1 - head) + ROUNDS, ROUNDS), CELL)


def halves_sent(place, core):
    ahead = lax.rem(place - home_of(0) - core - 1 + 2 * CELL, CELL)
    turn0 = lax.rem(ahead + 1 - core, ROUNDS)
    turn1 = lax.rem(turn0 + ROUNDS - 1, ROUNDS)
    return turn0, turn1


def run_copies(copies):
    for copy in copies:
        copy.start()
    for copy in copies:
        copy.wait()


def weight_rows(rows):
    return rows * 3 // 2 if rows % 16 == 0 else rows * 2


def weight_blocks(rows, cols):
    blocks = [(0, 0, rows, 0, 0), (1, 0, rows, 0, cols)]
    if rows % 16 == 0:
        return blocks + [(2, 0, rows // 2, rows, 0), (2, rows // 2, rows // 2, rows, cols)]
    return blocks + [(2, 0, rows, rows, 0)]


def pack_kernel(half, with_weights, *refs):
    if with_weights:
        *sources, scale = refs[:6]
        first, second, gate, up, down = refs[-9:-4]
        outs, (load_sems, held, sems, weight_sems) = refs[6:-9], refs[-4:]
        loads = [
            pltpu.make_async_copy(source, there, load_sems.at[number])
            for number, (source, there) in enumerate(zip(sources, (first, second, gate, up, down)))
        ]
        for load in loads:
            load.start()
        loads[0].wait()
    else:
        first, second, *outs, sems = refs
    place, core = position()
    _, turn1 = halves_sent(place, core)

    def copies_of(which, ref):
        copies = []
        for piece in range(ROUNDS):
            begin = pl.multiple_of(jnp.where(turn1 == piece, half, 0), half)
            copies.append(
                pltpu.make_async_copy(
                    ref.at[pl.ds(begin, half)],
                    outs[piece].at[pl.ds(which * half, half)],
                    sems.at[piece, which],
                )
            )
        copies.append(
            pltpu.make_async_copy(
                ref, outs[ROUNDS].at[pl.ds(which * 2 * half, 2 * half)], sems.at[ROUNDS, which]
            )
        )
        return copies

    copies = copies_of(0, first)
    for copy in copies:
        copy.start()
    if with_weights:
        loads[1].wait()
        held[...] = second[...] * scale[...]
    late = copies_of(1, held if with_weights else second)
    for copy in late:
        copy.start()
    if with_weights:
        for load in loads[2:]:
            load.wait()
        rows, width = gate.shape
        cols = width // 2
        for piece, out in enumerate(outs):
            if piece < ROUNDS:
                part, top = jnp.where(turn1 == piece, 1, 0), 2 * half
            elif piece == ROUNDS:
                part, top = 1 - core, 4 * half
            else:
                part, top = core, 0
            begin = pl.multiple_of(part * cols, cols)
            for number, (which, start, size, row, col) in enumerate(weight_blocks(rows, cols)):
                copies.append(
                    pltpu.make_async_copy(
                        (gate, up, down)[which].at[pl.ds(start, size), pl.ds(begin, cols)],
                        out.at[pl.ds(top + row, size), pl.ds(col, cols)],
                        weight_sems.at[piece, number],
                    )
                )
                copies[-1].start()
    for copy in copies + late:
        copy.wait()


def fetch_rows(near, far, own, got, buffers, sems):
    half = buffers[0].shape[1] // 2
    place, core = position()
    mine = core == place - home_of(0)
    last = len(near)
    for block in range(last):
        for which in range(2):
            rows = pl.ds(which * half, half)
            for side, group in enumerate((near, far)):
                pltpu.make_async_copy(
                    group[block].at[rows],
                    buffers[which].at[block, pl.ds(side * half, half)],
                    sems.at[block, which * 2 + side],
                ).start()

    def local(source):
        for which in range(2):
            for side in range(2):
                pltpu.make_async_copy(
                    source.at[pl.ds((which * 2 + side) * half, half)],
                    buffers[which].at[last, pl.ds(side * half, half)],
                    sems.at[last, which * 2 + side],
                ).start()

    if own is None:
        return

    @pl.when(mine)
    def _():
        local(own)

    @pl.when(jnp.logical_not(mine))
    def _():
        local(got)


def take_rows(buffers, group, sems):
    size, depth = buffers[0].shape[1:]
    half = size // 2
    for each in range(GROUP):
        block = group * GROUP + each
        for part in range(4):
            view = buffers[part // 2].at[block, pl.ds((part % 2) * half, half)]
            pltpu.make_async_copy(view, view, sems.at[block, part]).wait()
    first, second = (
        buffer[pl.ds(group * GROUP, GROUP)].reshape(GROUP * size, depth) for buffer in buffers
    )
    return split(first), split(second)


def fetch_half(rounds, own, got, side, buffers, sems):
    half = buffers[0].shape[0] // CELL
    place, core = position()
    mine = core == place - home_of(0)
    for which in range(2):
        for turn, piece in enumerate(rounds):
            pltpu.make_async_copy(
                piece.at[pl.ds(which * half, half)],
                buffers[which].at[pl.ds(turn * half, half)],
                sems.at[which, turn],
            ).start()

    def local(source):
        for which in range(2):
            pltpu.make_async_copy(
                source.at[pl.ds((which * 2 + side) * half, half)],
                buffers[which].at[pl.ds(ROUNDS * half, half)],
                sems.at[which, ROUNDS],
            ).start()

    @pl.when(mine)
    def _():
        local(own)

    @pl.when(jnp.logical_not(mine))
    def _():
        local(got)


def take_half(buffers, sems):
    half = buffers[0].shape[0] // CELL
    for which in range(2):
        for chunk in range(CELL):
            view = buffers[which].at[pl.ds(chunk * half, half)]
            pltpu.make_async_copy(view, view, sems.at[which, chunk]).wait()
    return split(buffers[0][...]), split(buffers[1][...])


def row_starts(cells, reps, rows):
    place, core = position()
    rep = lax.axis_index("rep")
    starts = {}
    for cell in range(cells):
        for shift in range(reps):
            owner_rep = lax.rem(rep - shift + reps, reps)
            for slot in range(CELL):
                spot = spot_of(place, core, slot)
                begin = ((cell * CELL + spot) * reps + owner_rep) * rows
                starts[cell, shift, slot] = pl.multiple_of(begin, rows)
    return starts


def silu_parts(pre):
    sigma = jax.nn.sigmoid(pre)
    rest = 1.0 - sigma
    return sigma, pre * sigma, sigma * (1.0 + pre * rest)


def store_split(ref, index, value):
    high, low = split(value)
    ref[(0,) + index] = high
    ref[(1,) + index] = low


def pair_of(ref, *index):
    return ref[(0,) + index], ref[(1,) + index]


def inner_kernel(cells, reps, *refs):
    pieces = reps if cells == 1 else 1
    parts, refs = refs[:pieces], refs[pieces:]
    near, far, (own, got), refs = refs[:3], refs[3:6], refs[6:8], refs[8:]
    weights, gates, ups, backs, turned, steps, *scratch = refs
    keys, targets, wide, acts, row_sems, weight_sems = scratch
    rows, cols = weights.shape[1] // (cells * reps * CELL), weights.shape[2]
    copies = []
    for (cell, shift, slot), begin in row_starts(cells, reps, rows).items():
        source = parts[shift].at[slot] if cells == 1 else parts[0].at[cell, shift, slot]
        for which, start, size, row, col in weight_blocks(rows, cols):
            copies.append(
                pltpu.make_async_copy(
                    source.at[pl.ds(row, size), pl.ds(col, cols)],
                    weights.at[which, pl.ds(pl.multiple_of(begin + start, size), size)],
                    weight_sems.at[len(copies)],
                )
            )
    for copy in copies:
        copy.start()
    fetch_rows(near, far, own, got, (keys, targets), row_sems)
    for copy in copies:
        copy.wait()
    for which in range(3):
        store_split(wide, (which,), weights[which])
    size = keys.shape[1] * GROUP

    @pl.loop(0, CELL // GROUP)
    def _(group):
        key, target = take_rows((keys, targets), group, row_sems)
        where = pl.ds(pl.multiple_of(group * size, size), size)
        gate_pre = dot3(key, pair_of(wide, 0), NN)
        up_pre = dot3(key, pair_of(wide, 1), NN)
        back = dot3(target, pair_of(wide, 2), NN)
        gates[where] = gate_pre
        ups[where] = up_pre
        backs[where] = back
        _, act, slope = silu_parts(gate_pre)
        store_split(acts, (0, where), back * up_pre * slope)
        store_split(acts, (1, where), back * act)
        store_split(acts, (2, where), act * up_pre)
        for part in range(2):
            turned[part, 0, :, where] = key[part].T
            turned[part, 1, :, where] = target[part].T

    for which in range(3):
        steps[which] = dot3(pair_of(turned, which // 2), pair_of(acts, which), NN)


def renew_kernel(weights, steps, high, low):
    for which in range(3):
        weight = weights[which]
        moved = weight - steps[which]
        old = jnp.mean(weight * weight, axis=0, keepdims=True) + EPSILON
        new = jnp.mean(moved * moved, axis=0, keepdims=True) + EPSILON
        high[which], low[which] = split(moved * (jnp.sqrt(old) / jnp.sqrt(new)))


def read_kernel(side, *refs):
    rounds, (own, got, high, low), refs = refs[:3], refs[3:7], refs[7:]
    before, refs = (refs[:2], refs[2:]) if side else ((), refs)
    main, refs = (refs[0], refs[1:]) if side else (None, refs)
    round_out, rest_out = (refs[:3], refs[3]) if side == 0 else (None, refs[0])
    refs = refs[4:] if side == 0 else refs[1:]
    turned, acts, queries, cots, sent, row_sems, out_sems = refs
    half = queries.shape[0] // CELL
    fetch_half(rounds, own, got, side, (queries, cots), row_sems)

    def weight(which):
        return high[which], low[which]

    query, cot = take_half((queries, cots), row_sems)
    gate_pre = dot3(query, weight(0), NN)
    up_pre = dot3(query, weight(1), NN)
    back = dot3(cot, weight(2), NN)
    _, act, slope = silu_parts(gate_pre)
    gate_back = split(back * up_pre * slope)
    up_back = split(back * act)
    sent[...] = dot3(gate_back, weight(0), NT) + dot3(up_back, weight(1), NT)
    if side == 0:
        copies = [
            pltpu.make_async_copy(sent.at[pl.ds(turn * half, half)], out, out_sems.at[turn])
            for turn, out in enumerate(round_out)
        ]
        copies.append(
            pltpu.make_async_copy(
                sent.at[pl.ds(ROUNDS * half, half)], rest_out, out_sems.at[ROUNDS]
            )
        )
    else:
        copies = [pltpu.make_async_copy(sent, rest_out, out_sems.at[0])]
    for copy in copies:
        copy.start()
    for part in range(2):
        acts[part, 0] = gate_back[part]
        acts[part, 1] = up_back[part]
        turned[part, 0] = query[part].T
        turned[part, 1] = cot[part].T
    store_split(acts, (2,), act * up_pre)
    if side:
        for which in range(3):
            main[which] = dot3(
                pair_of(before[0], which // 2), pair_of(before[1], which), NN
            ) + dot3(pair_of(turned, which // 2), pair_of(acts, which), NN)
    for copy in copies:
        copy.wait()


def renew_back_kernel(cells, weights, steps, totals, cots, direct):
    scale = 1.0 / weights.shape[1]
    for which in range(3):
        weight, total = weights[which], totals[which]
        moved = weight - steps[which]
        old = jnp.mean(weight * weight, axis=0, keepdims=True) + EPSILON
        new = jnp.mean(moved * moved, axis=0, keepdims=True) + EPSILON
        ratio = jnp.sqrt(old) / jnp.sqrt(new)
        ratio_cot = jnp.sum(total * moved, axis=0, keepdims=True) * scale
        moved_cot = ratio * (total - moved * (ratio_cot / new))
        grad = moved_cot + weight * (ratio_cot * ratio / old)
        if cells > 1:
            grad = grad * jnp.where(lax.axis_index("tok") < CELL, 1.0, 0.0)
        direct[which] = grad
        store_split(cots, (which,), -moved_cot)


def write_grads(cells, reps, turned, direct, parts, pieces, grads, grad_sems):
    for which in range(3):
        total = direct[which]
        begin = 0
        for acts in parts:
            span = pl.ds(begin, acts.shape[2])
            begin += acts.shape[2]
            left = turned[0, which // 2, :, span], turned[1, which // 2, :, span]
            total = total + dot3(left, pair_of(acts, which), NN)
        grads[which] = total
    rows = pieces[0].shape[-2]
    copies = []
    place, core = position()
    rep = lax.axis_index("rep")
    for cell in range(cells):
        for shift in range(reps):
            owner_rep = lax.rem(rep + shift, reps)
            for slot in range(CELL):
                spot = spot_of(place, core, slot)
                begin = pl.multiple_of(((cell * CELL + spot) * reps + owner_rep) * rows, rows)
                copies.append(
                    pltpu.make_async_copy(
                        grads.at[:, pl.ds(begin, rows)],
                        pieces[shift].at[cell, slot],
                        grad_sems.at[len(copies)],
                    )
                )
    run_copies(copies)


def token_grad_kernel(cells, reps, first, last, *refs):
    rounds = min(last, ROUNDS) - first
    near, far, refs = refs[:rounds], refs[rounds : 2 * rounds], refs[2 * rounds :]
    own, got, final = None, None, last > ROUNDS
    if final:
        (own, got, turned, direct, before), refs = refs[:5], refs[5:]
    (weights, cots, gates, ups, backs), refs = refs[:5], refs[5:]
    near_out, far_out, refs = refs[:rounds], refs[rounds], refs[rounds + 1 :]
    if final:
        pieces, (acts, grads, grad_sems), refs = refs[:reps], refs[reps : reps + 3], refs[reps + 3 :]
    else:
        acts, refs = refs[0], refs[1:]
    keys, targets, wide, sent, row_sems, out_sems = refs
    fetch_rows(near, far, own, got, (keys, targets), row_sems)
    size = sent.shape[2]
    half = size // 2
    for which in range(3):
        store_split(wide, (which,), weights[which])

    def outgoing(number):
        if number < rounds:
            near = [
                (sent.at[which, number, pl.ds(0, half)], near_out[number].at[pl.ds(which * half, half)])
                for which in range(2)
            ]
            far = [
                (
                    sent.at[which, number, pl.ds(half, half)],
                    far_out.at[pl.ds(number * size + which * half, half)],
                )
                for which in range(2)
            ]
            return near + far
        return [
            (sent.at[which, number], far_out.at[pl.ds((rounds + which) * size, size)])
            for which in range(2)
        ]

    @pl.loop(0, (last - first) // GROUP)
    def _(group):
        key, target = take_rows((keys, targets), group, row_sems)
        many = GROUP * size
        where = pl.ds(pl.multiple_of(first * size + group * many, many), many)
        here = pl.ds(pl.multiple_of(group * many, many), many)
        there = pl.ds(group * GROUP, GROUP)
        gate_back_cot = dot3(key, pair_of(cots, 0), NN)
        up_back_cot = dot3(key, pair_of(cots, 1), NN)
        hidden_cot = dot3(target, pair_of(cots, 2), NN)
        gate_pre, up_pre, back = gates[where], ups[where], backs[where]
        sigma, act, slope = silu_parts(gate_pre)
        bend = sigma * (1.0 - sigma) * (2.0 + gate_pre * (1.0 - 2.0 * sigma))
        mixed = gate_back_cot * slope
        gate_cot = split(
            gate_back_cot * back * up_pre * bend
            + (up_back_cot * back + hidden_cot * up_pre) * slope
        )
        up_cot = split(mixed * back + hidden_cot * act)
        back_cot = split(mixed * up_pre + up_back_cot * act)
        for part in range(2):
            acts[part, 0, here] = gate_cot[part]
            acts[part, 1, here] = up_cot[part]
            acts[part, 2, here] = back_cot[part]
        key_part = (
            dot3(gate_cot, pair_of(wide, 0), NT)
            + dot3(up_cot, pair_of(wide, 1), NT)
            + dot3(split(back * up_pre * slope), pair_of(cots, 0), NT)
            + dot3(split(back * act), pair_of(cots, 1), NT)
        )
        target_part = dot3(back_cot, pair_of(wide, 2), NT) + dot3(
            split(act * up_pre), pair_of(cots, 2), NT
        )
        sent[0, there] = key_part.reshape(GROUP, size, key_part.shape[1])
        sent[1, there] = target_part.reshape(GROUP, size, target_part.shape[1])
        for each in range(last - first):

            @pl.when(group == each // GROUP)
            def _():
                for side, (source, out) in enumerate(outgoing(each)):
                    pltpu.make_async_copy(source, out, out_sems.at[each, side]).start()

    if final:
        write_grads(cells, reps, turned, direct, (before, acts), pieces, grads, grad_sems)
    for each in range(last - first):
        for side, (source, out) in enumerate(outgoing(each)):
            pltpu.make_async_copy(source, out, out_sems.at[each, side]).wait()


def call(kernel, inputs, in_specs, outs, out_specs, scratch, flops=0, grant=26):
    moved = sum(math.prod(value.shape) * value.dtype.itemsize for value in list(inputs) + list(outs))
    return pl.pallas_call(
        kernel,
        out_shape=outs,
        in_specs=in_specs,
        out_specs=out_specs,
        scratch_shapes=scratch,
        cost_estimate=pl.CostEstimate(flops=flops, bytes_accessed=moved, transcendentals=0),
        compiler_params=pltpu.CompilerParams(vmem_limit_bytes=grant << 20),
    )(*inputs)


def per_device(
    query_rows, key_rows, value_rows, step_logits, read_cotangent, fast_gate, fast_up, fast_down
):
    tokens_here, depth = key_rows.shape[2:]
    half = tokens_here // 2
    tok_size = lax.axis_size("tok")
    reps = lax.axis_size("rep")
    cells = tok_size // CELL
    assert tok_size % CELL == 0 and lax.axis_size("head") == 2
    factor = 1.0 / (8.0 * math.sqrt(tokens_here * tok_size))
    pairs = routes(cells)
    place, core = position()
    turn0, turn1 = halves_sent(place, core)
    at_home = place == home_of(0) + core
    cell_groups = [[cell * CELL + spot for cell in range(cells)] for spot in range(CELL)]
    rows, width = fast_gate.shape[1:]
    cols = width // 2
    shape = jax.ShapeDtypeStruct
    dma = pltpu.SemaphoreType.DMA

    def shifted(shift, sign):
        return [(rep, (rep + sign * shift) % reps) for rep in range(reps)]

    step = jax.nn.softplus(step_logits[0, 0]) * factor

    weight_count = weight_rows(rows)

    def gather(first, second, *rest):
        extra = weight_count if rest else 0
        outs = [shape((2 * half + extra, depth), F32)] * ROUNDS
        outs.append(shape((4 * half + extra, depth), F32))
        scratch = [dma((CELL, 2))]
        if rest:
            outs.append(shape((extra, depth), F32))
            weights_held = [pltpu.VMEM((rows, width), F32)] * 3
            scratch = (
                [pltpu.VMEM((2 * half, depth), F32)] * 2
                + weights_held
                + [dma((5,)), pltpu.VMEM((2 * half, depth), F32)]
                + scratch
                + [dma((CELL + 1, 4))]
            )
        inputs = [first, second, *rest]
        packed = call(
            functools.partial(pack_kernel, half, bool(rest)),
            inputs,
            [HBM] * 5 + [VMEM] if rest else [VMEM] * 2,
            outs,
            [HBM] * len(outs),
            scratch,
            grant=60 if rest else 26,
        )
        near = [lax.ppermute(packed[turn], PLACE, pairs[turn]) for turn in range(ROUNDS)]
        return near, *packed[ROUNDS:]

    def spread(near, local):
        far = [lax.ppermute(piece, "head", SWAP) for piece in near]
        return near + far + [local, lax.ppermute(local, "head", SWAP)]

    def combine(near, far, across=None):
        if across is None:
            across = lax.ppermute(far, "head", SWAP)
        length = near[0].shape[0]
        found = [
            part + across[number * length : (number + 1) * length]
            for number, part in enumerate(near)
        ]
        return found, far[len(near) * length :] + across[len(near) * length :]

    def hand_back(totals, first):
        return [
            lax.ppermute(total, PLACE, flipped(pairs[first + number]))
            for number, total in enumerate(totals)
        ]

    def settle(back, local):
        def choose(turn):
            return jnp.where(turn == 0, back[0], jnp.where(turn == 1, back[1], back[2]))

        low, high = choose(turn0), choose(turn1)
        found = []
        for which in range(low.shape[0] // half):
            span = slice(which * half, (which + 1) * half)
            remote = jnp.concatenate((low[span], high[span]))
            here = local[which * 2 * half : (which + 1) * 2 * half]
            found.append(jnp.where(at_home, here, remote))
        return found

    inner_near, inner_local, kept = gather(
        key_rows[0, 0],
        value_rows[0, 0],
        fast_gate[0],
        fast_up[0],
        fast_down[0],
        -step[:, None],
    )
    inner_near = list(lax.optimization_barrier(tuple(inner_near)))
    inner_rows = spread(inner_near, inner_local)
    inner_rows[-1], queries = lax.optimization_barrier((inner_rows[-1], query_rows[0, 0]))
    read_near, read_local = gather(queries, read_cotangent[0, 0])
    slots = [piece[2 * half :] for piece in inner_near]
    slots.append(jnp.where(core == place - home_of(0), kept, inner_rows[-1][4 * half :]))
    together = jnp.stack(slots)
    parts = [together]
    for shift in range(1, reps):
        parts.append(lax.ppermute(together, "rep", shifted(shift, 1)))
    if cells > 1:
        parts = [lax.all_gather(jnp.stack(parts), "tok", axis_index_groups=cell_groups)]

    size = 2 * half
    count = CELL * size
    square = shape((3, width, cols), F32)
    tall = shape((count, cols), F32)
    product = 6 * count * width * cols
    buffers = [pltpu.VMEM((CELL, size, depth), F32)] * 2
    turned = pltpu.VMEM((2, 2, depth, count), BF16)
    acts = pltpu.VMEM((2, 3, count, cols), BF16)
    split_square = pltpu.VMEM((2, 3, width, cols), BF16)
    weights, gates, ups, backs, key_turned, steps = call(
        functools.partial(inner_kernel, cells, reps),
        parts + inner_rows,
        [HBM] * (len(parts) + 8),
        [square, tall, tall, tall, shape((2, 2, depth, count), BF16), square],
        [VMEM] * 6,
        buffers + [split_square, acts, dma((CELL, 4)), dma((cells * reps * CELL * 4,))],
        6 * product,
    )
    if cells > 1:
        steps = lax.psum(steps, "tok", axis_index_groups=cell_groups)
    narrow = shape((3, width, cols), BF16)
    high, low = call(
        renew_kernel, (weights, steps), [VMEM] * 2, [narrow, narrow], [VMEM] * 2, []
    )
    *read_near, read_local, high = lax.optimization_barrier((*read_near, read_local, high))
    read_rows = spread(list(read_near), read_local)
    span = CELL * half
    piece = shape((half, depth), F32)
    turned_shape = shape((2, 2, depth, span), BF16)
    acts_shape = shape((2, 3, span, cols), BF16)
    read_scratch = [pltpu.VMEM((span, depth), F32)] * 3 + [dma((2, CELL)), dma((CELL,))]
    *query_near, query_first, turned_first, read_acts = call(
        functools.partial(read_kernel, 0),
        read_rows[:ROUNDS] + read_rows[2 * ROUNDS :] + [high, low],
        [HBM] * (ROUNDS + 2) + [VMEM] * 2,
        [piece] * CELL + [turned_shape, acts_shape],
        [HBM] * CELL + [VMEM] * 2,
        read_scratch,
        5 * product // 2,
        18,
    )
    totals, query_far = call(
        functools.partial(read_kernel, 1),
        read_rows[ROUNDS:] + [high, low, turned_first, read_acts],
        [HBM] * (ROUNDS + 2) + [VMEM] * 4,
        [square, shape((span, depth), F32)],
        [VMEM, HBM],
        [pltpu.VMEM(turned_shape.shape, BF16), pltpu.VMEM(acts_shape.shape, BF16)] + read_scratch,
        11 * product // 2,
        18,
    )
    if cells > 1:
        totals = lax.psum(totals, "tok", axis_index_groups=cell_groups)
    cots, direct = call(
        functools.partial(renew_back_kernel, cells),
        [weights, steps, totals],
        [VMEM] * 3,
        [shape((2, 3, width, cols), BF16), square],
        [VMEM] * 2,
        [],
    )
    middle = 2

    def token_grads(first, last, cots, *more):
        rounds = min(last, ROUNDS) - first
        span = slice(first, first + rounds)
        inputs = inner_rows[:ROUNDS][span] + inner_rows[ROUNDS : 2 * ROUNDS][span]
        if more:
            inputs = inputs + inner_rows[2 * ROUNDS :]
        blocks = last - first
        specs = [HBM] * len(inputs) + [VMEM] * (len(more) + 5)
        outs = [shape((size, depth), F32)] * rounds
        outs.append(shape((size * (2 * blocks - rounds), depth), F32))
        acts = (2, 3, blocks * size, cols)
        if more:
            outs += [shape((cells, CELL, 3, rows, cols), F32)] * reps
            scratch = [
                pltpu.VMEM(acts, BF16),
                pltpu.VMEM((3, width, cols), F32),
                dma((cells * reps * CELL,)),
            ]
            out_specs = [HBM] * len(outs)
        else:
            out_specs = [HBM] * len(outs) + [VMEM]
            outs.append(shape(acts, BF16))
            scratch = []
        outs = call(
            functools.partial(token_grad_kernel, cells, reps, first, last),
            inputs + [*more, weights, cots, gates, ups, backs],
            specs,
            outs,
            out_specs,
            scratch
            + [pltpu.VMEM((blocks, size, depth), F32)] * 2
            + [
                split_square,
                pltpu.VMEM((2, blocks, size, depth), F32),
                dma((blocks, 4)),
                dma((blocks, 4)),
            ],
            9 * product * blocks // CELL + (3 * product if more else 0),
        )
        return outs[:rounds], outs[rounds], list(outs[rounds + 1 :])

    near_first, far_first, (acts_first,) = token_grads(0, middle, cots)
    query_got = lax.ppermute(query_far, "head", SWAP)
    query_totals = [
        part + query_got[turn * half : (turn + 1) * half] for turn, part in enumerate(query_near)
    ]
    cots, *query_totals = lax.optimization_barrier((cots, *query_totals))
    query_back = hand_back(query_totals, 0)
    near_last, far_last, given = token_grads(middle, CELL, cots, key_turned, direct, acts_first)
    got_first = lax.ppermute(far_first, "head", SWAP)
    far_last, got_first, *rest = lax.optimization_barrier(
        (far_last, got_first, *near_first, *query_back)
    )
    near_first, query_back = rest[:-ROUNDS], rest[-ROUNDS:]
    totals_first, _ = combine(near_first, far_first, got_first)
    back = hand_back(totals_first, 0)
    totals_last, local = combine(near_last, far_last)
    back += hand_back(totals_last, middle)
    query_first, *totals_last = lax.optimization_barrier((query_first, *totals_last))
    query_local = jnp.concatenate(
        (
            query_first + lax.ppermute(query_first, "head", SWAP),
            (query_far + query_got)[ROUNDS * half :],
        )
    )
    given[0], *back = lax.optimization_barrier((given[0], *back))
    (query_grad,) = settle(query_back, query_local)
    key_grad, target_grad = settle(back, local)

    if cells > 1:
        given = [
            lax.psum_scatter(value, "tok", scatter_dimension=0, tiled=True, axis_index_groups=cell_groups)
            for value in given
        ]
    total = given[0][0]
    for shift in range(1, reps):
        total = total + lax.ppermute(given[shift][0], "rep", shifted(shift, 1))
    returned = [
        lax.ppermute(total[turn], PLACE, flipped(pairs[turn])) for turn in range(ROUNDS)
    ]
    home_piece = total[ROUNDS]
    home_other = lax.ppermute(home_piece, "head", SWAP)

    def choose(turn):
        return jnp.where(turn == 0, returned[0], jnp.where(turn == 1, returned[1], returned[2]))

    left = jnp.where(at_home, jnp.where(core == 0, home_piece, home_other), choose(turn0))
    right = jnp.where(at_home, jnp.where(core == 0, home_other, home_piece), choose(turn1))
    owned = jnp.concatenate((left, right), axis=2)

    value_grad = -step[:, None] * target_grad
    step_grad = -jnp.sum(value_rows[0, 0] * target_grad, axis=1)
    logit_grad = step_grad * factor * jax.nn.sigmoid(step_logits[0, 0])
    return (
        query_grad[None, None],
        key_grad[None, None],
        value_grad[None, None],
        logit_grad[None, None],
        owned[0][None],
        owned[1][None],
        owned[2][None],
    )


def solution(mesh):
    tokens = P(("groups", "rep"), "head", "tok", None)
    logits = P(("groups", "rep"), "head", "tok")
    weight = P("head", ("tok", "rep"), None)
    grad = P(("groups", "head"), ("tok", "rep"), None)
    return jax.shard_map(
        per_device,
        mesh=mesh,
        in_specs=(tokens, tokens, tokens, logits, tokens, weight, weight, weight),
        out_specs=(tokens, tokens, tokens, logits, grad, grad, grad),
        check_vma=False,
    )
```

```python
import functools
import math

import jax
import jax.numpy as jnp
from jax import lax
from jax.experimental import pallas as pl
from jax.experimental.pallas import tpu as pltpu
from jax.sharding import PartitionSpec as P

EPSILON = 1e-06
CELL = 4
ROUNDS = CELL - 1
PLACE = ("tok", "head")
SWAP = [(0, 1), (1, 0)]
F32 = jnp.float32
BF16 = jnp.bfloat16
NN = ((1,), (0,))
NT = ((1,), (1,))
GROUP = 2
HBM = pl.BlockSpec(memory_space=pltpu.MemorySpace.HBM)
VMEM = pl.BlockSpec(memory_space=pltpu.VMEM)


def home_of(head):
    return (CELL - 1) // 2 + head


def source_of(head, turn):
    return (home_of(head) + 1 + (turn + 2 * (1 - head)) % ROUNDS) % CELL


def routes(cells):
    rounds = []
    for turn in range(ROUNDS):
        pairs = []
        for cell in range(cells):
            here = []
            for head in range(2):
                for core in range(2):
                    origin = cell * CELL + source_of(head, turn + core)
                    home = cell * CELL + home_of(head)
                    here.append((origin * 2 + head, home * 2 + core))
            everyone = range(cell * CELL * 2, (cell + 1) * CELL * 2)
            idle = sorted(set(everyone) - {first for first, _ in here})
            free = sorted(set(everyone) - {second for _, second in here})
            pairs += here + list(zip(idle, free))
        rounds.append(pairs)
    return rounds


def flipped(pairs):
    return [(second, first) for first, second in pairs]


def split(value):
    high = value.astype(BF16)
    return high, (value - high.astype(F32)).astype(BF16)


def dot3(left, right, form):
    def one(first, second):
        return lax.dot_general(first, second, (form, ((), ())), preferred_element_type=F32)

    return one(left[0], right[0]) + (one(left[0], right[1]) + one(left[1], right[0]))


def position():
    place = lax.rem(lax.axis_index("tok"), CELL)
    core = lax.axis_index("head")
    return place, core


def spot_of(place, core, slot):
    if slot == ROUNDS:
        return place
    head = place - home_of(0)
    return lax.rem(place + 1 + lax.rem(slot + core + 2 * (1 - head) + ROUNDS, ROUNDS), CELL)


def halves_sent(place, core):
    ahead = lax.rem(place - home_of(0) - core - 1 + 2 * CELL, CELL)
    turn0 = lax.rem(ahead + 1 - core, ROUNDS)
    turn1 = lax.rem(turn0 + ROUNDS - 1, ROUNDS)
    return turn0, turn1


def run_copies(copies):
    for copy in copies:
        copy.start()
    for copy in copies:
        copy.wait()


def weight_rows(rows):
    return rows * 3 // 2 if rows % 16 == 0 else rows * 2


def weight_blocks(rows, cols):
    blocks = [(0, 0, rows, 0, 0), (1, 0, rows, 0, cols)]
    if rows % 16 == 0:
        return blocks + [(2, 0, rows // 2, rows, 0), (2, rows // 2, rows // 2, rows, cols)]
    return blocks + [(2, 0, rows, rows, 0)]


def pack_kernel(half, with_weights, *refs):
    if with_weights:
        *sources, scale = refs[:6]
        first, second, gate, up, down = refs[-9:-4]
        outs, (load_sems, held, sems, weight_sems) = refs[6:-9], refs[-4:]
        loads = [
            pltpu.make_async_copy(source, there, load_sems.at[number])
            for number, (source, there) in enumerate(zip(sources, (first, second, gate, up, down)))
        ]
        for load in loads:
            load.start()
        loads[0].wait()
    else:
        first, second, *outs, sems = refs
    place, core = position()
    _, turn1 = halves_sent(place, core)

    def copies_of(which, ref):
        copies = []
        for piece in range(ROUNDS):
            begin = pl.multiple_of(jnp.where(turn1 == piece, half, 0), half)
            copies.append(
                pltpu.make_async_copy(
                    ref.at[pl.ds(begin, half)],
                    outs[piece].at[pl.ds(which * half, half)],
                    sems.at[piece, which],
                )
            )
        copies.append(
            pltpu.make_async_copy(
                ref, outs[ROUNDS].at[pl.ds(which * 2 * half, 2 * half)], sems.at[ROUNDS, which]
            )
        )
        return copies

    copies = copies_of(0, first)
    for copy in copies:
        copy.start()
    if with_weights:
        loads[1].wait()
        held[...] = second[...] * scale[...]
    late = copies_of(1, held if with_weights else second)
    for copy in late:
        copy.start()
    if with_weights:
        for load in loads[2:]:
            load.wait()
        rows, width = gate.shape
        cols = width // 2
        for piece, out in enumerate(outs):
            if piece < ROUNDS:
                part, top = jnp.where(turn1 == piece, 1, 0), 2 * half
            elif piece == ROUNDS:
                part, top = 1 - core, 4 * half
            else:
                part, top = core, 0
            begin = pl.multiple_of(part * cols, cols)
            for number, (which, start, size, row, col) in enumerate(weight_blocks(rows, cols)):
                copies.append(
                    pltpu.make_async_copy(
                        (gate, up, down)[which].at[pl.ds(start, size), pl.ds(begin, cols)],
                        out.at[pl.ds(top + row, size), pl.ds(col, cols)],
                        weight_sems.at[piece, number],
                    )
                )
                copies[-1].start()
    for copy in copies + late:
        copy.wait()


def fetch_rows(near, far, own, got, buffers, sems):
    half = buffers[0].shape[1] // 2
    place, core = position()
    mine = core == place - home_of(0)
    last = len(near)
    for block in range(last):
        for which in range(2):
            rows = pl.ds(which * half, half)
            for side, group in enumerate((near, far)):
                pltpu.make_async_copy(
                    group[block].at[rows],
                    buffers[which].at[block, pl.ds(side * half, half)],
                    sems.at[block, which * 2 + side],
                ).start()

    def local(source):
        for which in range(2):
            for side in range(2):
                pltpu.make_async_copy(
                    source.at[pl.ds((which * 2 + side) * half, half)],
                    buffers[which].at[last, pl.ds(side * half, half)],
                    sems.at[last, which * 2 + side],
                ).start()

    if own is None:
        return

    @pl.when(mine)
    def _():
        local(own)

    @pl.when(jnp.logical_not(mine))
    def _():
        local(got)


def take_rows(buffers, group, sems):
    size, depth = buffers[0].shape[1:]
    half = size // 2
    for each in range(GROUP):
        block = group * GROUP + each
        for part in range(4):
            view = buffers[part // 2].at[block, pl.ds((part % 2) * half, half)]
            pltpu.make_async_copy(view, view, sems.at[block, part]).wait()
    first, second = (
        buffer[pl.ds(group * GROUP, GROUP)].reshape(GROUP * size, depth) for buffer in buffers
    )
    return split(first), split(second)


def fetch_half(rounds, own, got, side, buffers, sems):
    half = buffers[0].shape[0] // CELL
    place, core = position()
    mine = core == place - home_of(0)
    for which in range(2):
        for turn, piece in enumerate(rounds):
            pltpu.make_async_copy(
                piece.at[pl.ds(which * half, half)],
                buffers[which].at[pl.ds(turn * half, half)],
                sems.at[which, turn],
            ).start()

    def local(source):
        for which in range(2):
            pltpu.make_async_copy(
                source.at[pl.ds((which * 2 + side) * half, half)],
                buffers[which].at[pl.ds(ROUNDS * half, half)],
                sems.at[which, ROUNDS],
            ).start()

    @pl.when(mine)
    def _():
        local(own)

    @pl.when(jnp.logical_not(mine))
    def _():
        local(got)


def take_half(buffers, sems):
    half = buffers[0].shape[0] // CELL
    for which in range(2):
        for chunk in range(CELL):
            view = buffers[which].at[pl.ds(chunk * half, half)]
            pltpu.make_async_copy(view, view, sems.at[which, chunk]).wait()
    return split(buffers[0][...]), split(buffers[1][...])


def row_starts(cells, reps, rows):
    place, core = position()
    rep = lax.axis_index("rep")
    starts = {}
    for cell in range(cells):
        for shift in range(reps):
            owner_rep = lax.rem(rep - shift + reps, reps)
            for slot in range(CELL):
                spot = spot_of(place, core, slot)
                begin = ((cell * CELL + spot) * reps + owner_rep) * rows
                starts[cell, shift, slot] = pl.multiple_of(begin, rows)
    return starts


def silu_parts(pre):
    sigma = jax.nn.sigmoid(pre)
    rest = 1.0 - sigma
    return sigma, pre * sigma, sigma * (1.0 + pre * rest)


def store_split(ref, index, value):
    high, low = split(value)
    ref[(0,) + index] = high
    ref[(1,) + index] = low


def pair_of(ref, *index):
    return ref[(0,) + index], ref[(1,) + index]


def inner_kernel(cells, reps, *refs):
    pieces = reps if cells == 1 else 1
    parts, refs = refs[:pieces], refs[pieces:]
    near, far, (own, got), refs = refs[:3], refs[3:6], refs[6:8], refs[8:]
    weights, gates, ups, backs, turned, steps, *scratch = refs
    keys, targets, wide, acts, row_sems, weight_sems = scratch
    rows, cols = weights.shape[1] // (cells * reps * CELL), weights.shape[2]
    copies = []
    for (cell, shift, slot), begin in row_starts(cells, reps, rows).items():
        source = parts[shift].at[slot] if cells == 1 else parts[0].at[cell, shift, slot]
        for which, start, size, row, col in weight_blocks(rows, cols):
            copies.append(
                pltpu.make_async_copy(
                    source.at[pl.ds(row, size), pl.ds(col, cols)],
                    weights.at[which, pl.ds(pl.multiple_of(begin + start, size), size)],
                    weight_sems.at[len(copies)],
                )
            )
    for copy in copies:
        copy.start()
    fetch_rows(near, far, own, got, (keys, targets), row_sems)
    for copy in copies:
        copy.wait()
    for which in range(3):
        store_split(wide, (which,), weights[which])
    size = keys.shape[1] * GROUP

    @pl.loop(0, CELL // GROUP)
    def _(group):
        key, target = take_rows((keys, targets), group, row_sems)
        where = pl.ds(pl.multiple_of(group * size, size), size)
        gate_pre = dot3(key, pair_of(wide, 0), NN)
        up_pre = dot3(key, pair_of(wide, 1), NN)
        back = dot3(target, pair_of(wide, 2), NN)
        gates[where] = gate_pre
        ups[where] = up_pre
        backs[where] = back
        _, act, slope = silu_parts(gate_pre)
        store_split(acts, (0, where), back * up_pre * slope)
        store_split(acts, (1, where), back * act)
        store_split(acts, (2, where), act * up_pre)
        for part in range(2):
            turned[part, 0, :, where] = key[part].T
            turned[part, 1, :, where] = target[part].T

    for which in range(3):
        steps[which] = dot3(pair_of(turned, which // 2), pair_of(acts, which), NN)


def renew_kernel(weights, steps, high, low):
    for which in range(3):
        weight = weights[which]
        moved = weight - steps[which]
        old = jnp.mean(weight * weight, axis=0, keepdims=True) + EPSILON
        new = jnp.mean(moved * moved, axis=0, keepdims=True) + EPSILON
        high[which], low[which] = split(moved * (jnp.sqrt(old) / jnp.sqrt(new)))


def read_kernel(side, *refs):
    rounds, (own, got, high, low), refs = refs[:3], refs[3:7], refs[7:]
    before, refs = (refs[:2], refs[2:]) if side else ((), refs)
    main, refs = (refs[0], refs[1:]) if side else (None, refs)
    round_out, rest_out = (refs[:3], refs[3]) if side == 0 else (None, refs[0])
    refs = refs[4:] if side == 0 else refs[1:]
    turned, acts, queries, cots, sent, row_sems, out_sems = refs
    half = queries.shape[0] // CELL
    fetch_half(rounds, own, got, side, (queries, cots), row_sems)

    def weight(which):
        return high[which], low[which]

    query, cot = take_half((queries, cots), row_sems)
    gate_pre = dot3(query, weight(0), NN)
    up_pre = dot3(query, weight(1), NN)
    back = dot3(cot, weight(2), NN)
    _, act, slope = silu_parts(gate_pre)
    gate_back = split(back * up_pre * slope)
    up_back = split(back * act)
    sent[...] = dot3(gate_back, weight(0), NT) + dot3(up_back, weight(1), NT)
    if side == 0:
        copies = [
            pltpu.make_async_copy(sent.at[pl.ds(turn * half, half)], out, out_sems.at[turn])
            for turn, out in enumerate(round_out)
        ]
        copies.append(
            pltpu.make_async_copy(
                sent.at[pl.ds(ROUNDS * half, half)], rest_out, out_sems.at[ROUNDS]
            )
        )
    else:
        copies = [pltpu.make_async_copy(sent, rest_out, out_sems.at[0])]
    for copy in copies:
        copy.start()
    for part in range(2):
        acts[part, 0] = gate_back[part]
        acts[part, 1] = up_back[part]
        turned[part, 0] = query[part].T
        turned[part, 1] = cot[part].T
    store_split(acts, (2,), act * up_pre)
    if side:
        for which in range(3):
            main[which] = dot3(
                pair_of(before[0], which // 2), pair_of(before[1], which), NN
            ) + dot3(pair_of(turned, which // 2), pair_of(acts, which), NN)
    for copy in copies:
        copy.wait()


def renew_back_kernel(cells, weights, steps, totals, cots, direct):
    scale = 1.0 / weights.shape[1]
    for which in range(3):
        weight, total = weights[which], totals[which]
        moved = weight - steps[which]
        old = jnp.mean(weight * weight, axis=0, keepdims=True) + EPSILON
        new = jnp.mean(moved * moved, axis=0, keepdims=True) + EPSILON
        ratio = jnp.sqrt(old) / jnp.sqrt(new)
        ratio_cot = jnp.sum(total * moved, axis=0, keepdims=True) * scale
        moved_cot = ratio * (total - moved * (ratio_cot / new))
        grad = moved_cot + weight * (ratio_cot * ratio / old)
        if cells > 1:
            grad = grad * jnp.where(lax.axis_index("tok") < CELL, 1.0, 0.0)
        direct[which] = grad
        store_split(cots, (which,), -moved_cot)


def weight_grad_kernel(cells, reps, turned, direct, before, after, *refs):
    parts, pieces, (grads, grad_sems) = (before, after), refs[:reps], refs[reps:]
    for which in range(3):
        total = direct[which]
        begin = 0
        for acts in parts:
            span = pl.ds(begin, acts.shape[2])
            begin += acts.shape[2]
            left = turned[0, which // 2, :, span], turned[1, which // 2, :, span]
            total = total + dot3(left, pair_of(acts, which), NN)
        grads[which] = total
    rows = pieces[0].shape[-2]
    copies = []
    place, core = position()
    rep = lax.axis_index("rep")
    for cell in range(cells):
        for shift in range(reps):
            owner_rep = lax.rem(rep + shift, reps)
            for slot in range(CELL):
                spot = spot_of(place, core, slot)
                begin = pl.multiple_of(((cell * CELL + spot) * reps + owner_rep) * rows, rows)
                copies.append(
                    pltpu.make_async_copy(
                        grads.at[:, pl.ds(begin, rows)],
                        pieces[shift].at[cell, slot],
                        grad_sems.at[len(copies)],
                    )
                )
    run_copies(copies)


def token_grad_kernel(first, last, *refs):
    rounds = min(last, ROUNDS) - first
    near, far, refs = refs[:rounds], refs[rounds : 2 * rounds], refs[2 * rounds :]
    own, got, final = None, None, last > ROUNDS
    if final:
        (own, got), refs = refs[:2], refs[2:]
    (weights, cots, gates, ups, backs), refs = refs[:5], refs[5:]
    near_out, far_out, refs = refs[:rounds], refs[rounds], refs[rounds + 1 :]
    acts, refs = refs[0], refs[1:]
    keys, targets, wide, sent, row_sems, out_sems = refs
    fetch_rows(near, far, own, got, (keys, targets), row_sems)
    size = sent.shape[2]
    half = size // 2
    for which in range(3):
        store_split(wide, (which,), weights[which])

    def outgoing(number):
        if number < rounds:
            near = [
                (sent.at[which, number, pl.ds(0, half)], near_out[number].at[pl.ds(which * half, half)])
                for which in range(2)
            ]
            far = [
                (
                    sent.at[which, number, pl.ds(half, half)],
                    far_out.at[pl.ds(number * size + which * half, half)],
                )
                for which in range(2)
            ]
            return near + far
        return [
            (sent.at[which, number], far_out.at[pl.ds((rounds + which) * size, size)])
            for which in range(2)
        ]

    @pl.loop(0, (last - first) // GROUP)
    def _(group):
        key, target = take_rows((keys, targets), group, row_sems)
        many = GROUP * size
        where = pl.ds(pl.multiple_of(first * size + group * many, many), many)
        here = pl.ds(pl.multiple_of(group * many, many), many)
        there = pl.ds(group * GROUP, GROUP)
        gate_back_cot = dot3(key, pair_of(cots, 0), NN)
        up_back_cot = dot3(key, pair_of(cots, 1), NN)
        hidden_cot = dot3(target, pair_of(cots, 2), NN)
        gate_pre, up_pre, back = gates[where], ups[where], backs[where]
        sigma, act, slope = silu_parts(gate_pre)
        bend = sigma * (1.0 - sigma) * (2.0 + gate_pre * (1.0 - 2.0 * sigma))
        mixed = gate_back_cot * slope
        gate_cot = split(
            gate_back_cot * back * up_pre * bend
            + (up_back_cot * back + hidden_cot * up_pre) * slope
        )
        up_cot = split(mixed * back + hidden_cot * act)
        back_cot = split(mixed * up_pre + up_back_cot * act)
        for part in range(2):
            acts[part, 0, here] = gate_cot[part]
            acts[part, 1, here] = up_cot[part]
            acts[part, 2, here] = back_cot[part]
        key_part = (
            dot3(gate_cot, pair_of(wide, 0), NT)
            + dot3(up_cot, pair_of(wide, 1), NT)
            + dot3(split(back * up_pre * slope), pair_of(cots, 0), NT)
            + dot3(split(back * act), pair_of(cots, 1), NT)
        )
        target_part = dot3(back_cot, pair_of(wide, 2), NT) + dot3(
            split(act * up_pre), pair_of(cots, 2), NT
        )
        sent[0, there] = key_part.reshape(GROUP, size, key_part.shape[1])
        sent[1, there] = target_part.reshape(GROUP, size, target_part.shape[1])
        for each in range(last - first):

            @pl.when(group == each // GROUP)
            def _():
                for side, (source, out) in enumerate(outgoing(each)):
                    pltpu.make_async_copy(source, out, out_sems.at[each, side]).start()

    for each in range(last - first):
        for side, (source, out) in enumerate(outgoing(each)):
            pltpu.make_async_copy(source, out, out_sems.at[each, side]).wait()


def call(kernel, inputs, in_specs, outs, out_specs, scratch, flops=0, grant=26):
    moved = sum(math.prod(value.shape) * value.dtype.itemsize for value in list(inputs) + list(outs))
    return pl.pallas_call(
        kernel,
        out_shape=outs,
        in_specs=in_specs,
        out_specs=out_specs,
        scratch_shapes=scratch,
        cost_estimate=pl.CostEstimate(flops=flops, bytes_accessed=moved, transcendentals=0),
        compiler_params=pltpu.CompilerParams(vmem_limit_bytes=grant << 20),
    )(*inputs)


def per_device(
    query_rows, key_rows, value_rows, step_logits, read_cotangent, fast_gate, fast_up, fast_down
):
    tokens_here, depth = key_rows.shape[2:]
    half = tokens_here // 2
    tok_size = lax.axis_size("tok")
    reps = lax.axis_size("rep")
    cells = tok_size // CELL
    assert tok_size % CELL == 0 and lax.axis_size("head") == 2
    factor = 1.0 / (8.0 * math.sqrt(tokens_here * tok_size))
    pairs = routes(cells)
    place, core = position()
    turn0, turn1 = halves_sent(place, core)
    at_home = place == home_of(0) + core
    cell_groups = [[cell * CELL + spot for cell in range(cells)] for spot in range(CELL)]
    rows, width = fast_gate.shape[1:]
    cols = width // 2
    shape = jax.ShapeDtypeStruct
    dma = pltpu.SemaphoreType.DMA

    def shifted(shift, sign):
        return [(rep, (rep + sign * shift) % reps) for rep in range(reps)]

    step = jax.nn.softplus(step_logits[0, 0]) * factor

    weight_count = weight_rows(rows)

    def gather(first, second, *rest):
        extra = weight_count if rest else 0
        outs = [shape((2 * half + extra, depth), F32)] * ROUNDS
        outs.append(shape((4 * half + extra, depth), F32))
        scratch = [dma((CELL, 2))]
        if rest:
            outs.append(shape((extra, depth), F32))
            weights_held = [pltpu.VMEM((rows, width), F32)] * 3
            scratch = (
                [pltpu.VMEM((2 * half, depth), F32)] * 2
                + weights_held
                + [dma((5,)), pltpu.VMEM((2 * half, depth), F32)]
                + scratch
                + [dma((CELL + 1, 4))]
            )
        inputs = [first, second, *rest]
        packed = call(
            functools.partial(pack_kernel, half, bool(rest)),
            inputs,
            [HBM] * 5 + [VMEM] if rest else [VMEM] * 2,
            outs,
            [HBM] * len(outs),
            scratch,
            grant=60 if rest else 26,
        )
        near = [lax.ppermute(packed[turn], PLACE, pairs[turn]) for turn in range(ROUNDS)]
        return near, *packed[ROUNDS:]

    def spread(near, local):
        far = [lax.ppermute(piece, "head", SWAP) for piece in near]
        return near + far + [local, lax.ppermute(local, "head", SWAP)]

    def combine(near, far, across=None):
        if across is None:
            across = lax.ppermute(far, "head", SWAP)
        length = near[0].shape[0]
        found = [
            part + across[number * length : (number + 1) * length]
            for number, part in enumerate(near)
        ]
        return found, far[len(near) * length :] + across[len(near) * length :]

    def hand_back(totals, first):
        return [
            lax.ppermute(total, PLACE, flipped(pairs[first + number]))
            for number, total in enumerate(totals)
        ]

    def settle(back, local):
        def choose(turn):
            return jnp.where(turn == 0, back[0], jnp.where(turn == 1, back[1], back[2]))

        low, high = choose(turn0), choose(turn1)
        found = []
        for which in range(low.shape[0] // half):
            span = slice(which * half, (which + 1) * half)
            remote = jnp.concatenate((low[span], high[span]))
            here = local[which * 2 * half : (which + 1) * 2 * half]
            found.append(jnp.where(at_home, here, remote))
        return found

    inner_near, inner_local, kept = gather(
        key_rows[0, 0],
        value_rows[0, 0],
        fast_gate[0],
        fast_up[0],
        fast_down[0],
        -step[:, None],
    )
    inner_near = list(lax.optimization_barrier(tuple(inner_near)))
    inner_rows = spread(inner_near, inner_local)
    inner_rows[-1], queries = lax.optimization_barrier((inner_rows[-1], query_rows[0, 0]))
    read_near, read_local = gather(queries, read_cotangent[0, 0])
    slots = [piece[2 * half :] for piece in inner_near]
    slots.append(jnp.where(core == place - home_of(0), kept, inner_rows[-1][4 * half :]))
    together = jnp.stack(slots)
    parts = [together]
    for shift in range(1, reps):
        parts.append(lax.ppermute(together, "rep", shifted(shift, 1)))
    if cells > 1:
        parts = [lax.all_gather(jnp.stack(parts), "tok", axis_index_groups=cell_groups)]

    size = 2 * half
    count = CELL * size
    square = shape((3, width, cols), F32)
    tall = shape((count, cols), F32)
    product = 6 * count * width * cols
    buffers = [pltpu.VMEM((CELL, size, depth), F32)] * 2
    turned = pltpu.VMEM((2, 2, depth, count), BF16)
    acts = pltpu.VMEM((2, 3, count, cols), BF16)
    split_square = pltpu.VMEM((2, 3, width, cols), BF16)
    weights, gates, ups, backs, key_turned, steps = call(
        functools.partial(inner_kernel, cells, reps),
        parts + inner_rows,
        [HBM] * (len(parts) + 8),
        [square, tall, tall, tall, shape((2, 2, depth, count), BF16), square],
        [VMEM] * 6,
        buffers + [split_square, acts, dma((CELL, 4)), dma((cells * reps * CELL * 4,))],
        6 * product,
    )
    if cells > 1:
        steps = lax.psum(steps, "tok", axis_index_groups=cell_groups)
    narrow = shape((3, width, cols), BF16)
    high, low = call(
        renew_kernel, (weights, steps), [VMEM] * 2, [narrow, narrow], [VMEM] * 2, []
    )
    *read_near, read_local, high = lax.optimization_barrier((*read_near, read_local, high))
    read_rows = spread(list(read_near), read_local)
    span = CELL * half
    piece = shape((half, depth), F32)
    turned_shape = shape((2, 2, depth, span), BF16)
    acts_shape = shape((2, 3, span, cols), BF16)
    read_scratch = [pltpu.VMEM((span, depth), F32)] * 3 + [dma((2, CELL)), dma((CELL,))]
    *query_near, query_first, turned_first, read_acts = call(
        functools.partial(read_kernel, 0),
        read_rows[:ROUNDS] + read_rows[2 * ROUNDS :] + [high, low],
        [HBM] * (ROUNDS + 2) + [VMEM] * 2,
        [piece] * CELL + [turned_shape, acts_shape],
        [HBM] * CELL + [VMEM] * 2,
        read_scratch,
        5 * product // 2,
        18,
    )
    totals, query_far = call(
        functools.partial(read_kernel, 1),
        read_rows[ROUNDS:] + [high, low, turned_first, read_acts],
        [HBM] * (ROUNDS + 2) + [VMEM] * 4,
        [square, shape((span, depth), F32)],
        [VMEM, HBM],
        [pltpu.VMEM(turned_shape.shape, BF16), pltpu.VMEM(acts_shape.shape, BF16)] + read_scratch,
        11 * product // 2,
        18,
    )
    if cells > 1:
        totals = lax.psum(totals, "tok", axis_index_groups=cell_groups)
    cots, direct = call(
        functools.partial(renew_back_kernel, cells),
        [weights, steps, totals],
        [VMEM] * 3,
        [shape((2, 3, width, cols), BF16), square],
        [VMEM] * 2,
        [],
    )
    middle = 2

    def token_grads(first, last, cots):
        rounds = min(last, ROUNDS) - first
        span = slice(first, first + rounds)
        inputs = inner_rows[:ROUNDS][span] + inner_rows[ROUNDS : 2 * ROUNDS][span]
        if last > ROUNDS:
            inputs = inputs + inner_rows[2 * ROUNDS :]
        blocks = last - first
        specs = [HBM] * len(inputs) + [VMEM] * 5
        outs = [shape((size, depth), F32)] * rounds
        outs.append(shape((size * (2 * blocks - rounds), depth), F32))
        acts = (2, 3, blocks * size, cols)
        out_specs = [HBM] * len(outs) + [VMEM]
        outs.append(shape(acts, BF16))
        outs = call(
            functools.partial(token_grad_kernel, first, last),
            inputs + [weights, cots, gates, ups, backs],
            specs,
            outs,
            out_specs,
            [pltpu.VMEM((blocks, size, depth), F32)] * 2
            + [
                split_square,
                pltpu.VMEM((2, blocks, size, depth), F32),
                dma((blocks, 4)),
                dma((blocks, 4)),
            ],
            9 * product * blocks // CELL,
        )
        return outs[:rounds], outs[rounds], list(outs[rounds + 1 :])

    near_first, far_first, (acts_first,) = token_grads(0, middle, cots)
    query_got = lax.ppermute(query_far, "head", SWAP)
    query_totals = [
        part + query_got[turn * half : (turn + 1) * half] for turn, part in enumerate(query_near)
    ]
    cots, *query_totals = lax.optimization_barrier((cots, *query_totals))
    query_back = hand_back(query_totals, 0)
    near_last, far_last, (acts_last,) = token_grads(middle, CELL, cots)
    got_first = lax.ppermute(far_first, "head", SWAP)
    far_last, got_first, *rest = lax.optimization_barrier(
        (far_last, got_first, *near_first, *query_back)
    )
    near_first, query_back = rest[:-ROUNDS], rest[-ROUNDS:]
    totals_first, _ = combine(near_first, far_first, got_first)
    acts_last, *totals_first = lax.optimization_barrier((acts_last, *totals_first))
    back = hand_back(totals_first, 0)
    given = list(
        call(
            functools.partial(weight_grad_kernel, cells, reps),
            [key_turned, direct, acts_first, acts_last],
            [VMEM] * 4,
            [shape((cells, CELL, 3, rows, cols), F32)] * reps,
            [HBM] * reps,
            [pltpu.VMEM((3, width, cols), F32), dma((cells * reps * CELL,))],
            3 * product,
            16,
        )
    )
    totals_last, local = combine(near_last, far_last)
    back += hand_back(totals_last, middle)
    query_first, *totals_last = lax.optimization_barrier((query_first, *totals_last))
    query_local = jnp.concatenate(
        (
            query_first + lax.ppermute(query_first, "head", SWAP),
            (query_far + query_got)[ROUNDS * half :],
        )
    )
    given[0], *back = lax.optimization_barrier((given[0], *back))
    (query_grad,) = settle(query_back, query_local)
    key_grad, target_grad = settle(back, local)

    if cells > 1:
        given = [
            lax.psum_scatter(value, "tok", scatter_dimension=0, tiled=True, axis_index_groups=cell_groups)
            for value in given
        ]
    total = given[0][0]
    for shift in range(1, reps):
        total = total + lax.ppermute(given[shift][0], "rep", shifted(shift, 1))
    returned = [
        lax.ppermute(total[turn], PLACE, flipped(pairs[turn])) for turn in range(ROUNDS)
    ]
    home_piece = total[ROUNDS]
    home_other = lax.ppermute(home_piece, "head", SWAP)

    def choose(turn):
        return jnp.where(turn == 0, returned[0], jnp.where(turn == 1, returned[1], returned[2]))

    left = jnp.where(at_home, jnp.where(core == 0, home_piece, home_other), choose(turn0))
    right = jnp.where(at_home, jnp.where(core == 0, home_other, home_piece), choose(turn1))
    owned = jnp.concatenate((left, right), axis=2)

    value_grad = -step[:, None] * target_grad
    step_grad = -jnp.sum(value_rows[0, 0] * target_grad, axis=1)
    logit_grad = step_grad * factor * jax.nn.sigmoid(step_logits[0, 0])
    return (
        query_grad[None, None],
        key_grad[None, None],
        value_grad[None, None],
        logit_grad[None, None],
        owned[0][None],
        owned[1][None],
        owned[2][None],
    )


def solution(mesh):
    tokens = P(("groups", "rep"), "head", "tok", None)
    logits = P(("groups", "rep"), "head", "tok")
    weight = P("head", ("tok", "rep"), None)
    grad = P(("groups", "head"), ("tok", "rep"), None)
    return jax.shard_map(
        per_device,
        mesh=mesh,
        in_specs=(tokens, tokens, tokens, logits, tokens, weight, weight, weight),
        out_specs=(tokens, tokens, tokens, logits, grad, grad, grad),
        check_vma=False,
    )
```
